128 devices in a mesh: mem: 8 (over x, core), tx: 4 (over z), ty: 4 (over y).
Axes of the slice: x: 4, y: 4, z: 4, core: 2. Of those that a mesh axis runs over, the one named last changes fastest.
Arguments:
- pressure: float32 [64, 1024, 1024], P('mem', 'tx', 'ty'), may hold values from -6 to 6
- elevation: float32 [1024, 1024], P('tx', 'ty'), may hold values from -4 to 4
- ks_field: float32 [1024, 1024], P('tx', 'ty'), may hold values from 0.03 to 0.24
- melt_rate: float32 [64, 1024, 1024], P('mem', 'tx', 'ty'), may hold values from -1.5 to 1.5
- obs_index: int32 [1024], replicated, may hold values from 0 to 1048575
- obs_value: float32 [1024], P(('tx', 'ty')), may hold values from -6 to 6
- obs_error: float32 [1024], P(('tx', 'ty')), may hold values from 0.3 to 1
- perturbation: float32 [1024, 64], P(('tx', 'ty'), 'mem'), may hold values from -6 to 6
Outputs:
- analysis: float32 [64, 1024, 1024], P('mem', 'tx', 'ty')
The draws below stay inside these ranges and needn't reach their ends.
All inputs are finite; a program needn't handle non-finite values.
Results may differ from the reference program's by a relative error of at most 0.0089.
Values may be sent and summed in bfloat16 or wider, within the bound.
No kernel may reach another device: no remote copies, remote signals or barrier semaphores. Data moves between devices by JAX's collectives and lax.ppermute only.
A program may use at most 128 MiB of HBM per device.

```python
import math
import jax
import jax.numpy as jnp
from jax import lax

MEM_DEV = 8
NOBS = 1024
SUBSTEPS = 4
NODES_ACROSS = 1024
NODES_DOWNSLOPE = 1024
REPLICA_COUNT = 64
N_MEM = 8


def touch_ends(array, stream_key, smallest, high):
    index_at = [jax.random.randint(jax.random.fold_in(stream_key, axis), (), 0, length) for axis, length in enumerate(array.shape)]
    longest = array.shape.index(max(array.shape))
    beside = index_at[:longest] + [(index_at[longest] + 1) % array.shape[longest]] + index_at[longest + 1:]
    return array.at[tuple(index_at)].set(smallest).at[tuple(beside)].set(high)


def block_levels(key, dims, pieces, least, largest):
    def one(axis_at, parts):
        heights = jax.random.uniform(jax.random.fold_in(jax.random.fold_in(key, 6), axis_at), (parts,), jnp.float32, least / len(pieces), largest / len(pieces))
        return jnp.repeat(jnp.exp(heights), dims[axis_at] // parts).reshape((-1,) + (1,) * (len(dims) - axis_at - 1))

    loudness = one(*pieces[0])
    for cut in pieces[1:]:
        loudness = loudness * one(*cut)
    return loudness


def noise(own_key, extent, deviation, limit, shards=(), kind=jnp.bfloat16):
    level = block_levels(own_key, extent, shards, -0.22, 0.18) if shards else 1.0
    entries = jax.random.normal(own_key, extent, jnp.float32) * deviation * level
    return jnp.minimum(jnp.maximum(entries, -limit), limit).astype(kind)


def setup_inputs(seed: int = 0) -> dict:
    streams_of = jax.random.split(jax.random.key(seed), 9)
    pressure = noise(streams_of[0], (REPLICA_COUNT, NODES_ACROSS, NODES_DOWNSLOPE), 1.0, 6.0, ((0, 8), (1, 4), (2, 4)), jnp.float32)
    elevation = noise(streams_of[1], (NODES_ACROSS, NODES_DOWNSLOPE), 0.5, 4.0, ((0, 4), (1, 4)), jnp.float32)
    ks_field = jnp.clip(jnp.exp(math.log(0.24) - 2.0794415 * jax.random.uniform(streams_of[2], (NODES_ACROSS, NODES_DOWNSLOPE), jnp.float32) ** block_levels(streams_of[2], (NODES_ACROSS, NODES_DOWNSLOPE), ((0, 4), (1, 4)), -0.2, 0.2)), 0.03, 0.24)
    melt_rate = noise(streams_of[3], (REPLICA_COUNT, NODES_ACROSS, NODES_DOWNSLOPE), 0.25, 1.5, ((0, 8), (1, 4), (2, 4)), jnp.float32)
    obs_index = touch_ends(jax.random.randint(streams_of[4], (NOBS,), 0, NODES_ACROSS * NODES_DOWNSLOPE), jax.random.fold_in(streams_of[4], 1), 0, (NODES_ACROSS * NODES_DOWNSLOPE) - 1).astype(jnp.int32)
    obs_value = noise(streams_of[5], (NOBS,), 1.0, 6.0, ((0, 16),), jnp.float32)
    obs_error = jnp.clip(jnp.exp(math.log(1.0) - 1.2039728 * jax.random.uniform(streams_of[6], (NOBS,), jnp.float32) ** block_levels(streams_of[6], (NOBS,), ((0, 16),), -0.2, 0.2)), 0.3, 1.0)
    perturbation = noise(streams_of[7], (NOBS, REPLICA_COUNT), 1.0, 6.0, ((0, 16), (1, 8)), jnp.float32)
    return {"pressure": pressure, "elevation": elevation, "ks_field": ks_field, "melt_rate": melt_rate, "obs_index": obs_index, "obs_value": obs_value, "obs_error": obs_error, "perturbation": perturbation}


def flux_total(padded_head, padded_cond, total_head, conduct, row_global, col_global, total_x, total_y):
    size_x = total_head.shape[1]
    size_y = total_head.shape[2]
    change = jnp.zeros_like(total_head)
    moves = ((-1, 0, row_global > 0), (1, 0, row_global < total_x - 1), (0, -1, col_global > 0), (0, 1, col_global < total_y - 1))
    for shift_x, shift_y, valid in moves:
        near_head = padded_head[:, 1 + shift_x:1 + shift_x + size_x, 1 + shift_y:1 + shift_y + size_y]
        near_cond = padded_cond[:, 1 + shift_x:1 + shift_x + size_x, 1 + shift_y:1 + shift_y + size_y]
        flux = 0.5 * (conduct + near_cond) * (near_head - total_head)
        change = change + jnp.where(valid, flux, jnp.float32(0.0))
    return change

def advance_block(pressure, elevation, ks_field, melt_rate):
    row_global = jnp.arange(NODES_ACROSS, dtype=jnp.int32)[None, :, None]
    col_global = jnp.arange(NODES_DOWNSLOPE, dtype=jnp.int32)[None, None, :]
    for step in range(SUBSTEPS):
        total_head = pressure + elevation[None, :, :]
        conduct = ks_field[None, :, :] * jax.nn.sigmoid(pressure)
        padded_head = jnp.pad(total_head, ((0, 0), (1, 1), (1, 1)))
        padded_cond = jnp.pad(conduct, ((0, 0), (1, 1), (1, 1)))
        change = flux_total(padded_head, padded_cond, total_head, conduct, row_global, col_global, NODES_ACROSS, NODES_DOWNSLOPE)
        pressure = pressure + change + melt_rate
    return pressure

def reference(pressure, elevation, ks_field, melt_rate, obs_index, obs_value, obs_error, perturbation):
    partitioned_domain = pressure.reshape(N_MEM, MEM_DEV, NODES_ACROSS, NODES_DOWNSLOPE)
    snowwater_partitioned = melt_rate.reshape(N_MEM, MEM_DEV, NODES_ACROSS, NODES_DOWNSLOPE)

    def solitary_subdomain(pair):
        return advance_block(pair[0], elevation, ks_field, pair[1])
    predicted_states = lax.map(solitary_subdomain, (partitioned_domain, snowwater_partitioned)).reshape(REPLICA_COUNT, NODES_ACROSS, NODES_DOWNSLOPE)
    raveled_layout = predicted_states.reshape(REPLICA_COUNT, NODES_ACROSS * NODES_DOWNSLOPE)
    observed = jnp.take(raveled_layout, obs_index.astype(jnp.int32), axis=1).T
    scale = obs_error[:, None]
    innovation = (obs_value[:, None] + scale * perturbation - observed) / scale
    anomaly = (observed - jnp.mean(observed, axis=1, keepdims=True)) / scale
    gram = jnp.dot(anomaly.T.astype(jnp.float32), anomaly.astype(jnp.float32), precision=lax.Precision.HIGHEST, preferred_element_type=jnp.float32)
    coupling = jnp.dot(anomaly.T.astype(jnp.float32), innovation.astype(jnp.float32), precision=lax.Precision.HIGHEST, preferred_element_type=jnp.float32)
    system = gram + (REPLICA_COUNT - 1) * jnp.eye(REPLICA_COUNT, dtype=jnp.float32)
    lower = jnp.linalg.cholesky(system)
    weights = jax.scipy.linalg.cho_solve((lower, True), coupling).astype(jnp.bfloat16)
    rounded = raveled_layout.astype(jnp.bfloat16).astype(jnp.float32)
    assimilated_shift = jnp.dot(weights.astype(jnp.float32).T.astype(jnp.float32), rounded.astype(jnp.float32), precision=lax.Precision.HIGHEST, preferred_element_type=jnp.float32)
    return predicted_states + assimilated_shift.reshape(REPLICA_COUNT, NODES_ACROSS, NODES_DOWNSLOPE)
```

```python
import functools

import jax
import jax.numpy as jnp
from jax import lax
from jax.experimental import pallas as pl
from jax.experimental.pallas import tpu as pltpu
from jax.sharding import PartitionSpec as P

SUBSTEPS = 4
W = SUBSTEPS
GROUP = 128 // W
F32 = jnp.float32
BF16 = jnp.bfloat16
VMEM_SPEC = pl.BlockSpec(memory_space=pltpu.VMEM)


def lanes():
    return lax.broadcasted_iota(jnp.int32, (8, 128), 1)


def sublanes():
    return lax.broadcasted_iota(jnp.int32, (8, 128), 0)


def wide(row):
    return jnp.broadcast_to(row, (8, 128))


def turn_kernel(p_ref, w_ref, e_ref, k_ref, pt_ref, wt_ref, left_ref, right_ref):
    rows = p_ref.shape[1]
    pt_ref[...] = jnp.swapaxes(p_ref[...], 0, 1)
    wt_ref[...] = jnp.swapaxes(w_ref[...], 0, 1)
    lane, sub = lanes(), sublanes()
    for f, ref in enumerate((pt_ref, wt_ref, None)):
        left = jnp.zeros((8, 128), F32)
        right = jnp.zeros((8, 128), F32)
        for r in range(rows):
            if ref is not None:
                a, b = ref[r, :, 0:128], ref[r, :, 128:256]
            else:
                a = jnp.where(sub < 4, wide(e_ref[r : r + 1, 0:128]), wide(k_ref[r : r + 1, 0:128]))
                b = jnp.where(
                    sub < 4, wide(e_ref[r : r + 1, 128:256]), wide(k_ref[r : r + 1, 128:256])
                )
            if r:
                a = pltpu.roll(a, W * r, 1)
                b = pltpu.roll(b, W * r, 1)
            left = jnp.where(lane // W == r, a, left)
            right = jnp.where(lane // W == (r - 1) % GROUP, b, right)
        left_ref[0, f] = left
        right_ref[0, f] = right


def turn(p, w, e, k):
    members, size_x, size_y = p.shape
    groups = size_x // GROUP
    cube = pl.BlockSpec((members, GROUP, size_y), lambda g: (0, g, 0))
    flat = pl.BlockSpec((GROUP, size_y), lambda g: (g, 0))
    turned = pl.BlockSpec((GROUP, members, size_y), lambda g: (g, 0, 0))
    pack = pl.BlockSpec((1, 3, 8, 128), lambda g: (g, 0, 0, 0))
    return pl.pallas_call(
        turn_kernel,
        grid=(groups,),
        in_specs=[cube, cube, flat, flat],
        out_specs=[turned, turned, pack, pack],
        out_shape=[jax.ShapeDtypeStruct((size_x, members, size_y), F32)] * 2
        + [jax.ShapeDtypeStruct((groups + 1, 3, 8, 128), F32)] * 2,
        cost_estimate=pl.CostEstimate(flops=10**7, bytes_accessed=9 * 2**20, transcendentals=0),
        name="turn",
    )(p, w, e, k)


def rows_kernel(
    flag_ref, up_ref, down_ref, top_ref, bottom_ref, left_in, right_in, above_ref, below_ref,
    left_ref, right_ref,
):
    del left_in, right_in
    sub = sublanes()
    lane = lanes()
    first, last = flag_ref[0] > 0, flag_ref[1] > 0
    wide_sub = lax.broadcasted_iota(jnp.int32, (8, 256), 0)

    def turned_ek(block):
        out = block
        for i in range(4):
            for base in (0, 4):
                out = jnp.where(
                    wide_sub == base + i,
                    jnp.broadcast_to(block[base + 3 - i : base + 4 - i, :], (8, 256)),
                    out,
                )
        return out

    for flag, got, own, out in (
        (first, up_ref, top_ref, above_ref),
        (last, down_ref, bottom_ref, below_ref),
    ):
        for f in range(2):
            for i in range(W):
                out[f * W + i] = jnp.where(flag, own[f * W + W - 1 - i], got[f * W + i])
        out[2 * W] = jnp.where(flag, turned_ek(own[2 * W]), got[2 * W])
    for f in range(3):
        left = jnp.zeros((8, 128), F32)
        right = jnp.zeros((8, 128), F32)
        for half, out in enumerate((above_ref, below_ref)):
            for i in range(W):
                r = half * W + i
                if f < 2:
                    a, b = out[f * W + i, :, 0:128], out[f * W + i, :, 128:256]
                else:
                    a, b = (
                        jnp.where(
                            sub < 4,
                            wide(out[2 * W, i : i + 1, lo : lo + 128]),
                            wide(out[2 * W, 4 + i : 5 + i, lo : lo + 128]),
                        )
                        for lo in (0, 128)
                    )
                if r:
                    a = pltpu.roll(a, W * r, 1)
                    b = pltpu.roll(b, W * r, 1)
                left = jnp.where(lane // W == r, a, left)
                right = jnp.where(lane // W == (r - 1) % GROUP, b, right)
        left_ref[0, f] = left
        right_ref[0, f] = right


def halo_rows(flags, up, down, top, bottom, left, right):
    groups = left.shape[0]
    whole = pl.BlockSpec(up.shape, lambda g, s: (0, 0, 0))
    pack = pl.BlockSpec((1, 3, 8, 128), lambda g, s: (groups - 1, 0, 0, 0))
    return pl.pallas_call(
        rows_kernel,
        grid_spec=pltpu.PrefetchScalarGridSpec(
            num_scalar_prefetch=1,
            grid=(1,),
            in_specs=[whole] * 4 + [pl.BlockSpec(memory_space=pl.ANY)] * 2,
            out_specs=[whole, whole, pack, pack],
        ),
        out_shape=[jax.ShapeDtypeStruct(up.shape, F32)] * 2
        + [jax.ShapeDtypeStruct(left.shape, F32)] * 2,
        input_output_aliases={5: 2, 6: 3},
        name="rows",
    )(flags, up, down, top, bottom, left, right)


def steps_kernel(
    flag_ref, at_ref, turn_ref, pt_ref, wt_ref, e_ref, k_ref, above_ref, below_ref, fl_ref, fr_ref,
    inside_ref, out_ref, round_ref, pick_ref, p_s, w_s, e_s, k_s, f_s,
):
    size_x = pt_ref.shape[0]
    lane = lanes()
    groups = size_x // GROUP

    def interior(i, _):
        for u in range(8):
            x = i * 8 + u
            p_s[W + x, :, 0:256] = pt_ref[x]
            w_s[W + x, :, 0:256] = wt_ref[x]
        e8, k8 = e_ref[pl.ds(i * 8, 8), :], k_ref[pl.ds(i * 8, 8), :] * F32(0.25)
        for u in range(8):
            x = i * 8 + u
            e_s[W + x, :, 0:256] = jnp.broadcast_to(e8[u : u + 1], (8, 256))
            k_s[W + x, :, 0:256] = jnp.broadcast_to(k8[u : u + 1], (8, 256))
        return 0

    lax.fori_loop(0, size_x // 8, interior, 0)
    for half, ref in enumerate((above_ref, below_ref)):
        for i in range(W):
            x = i if half == 0 else W + size_x + i
            p_s[x, :, 0:256] = ref[i]
            w_s[x, :, 0:256] = ref[W + i]
            e_s[x, :, 0:256] = jnp.broadcast_to(ref[2 * W, i : i + 1, :], (8, 256))
            k_s[x, :, 0:256] = jnp.broadcast_to(ref[2 * W, 4 + i : 5 + i, :], (8, 256)) * F32(0.25)

    def unpack(g, r, x):
        got = []
        for f in range(3):
            a, b = fr_ref[g, f], fl_ref[g, f]
            if r:
                a = pltpu.roll(a, 128 - W * r, 1)
                b = pltpu.roll(b, 128 - W * r, 1)
            got.append(jnp.where(lane < 64, a, b))
        p_s[x, :, 256:384] = got[0]
        w_s[x, :, 256:384] = got[1]
        e_s[x, :, 256:384] = wide(got[2][0:1])
        k_s[x, :, 256:384] = wide(got[2][4:5]) * F32(0.25)

    def unpack_group(g, _):
        for r in range(GROUP):
            unpack(g, r, W + g * GROUP + r)
        return 0

    lax.fori_loop(0, groups, unpack_group, 0)
    for r in range(2 * W):
        unpack(groups, r, r if r < W else size_x + r)

    one, none = F32(1), F32(0)
    mask_right = jnp.where(
        (lane == 127) & (jnp.broadcast_to(flag_ref[3], (8, 128)) > 0), none, one
    )
    mask_left = jnp.where(
        (lane == 127) & (jnp.broadcast_to(flag_ref[2], (8, 128)) > 0), none, one
    )
    is_first, is_last = lane == 0, lane == 127

    def load(x):
        p = [p_s[x, :, 128 * t : 128 * t + 128] for t in range(3)]
        h = [p[t] + e_s[x, :, 128 * t : 128 * t + 128] for t in range(3)]
        k = [k_s[x, :, 128 * t : 128 * t + 128] for t in range(3)]
        c = [k[t] * jnp.tanh(p[t] * F32(0.5)) + k[t] for t in range(3)]
        return p, h, c

    def row(x, carry, last):
        p, h, c, before = carry
        pn, hn, cn = load(x + 1)
        after = [(c[t] + cn[t]) * (hn[t] - h[t]) for t in range(3)]
        hr = [pltpu.roll(v, 127, 1) for v in h]
        cr = [pltpu.roll(v, 127, 1) for v in c]
        hr = [jnp.where(is_last, hr[(t + 1) % 3], hr[t]) for t in range(3)]
        cr = [jnp.where(is_last, cr[(t + 1) % 3], cr[t]) for t in range(3)]
        across = [(c[t] + cr[t]) * (hr[t] - h[t]) for t in range(3)]
        across[1] = across[1] * mask_right
        across[2] = across[2] * mask_left
        back = [pltpu.roll(v, 1, 1) for v in across]
        back = [jnp.where(is_first, back[(t - 1) % 3], back[t]) for t in range(3)]
        for t in range(2 if last else 3):
            w = w_s[x, :, 128 * t : 128 * t + 128]
            new = (p[t] + w) + ((after[t] - before[t]) + (across[t] - back[t]))
            if last:
                f_s[x - W, t] = new
            else:
                p_s[x, :, 128 * t : 128 * t + 128] = new
        return pn, hn, cn, after

    def step(start, count, last):
        p0, h0, c0 = load(start - 1)
        p, h, c = load(start)
        before = [(c0[t] + c[t]) * (h[t] - h0[t]) for t in range(3)]

        def body(i, carry):
            for u in range(8):
                carry = row(start + i * 8 + u, carry, last)
            return carry

        lax.fori_loop(0, count // 8, body, (p, h, c, before))

    for s in range(SUBSTEPS - 1):
        step(1, size_x + 2 * W, False)
    step(W, size_x, True)

    def turn_back(i, _):
        x = pl.multiple_of(i * 16, 16)
        for t in range(2):
            block = jnp.swapaxes(f_s[pl.ds(x, 16), t], 0, 1)
            out_ref[:, pl.ds(x, 16), 128 * t : 128 * t + 128] = block
            round_ref[:, pl.ds(x, 16), 128 * t : 128 * t + 128] = block.astype(BF16)
        return 0

    lax.fori_loop(0, size_x // 16, turn_back, 0)

    count = pick_ref.shape[1]
    for g in range(count // 128):

        def pick(i, acc):
            for u in range(8):
                j = i * 8 + u
                at = at_ref[g * 128 + j]
                v = f_s[lax.shift_right_logical(at, 1), at & 1]
                v = pltpu.roll(v, turn_ref[g * 128 + j], 1)
                acc = jnp.where(lane == j, v, acc)
            return acc

        acc = lax.fori_loop(0, 16, pick, jnp.zeros((8, 128), F32))
        keep = wide(inside_ref[0:1, g * 128 : g * 128 + 128]) > F32(0.5)
        pick_ref[:, g * 128 : g * 128 + 128] = jnp.where(keep, acc, F32(0))


def run_steps(flags, at, turns, pt, wt, e, k, above, below, from_left, from_right, inside):
    size_x, members, size_y = pt.shape
    ext = (size_x + 2 * W + 2, members, size_y + 128)
    return pl.pallas_call(
        steps_kernel,
        grid_spec=pltpu.PrefetchScalarGridSpec(
            num_scalar_prefetch=3,
            grid=(),
            in_specs=[VMEM_SPEC] * 9,
            out_specs=[VMEM_SPEC] * 3,
            scratch_shapes=[pltpu.VMEM(ext, F32)] * 4
            + [pltpu.VMEM((size_x, 2, members, 128), F32)],
        ),
        out_shape=[
            jax.ShapeDtypeStruct((members, size_x, size_y), F32),
            jax.ShapeDtypeStruct((members, size_x, size_y), BF16),
            jax.ShapeDtypeStruct((members, at.shape[0]), F32),
        ],
        compiler_params=pltpu.CompilerParams(vmem_limit_bytes=48 * 2**20),
        name="steps",
    )(flags, at, turns, pt, wt, e, k, above, below, from_left, from_right, inside)


def weights_kernel(me_ref, scaled_ref, innovation_ref, out_ref, x_s, m_s):
    blocks = scaled_ref.shape[0]
    total = scaled_ref[0]
    for b in range(1, blocks):
        total = total + scaled_ref[b]
    mean = jnp.sum(total, axis=0, keepdims=True) * F32(1.0 / (8 * blocks))
    me = me_ref[0]
    for b in range(blocks):
        x_s[8 * b : 8 * b + 8, :] = scaled_ref[b ^ me] - mean
    x = x_s[...]
    dims = (((1,), (1,)), ((), ()))
    dot = functools.partial(
        lax.dot_general, dimension_numbers=dims, precision=lax.Precision.HIGHEST,
        preferred_element_type=F32,
    )
    members = 8 * blocks
    r = lax.broadcasted_iota(jnp.int32, (members, members), 0)
    c = lax.broadcasted_iota(jnp.int32, (members, members), 1)
    m_s[:, 0:members] = dot(x, x) + jnp.where(r == c, F32(members - 1), F32(0))
    m_s[:, members : 2 * members] = jnp.zeros((members, members), F32)
    m_s[:, members : members + 8] = dot(x, innovation_ref[...])
    m = [m_s[8 * b : 8 * b + 8, :] for b in range(blocks)]
    sub = sublanes()
    for kb in range(blocks):
        cols = [
            [jnp.broadcast_to(m[b][:, 8 * kb + j : 8 * kb + j + 1], (8, 128)) for j in range(8)]
            for b in range(blocks)
        ]
        rows = m[kb]
        piv = list(cols[kb])
        for j in range(8):
            inv = F32(1) / wide(piv[j][j : j + 1])
            here = sub == j
            factor = piv[j]
            top = wide(rows[j : j + 1]) * inv
            rows = jnp.where(here, top, rows - factor * top)
            for q in range(j + 1, 8):
                top = wide(piv[q][j : j + 1]) * inv
                piv[q] = jnp.where(here, top, piv[q] - factor * top)
        spread = [wide(rows[j : j + 1]) for j in range(8)]
        for b in range(blocks):
            if b == kb:
                m[b] = rows
            else:
                acc = cols[b][0] * spread[0]
                for j in range(1, 8):
                    acc = acc + cols[b][j] * spread[j]
                m[b] = m[b] - acc
    for b in range(blocks):
        out_ref[8 * b : 8 * b + 8, :] = m[b]


def solve_weights(me, scaled, innovation):
    blocks = scaled.shape[0]
    members = 8 * blocks
    out = pl.pallas_call(
        weights_kernel,
        grid_spec=pltpu.PrefetchScalarGridSpec(
            num_scalar_prefetch=1,
            grid=(),
            in_specs=[VMEM_SPEC] * 2,
            out_specs=VMEM_SPEC,
            scratch_shapes=[
                pltpu.VMEM((members, scaled.shape[2]), F32),
                pltpu.VMEM((members, 2 * members), F32),
            ],
        ),
        out_shape=jax.ShapeDtypeStruct((members, 2 * members), F32),
        name="weights",
    )(me, scaled, innovation)
    return out[:, members : members + 8].astype(BF16)


def local(pressure, elevation, ks_field, melt_rate, obs_index, obs_value, obs_error, perturbation):
    members, size_x, size_y = pressure.shape
    n_x, n_y, n_m = (lax.axis_size(a) for a in ("tx", "ty", "mem"))
    tile_x, tile_y, me = (lax.axis_index(a) for a in ("tx", "ty", "mem"))
    total_y = size_y * n_y
    flags = jnp.stack([tile_x == 0, tile_x == n_x - 1, tile_y == 0, tile_y == n_y - 1])
    flags = flags.astype(jnp.int32)

    def ends(lo):
        cut = functools.partial(lax.slice_in_dim, start_index=lo, limit_index=lo + W)
        return jnp.concatenate(
            [
                jnp.swapaxes(cut(pressure, axis=1), 0, 1),
                jnp.swapaxes(cut(melt_rate, axis=1), 0, 1),
                jnp.concatenate([cut(elevation, axis=0), cut(ks_field, axis=0)])[None],
            ]
        )

    def ring(n, by):
        return [(i, (i + by) % n) for i in range(n)]

    top, bottom = ends(0), ends(size_x - W)
    up = lax.ppermute(bottom, "tx", ring(n_x, 1))
    down = lax.ppermute(top, "tx", ring(n_x, -1))
    pt, wt, left, right = turn(pressure, melt_rate, elevation, ks_field)
    above, below, left, right = halo_rows(flags, up, down, top, bottom, left, right)
    from_left = lax.ppermute(right, "ty", ring(n_y, 1))
    from_right = lax.ppermute(left, "ty", ring(n_y, -1))

    local_x = obs_index // total_y - tile_x * size_x
    local_y = obs_index % total_y - tile_y * size_y
    inside = (local_x >= 0) & (local_x < size_x) & (local_y >= 0) & (local_y < size_y)
    cx, cy = jnp.clip(local_x, 0, size_x - 1), jnp.clip(local_y, 0, size_y - 1)
    at = cx * 2 + cy // 128
    n_obs = obs_index.shape[0]
    turns = (jnp.arange(n_obs, dtype=jnp.int32) - cy) % 128
    forecast, rounded, picked = run_steps(
        flags, at, turns, pt, wt, elevation, ks_field, above, below, from_left, from_right,
        inside.astype(F32)[None],
    )

    block = n_obs // (n_x * n_y)
    tile = tile_x * n_y + tile_y
    mine = jnp.concatenate(
        [
            (obs_value[:, None] + obs_error[:, None] * perturbation).T,
            jnp.broadcast_to(obs_error[None], (8, block)),
        ]
    )
    mine = lax.dynamic_update_slice(jnp.zeros((16, n_obs), F32), mine, (0, tile * block))
    line = jnp.concatenate([picked, mine])
    for axis, n in (("ty", n_y), ("tx", n_x)):
        bit = 1
        while bit < n:
            line = line + lax.ppermute(line, axis, [(i, i ^ bit) for i in range(n)])
            bit *= 2
    observed, target, error = line[0:8], line[8:16], line[16:17]
    innovation = (target - observed) / error
    scaled = (observed / error)[None]
    bit = 1
    while bit < n_m:
        got = lax.ppermute(scaled, "mem", [(i, i ^ bit) for i in range(n_m)])
        scaled = jnp.concatenate([scaled, got])
        bit *= 2
    weights = solve_weights(me[None].astype(jnp.int32), scaled, innovation)

    piece = lax.all_gather(rounded, "mem", axis=0, tiled=True)
    shift = lax.dot_general(
        weights,
        piece.reshape(piece.shape[0], size_x * size_y),
        (((0,), (0,)), ((), ())),
        preferred_element_type=F32,
    )
    return forecast + shift.reshape(members, size_x, size_y)


def solution(mesh):
    placed = (
        P("mem", "tx", "ty"),
        P("tx", "ty"),
        P("tx", "ty"),
        P("mem", "tx", "ty"),
        P(),
        P(("tx", "ty")),
        P(("tx", "ty")),
        P(("tx", "ty"), "mem"),
    )
    return jax.shard_map(
        local, mesh=mesh, in_specs=placed, out_specs=P("mem", "tx", "ty"), check_vma=False
    )
```

```python
import functools

import jax
import jax.numpy as jnp
from jax import lax
from jax.experimental import pallas as pl
from jax.experimental.pallas import tpu as pltpu
from jax.sharding import PartitionSpec as P

SUBSTEPS = 4
W = SUBSTEPS
GROUP = 128 // W
ROWS = 16
F32 = jnp.float32
BF16 = jnp.bfloat16
VMEM_SPEC = pl.BlockSpec(memory_space=pltpu.VMEM)


def lanes():
    return lax.broadcasted_iota(jnp.int32, (8, 128), 1)


def sublanes():
    return lax.broadcasted_iota(jnp.int32, (8, 128), 0)


def wide(row):
    return jnp.broadcast_to(row, (8, 128))


def pack_rows(rows):
    slot = lanes() // W
    left = jnp.zeros((8, 128), F32)
    right = jnp.zeros((8, 128), F32)
    for r, a, b in rows:
        if r:
            a = pltpu.roll(a, W * r, 1)
            b = pltpu.roll(b, W * r, 1)
        left = jnp.where(slot == r, a, left)
        right = jnp.where(slot == (r - 1) % GROUP, b, right)
    return left, right


def turn_kernel(p_ref, w_ref, e_ref, k_ref, pt_ref, wt_ref, left_ref, right_ref):
    rows = p_ref.shape[1]
    pt_ref[...] = jnp.swapaxes(p_ref[...] * F32(0.5), 0, 1)
    wt_ref[...] = jnp.swapaxes(w_ref[...] * F32(0.5), 0, 1)
    for f, ref in enumerate((pt_ref, wt_ref)):
        left_ref[0, f], right_ref[0, f] = pack_rows(
            (r, ref[r, :, 0:128], ref[r, :, 128:256]) for r in range(rows)
        )
    fields = []
    for base, ref, factor in ((0, e_ref, 0.5), (4, k_ref, 0.25)):
        for q in range(rows // 8):
            block = ref[8 * q : 8 * q + 8, :] * F32(factor)
            fields.append((base + q, block[:, 0:128], block[:, 128:256]))
    left_ref[0, 2], right_ref[0, 2] = pack_rows(fields)


def turn(p, w, e, k):
    members, size_x, size_y = p.shape
    groups = size_x // GROUP
    cube = pl.BlockSpec((members, GROUP, size_y), lambda g: (0, g, 0))
    flat = pl.BlockSpec((GROUP, size_y), lambda g: (g, 0))
    turned = pl.BlockSpec((GROUP, members, size_y), lambda g: (g, 0, 0))
    pack = pl.BlockSpec((1, 3, 8, 128), lambda g: (g, 0, 0, 0))
    return pl.pallas_call(
        turn_kernel,
        grid=(groups,),
        in_specs=[cube, cube, flat, flat],
        out_specs=[turned, turned, pack, pack],
        out_shape=[jax.ShapeDtypeStruct((size_x, members, size_y), F32)] * 2
        + [jax.ShapeDtypeStruct((groups + 1, 3, 8, 128), F32)] * 2,
        cost_estimate=pl.CostEstimate(flops=10**7, bytes_accessed=9 * 2**20, transcendentals=0),
        name="turn",
    )(p, w, e, k)


def rows_kernel(
    flag_ref, up_ref, down_ref, top_ref, bottom_ref, left_in, right_in, above_ref, below_ref,
    left_ref, right_ref,
):
    del left_in, right_in
    first, last = flag_ref[0] > 0, flag_ref[1] > 0
    sub = lax.broadcasted_iota(jnp.int32, (8, 256), 0)

    def mirrored(block):
        out = block
        for i in range(4):
            for base in (0, 4):
                row = block[base + 3 - i : base + 4 - i, :]
                out = jnp.where(sub == base + i, jnp.broadcast_to(row, (8, 256)), out)
        return out

    for flag, got, own, out in (
        (first, up_ref, top_ref, above_ref),
        (last, down_ref, bottom_ref, below_ref),
    ):
        for f in range(2):
            for i in range(W):
                row = jnp.where(flag, own[f * W + W - 1 - i], got[f * W + i])
                out[f * W + i] = row * F32(0.5)
        block = jnp.where(flag, mirrored(own[2 * W]), got[2 * W])
        out[2 * W] = block * jnp.where(sub < 4, F32(0.5), F32(0.25))
    for f in range(2):
        left_ref[0, f], right_ref[0, f] = pack_rows(
            (half * W + i, out[f * W + i, :, 0:128], out[f * W + i, :, 128:256])
            for half, out in enumerate((above_ref, below_ref))
            for i in range(W)
        )
    above, below = above_ref[2 * W], below_ref[2 * W]
    e = jnp.where(sub < 4, above, pltpu.roll(below, 4, 0))
    k = jnp.where(sub < 4, pltpu.roll(above, 4, 0), below)
    left_ref[0, 2], right_ref[0, 2] = pack_rows(
        (slot, v[:, 0:128], v[:, 128:256]) for slot, v in ((0, e), (4, k))
    )


def halo_rows(flags, up, down, top, bottom, left, right):
    groups = left.shape[0]
    whole = pl.BlockSpec(up.shape, lambda g, s: (0, 0, 0))
    pack = pl.BlockSpec((1, 3, 8, 128), lambda g, s: (groups - 1, 0, 0, 0))
    return pl.pallas_call(
        rows_kernel,
        grid_spec=pltpu.PrefetchScalarGridSpec(
            num_scalar_prefetch=1,
            grid=(1,),
            in_specs=[whole] * 4 + [pl.BlockSpec(memory_space=pl.ANY)] * 2,
            out_specs=[whole, whole, pack, pack],
        ),
        out_shape=[jax.ShapeDtypeStruct(up.shape, F32)] * 2
        + [jax.ShapeDtypeStruct(left.shape, F32)] * 2,
        input_output_aliases={5: 2, 6: 3},
        name="rows",
    )(flags, up, down, top, bottom, left, right)


def steps_kernel(
    flag_ref, code_ref, pt_ref, wt_ref, e_ref, k_ref, above_ref, below_ref, fl_ref, fr_ref,
    inside_ref, out_ref, round_ref, pick_ref,
    p0, p1, w_s, fy_s, sum_s, e_s, er_s, k_s, kr_s, f_s, sems,
):
    size_x = pt_ref.shape[0]
    lane = lanes()
    is_first, is_last = lane == 0, lane == 127
    groups = size_x // GROUP
    blocks = size_x // 8 + 2
    inner = (pl.ds(9, size_x), slice(None), pl.ds(0, 256))
    loads = [
        pltpu.make_async_copy(src, dst.at[inner], sems.at[i])
        for i, (src, dst) in enumerate(((pt_ref, p0), (wt_ref, w_s)))
    ]
    for c in loads:
        c.start()

    def halo(g, f, r):
        a, b = fr_ref[g, f], fl_ref[g, f]
        if r:
            a = pltpu.roll(a, 128 - W * r, 1)
            b = pltpu.roll(b, 128 - W * r, 1)
        return jnp.where(lane < 64, a, b)

    def spread(at, v, here, shifted):
        rolled = [pltpu.roll(u, 127, 1) for u in v]
        for t in range(3):
            here[at, :, 128 * t : 128 * t + 128] = v[t]
            shifted[at, :, 128 * t : 128 * t + 128] = jnp.where(
                is_last, rolled[(t + 1) % 3], rolled[t]
            )

    def unpack_group(g, _):
        for r in range(GROUP):
            for f, dst in ((0, p0), (1, w_s)):
                dst[g * GROUP + r + 9, :, 256:384] = halo(g, f, r)
        for q in range(GROUP // 8):
            rows = pl.ds(pl.multiple_of(g * GROUP + 8 * q, 8), 8)
            for base, ref, factor, here, shifted in (
                (0, e_ref, 0.5, e_s, er_s), (4, k_ref, 0.25, k_s, kr_s),
            ):
                v = [ref[rows, 128 * t : 128 * t + 128] * F32(factor) for t in range(2)]
                spread(g * (GROUP // 8) + q + 1, v + [halo(g, 2, base + q)], here, shifted)
        return 0

    lax.fori_loop(0, groups, unpack_group, 0)
    for r in range(2 * W):
        ref, y = (above_ref, 4 + r) if r < W else (below_ref, size_x + 4 + r)
        for f, dst in ((0, p0), (1, w_s)):
            dst[y + 1, :, 0:256] = ref[f * W + r % W]
            dst[y + 1, :, 256:384] = halo(groups, f, r)
    for base, here, shifted in ((0, e_s, er_s), (4, k_s, kr_s)):
        edge = pltpu.roll(halo(groups, 2, base), 4, 0)
        for at, ref, up in ((0, above_ref, base == 0), (blocks - 1, below_ref, base == 4)):
            v = ref[2 * W]
            v = pltpu.roll(v, 4, 0) if up else v
            spread(at, [v[:, 0:128], v[:, 128:256], edge], here, shifted)

    one, none = F32(1), F32(0)

    def edge_mask(flag):
        return jnp.where(is_last & (jnp.broadcast_to(flag, (8, 128)) > 0), none, one)

    mask_right, mask_left = edge_mask(flag_ref[3]), edge_mask(flag_ref[2])
    for c in loads:
        c.wait()

    def tiles(ref, at):
        return [ref[at, :, 128 * t : 128 * t + 128] for t in range(3)]

    def put(ref, at, v):
        for t in range(3):
            ref[at, :, 128 * t : 128 * t + 128] = v[t]

    def row_of(ref, b, u):
        return [wide(ref[b, u : u + 1, 128 * t : 128 * t + 128]) for t in range(3)]

    def step(src, dst):
        count = 8 * blocks // ROWS

        def body(i, carry):
            b_at = jnp.minimum(i, count - 1)
            c_at = jnp.maximum(i - 1, 0) * ROWS
            for u in range(ROWS):
                at = c_at + u
                s, fy = tiles(sum_s, at), tiles(fy_s, at)
                fr = [pltpu.roll(v, 1, 1) for v in fy]
                back = [jnp.where(is_first, fr[(t - 1) % 3], fr[t]) for t in range(3)]
                put(dst, at, [s[t] + (fy[t] - back[t]) for t in range(3)])
            p_old, h_old, c_old, fx_old = carry
            for u in range(ROWS):
                at = b_at * ROWS + u
                block = (b_at * (ROWS // 8) + u // 8, u % 8)
                p = tiles(src, at + 1)
                raw = [pltpu.roll(v, 127, 1) for v in p]
                pr = [jnp.where(is_last, raw[(t + 1) % 3], raw[t]) for t in range(3)]
                e, er = row_of(e_s, *block), row_of(er_s, *block)
                k, kr = row_of(k_s, *block), row_of(kr_s, *block)
                w = tiles(w_s, at)
                h = [p[t] + e[t] for t in range(3)]
                c = [k[t] * jnp.tanh(p[t]) + k[t] for t in range(3)]
                fy = [
                    (c[t] + (kr[t] * jnp.tanh(pr[t]) + kr[t])) * ((pr[t] + er[t]) - h[t])
                    for t in range(3)
                ]
                fy[1] = fy[1] * mask_right
                fy[2] = fy[2] * mask_left
                fx = [(c_old[t] + c[t]) * (h[t] - h_old[t]) for t in range(3)]
                put(sum_s, at, [(p_old[t] + w[t]) + (fx[t] - fx_old[t]) for t in range(3)])
                put(fy_s, at + 1, fy)
                p_old, h_old, c_old, fx_old = p, h, c, fx
            return p_old, h_old, c_old, fx_old

        zero = [jnp.zeros((8, 128), F32)] * 3
        lax.fori_loop(0, count + 1, body, (zero, zero, zero, zero))

    for s in range(SUBSTEPS):
        step(*((p0, p1) if s % 2 == 0 else (p1, p0)))
    last = p0 if SUBSTEPS % 2 == 0 else p1

    def turn_back(i, _):
        x = pl.multiple_of(i * 16, 16)
        for t in range(2):
            rows = last[pl.ds(x + 9, 16), :, 128 * t : 128 * t + 128] * F32(2)
            for u in range(16):
                f_s[x * 2 + (2 * u + t)] = rows[u]
            block = jnp.swapaxes(rows, 0, 1)
            out_ref[:, pl.ds(x, 16), 128 * t : 128 * t + 128] = block
            round_ref[:, pl.ds(x, 16), 128 * t : 128 * t + 128] = block.astype(BF16)
        return 0

    lax.fori_loop(0, size_x // 16, turn_back, 0)

    def pick(g, _):
        acc = jnp.zeros((8, 128), F32)
        for u in range(128):
            code = code_ref[g * 128 + u]
            v = pltpu.roll(f_s[lax.shift_right_logical(code, 7)], code & 127, 1)
            acc = jnp.where(lane == u, v, acc)
        cols = pl.ds(pl.multiple_of(g * 128, 128), 128)
        keep = wide(inside_ref[0:1, cols]) > F32(0.5)
        pick_ref[:, cols] = jnp.where(keep, acc, F32(0))
        return 0

    lax.fori_loop(0, pick_ref.shape[1] // 128, pick, 0)


def run_steps(flags, code, pt, wt, e, k, above, below, from_left, from_right, inside):
    size_x, members, size_y = pt.shape
    tile = pltpu.VMEM((size_x + 17, members, size_y + 128), F32)
    flat = pltpu.VMEM((size_x // 8 + 2, 8, size_y + 128), F32)
    anywhere = pl.BlockSpec(memory_space=pl.ANY)
    return pl.pallas_call(
        steps_kernel,
        grid_spec=pltpu.PrefetchScalarGridSpec(
            num_scalar_prefetch=2,
            grid=(),
            in_specs=[anywhere] * 2 + [VMEM_SPEC] * 7,
            out_specs=[VMEM_SPEC] * 3,
            scratch_shapes=[tile] * 5 + [flat] * 4
            + [pltpu.VMEM((2 * size_x, members, 128), F32), pltpu.SemaphoreType.DMA((2,))],
        ),
        out_shape=[
            jax.ShapeDtypeStruct((members, size_x, size_y), F32),
            jax.ShapeDtypeStruct((members, size_x, size_y), BF16),
            jax.ShapeDtypeStruct((members, code.shape[0]), F32),
        ],
        compiler_params=pltpu.CompilerParams(vmem_limit_bytes=50 * 2**20),
        name="steps",
    )(flags, code, pt, wt, e, k, above, below, from_left, from_right, inside)


def weights_kernel(me_ref, scaled_ref, innovation_ref, out_ref, x_s, m_s):
    blocks = scaled_ref.shape[0]
    total = scaled_ref[0]
    for b in range(1, blocks):
        total = total + scaled_ref[b]
    mean = jnp.sum(total, axis=0, keepdims=True) * F32(1.0 / (8 * blocks))
    me = me_ref[0]
    for b in range(blocks):
        x_s[8 * b : 8 * b + 8, :] = scaled_ref[b ^ me] - mean
    x = x_s[...]
    dims = (((1,), (1,)), ((), ()))
    dot = functools.partial(
        lax.dot_general, dimension_numbers=dims, precision=lax.Precision.HIGHEST,
        preferred_element_type=F32,
    )
    members = 8 * blocks
    r = lax.broadcasted_iota(jnp.int32, (members, members), 0)
    c = lax.broadcasted_iota(jnp.int32, (members, members), 1)
    m_s[:, 0:members] = dot(x, x) + jnp.where(r == c, F32(members - 1), F32(0))
    m_s[:, members : 2 * members] = jnp.zeros((members, members), F32)
    m_s[:, members : members + 8] = dot(x, innovation_ref[...])
    m = [m_s[8 * b : 8 * b + 8, :] for b in range(blocks)]
    sub = sublanes()
    for kb in range(blocks):
        cols = [
            [jnp.broadcast_to(m[b][:, 8 * kb + j : 8 * kb + j + 1], (8, 128)) for j in range(8)]
            for b in range(blocks)
        ]
        rows = m[kb]
        piv = list(cols[kb])
        for j in range(8):
            inv = F32(1) / wide(piv[j][j : j + 1])
            here = sub == j
            factor = piv[j]
            top = wide(rows[j : j + 1]) * inv
            rows = jnp.where(here, top, rows - factor * top)
            for q in range(j + 1, 8):
                top = wide(piv[q][j : j + 1]) * inv
                piv[q] = jnp.where(here, top, piv[q] - factor * top)
        spread = [wide(rows[j : j + 1]) for j in range(8)]
        for b in range(blocks):
            if b == kb:
                m[b] = rows
            else:
                acc = cols[b][0] * spread[0]
                for j in range(1, 8):
                    acc = acc + cols[b][j] * spread[j]
                m[b] = m[b] - acc
    for b in range(blocks):
        out_ref[8 * b : 8 * b + 8, :] = m[b]


def solve_weights(me, scaled, innovation):
    blocks = scaled.shape[0]
    members = 8 * blocks
    out = pl.pallas_call(
        weights_kernel,
        grid_spec=pltpu.PrefetchScalarGridSpec(
            num_scalar_prefetch=1,
            grid=(),
            in_specs=[VMEM_SPEC] * 2,
            out_specs=VMEM_SPEC,
            scratch_shapes=[
                pltpu.VMEM((members, scaled.shape[2]), F32),
                pltpu.VMEM((members, 2 * members), F32),
            ],
        ),
        out_shape=jax.ShapeDtypeStruct((members, 2 * members), F32),
        name="weights",
    )(me, scaled, innovation)
    return out[:, members : members + 8].astype(BF16)


def local(pressure, elevation, ks_field, melt_rate, obs_index, obs_value, obs_error, perturbation):
    members, size_x, size_y = pressure.shape
    n_x, n_y, n_m = (lax.axis_size(a) for a in ("tx", "ty", "mem"))
    tile_x, tile_y, me = (lax.axis_index(a) for a in ("tx", "ty", "mem"))
    total_y = size_y * n_y
    flags = jnp.stack([tile_x == 0, tile_x == n_x - 1, tile_y == 0, tile_y == n_y - 1])
    flags = flags.astype(jnp.int32)

    def ends(lo):
        cut = functools.partial(lax.slice_in_dim, start_index=lo, limit_index=lo + W)
        return jnp.concatenate(
            [
                jnp.swapaxes(cut(pressure, axis=1), 0, 1),
                jnp.swapaxes(cut(melt_rate, axis=1), 0, 1),
                jnp.concatenate([cut(elevation, axis=0), cut(ks_field, axis=0)])[None],
            ]
        )

    def ring(n, by):
        return [(i, (i + by) % n) for i in range(n)]

    top, bottom = ends(0), ends(size_x - W)
    up = lax.ppermute(bottom, "tx", ring(n_x, 1))
    down = lax.ppermute(top, "tx", ring(n_x, -1))
    pt, wt, left, right = turn(pressure, melt_rate, elevation, ks_field)
    above, below, left, right = halo_rows(flags, up, down, top, bottom, left, right)
    from_left = lax.ppermute(right, "ty", ring(n_y, 1))
    from_right = lax.ppermute(left, "ty", ring(n_y, -1))

    local_x = obs_index // total_y - tile_x * size_x
    local_y = obs_index % total_y - tile_y * size_y
    inside = (local_x >= 0) & (local_x < size_x) & (local_y >= 0) & (local_y < size_y)
    cx, cy = jnp.clip(local_x, 0, size_x - 1), jnp.clip(local_y, 0, size_y - 1)
    at = cx * 2 + cy // 128
    n_obs = obs_index.shape[0]
    turns = (jnp.arange(n_obs, dtype=jnp.int32) - cy) % 128
    forecast, rounded, picked = run_steps(
        flags, at * 128 + turns, pt, wt, elevation, ks_field, above, below, from_left, from_right,
        inside.astype(F32)[None],
    )

    block = n_obs // (n_x * n_y)
    tile = tile_x * n_y + tile_y
    mine = jnp.concatenate(
        [
            (obs_value[:, None] + obs_error[:, None] * perturbation).T,
            jnp.broadcast_to(obs_error[None], (8, block)),
        ]
    )
    mine = lax.dynamic_update_slice(jnp.zeros((16, n_obs), F32), mine, (0, tile * block))
    line = jnp.concatenate([picked, mine])
    for axis, n in (("ty", n_y), ("tx", n_x)):
        bit = 1
        while bit < n:
            line = line + lax.ppermute(line, axis, [(i, i ^ bit) for i in range(n)])
            bit *= 2
    observed, target, error = line[0:8], line[8:16], line[16:17]
    innovation = (target - observed) / error
    scaled = (observed / error)[None]
    bit = 1
    while bit < n_m:
        got = lax.ppermute(scaled, "mem", [(i, i ^ bit) for i in range(n_m)])
        scaled = jnp.concatenate([scaled, got])
        bit *= 2
    weights = solve_weights(me[None].astype(jnp.int32), scaled, innovation)

    piece = lax.all_gather(rounded, "mem", axis=0, tiled=True)
    shift = lax.dot_general(
        weights,
        piece.reshape(piece.shape[0], size_x * size_y),
        (((0,), (0,)), ((), ())),
        preferred_element_type=F32,
    )
    return forecast + shift.reshape(members, size_x, size_y)


def solution(mesh):
    placed = (
        P("mem", "tx", "ty"),
        P("tx", "ty"),
        P("tx", "ty"),
        P("mem", "tx", "ty"),
        P(),
        P(("tx", "ty")),
        P(("tx", "ty")),
        P(("tx", "ty"), "mem"),
    )
    return jax.shard_map(
        local, mesh=mesh, in_specs=placed, out_specs=P("mem", "tx", "ty"), check_vma=False
    )
```

```python
import functools

import jax
import jax.numpy as jnp
from jax import lax
from jax.experimental import pallas as pl
from jax.experimental.pallas import tpu as pltpu
from jax.sharding import PartitionSpec as P

SUBSTEPS = 4
W = SUBSTEPS
GROUP = 128 // W
ROWS = 16
F32 = jnp.float32
BF16 = jnp.bfloat16
VMEM_SPEC = pl.BlockSpec(memory_space=pltpu.VMEM)


def lanes():
    return lax.broadcasted_iota(jnp.int32, (8, 128), 1)


def sublanes():
    return lax.broadcasted_iota(jnp.int32, (8, 128), 0)


def wide(row):
    return jnp.broadcast_to(row, (8, 128))


def pack_rows(rows):
    slot = lanes() // W
    left = jnp.zeros((8, 128), F32)
    right = jnp.zeros((8, 128), F32)
    for r, a, b in rows:
        if r:
            a = pltpu.roll(a, W * r, 1)
            b = pltpu.roll(b, W * r, 1)
        left = jnp.where(slot == r, a, left)
        right = jnp.where(slot == (r - 1) % GROUP, b, right)
    return left, right


def turn_kernel(p_ref, w_ref, e_ref, k_ref, pt_ref, wt_ref, left_ref, right_ref):
    rows = p_ref.shape[1]
    pt_ref[...] = jnp.swapaxes(p_ref[...] * F32(0.5), 0, 1)
    wt_ref[...] = jnp.swapaxes(w_ref[...] * F32(0.5), 0, 1)
    for f, ref in enumerate((pt_ref, wt_ref)):
        left_ref[0, f], right_ref[0, f] = pack_rows(
            (r, ref[r, :, 0:128], ref[r, :, 128:256]) for r in range(rows)
        )
    fields = []
    for base, ref, factor in ((0, e_ref, 0.5), (4, k_ref, 0.25)):
        for q in range(rows // 8):
            block = ref[8 * q : 8 * q + 8, :] * F32(factor)
            fields.append((base + q, block[:, 0:128], block[:, 128:256]))
    left_ref[0, 2], right_ref[0, 2] = pack_rows(fields)


def turn(p, w, e, k):
    members, size_x, size_y = p.shape
    groups = size_x // GROUP
    cube = pl.BlockSpec((members, GROUP, size_y), lambda g: (0, g, 0))
    flat = pl.BlockSpec((GROUP, size_y), lambda g: (g, 0))
    turned = pl.BlockSpec((GROUP, members, size_y), lambda g: (g, 0, 0))
    pack = pl.BlockSpec((1, 3, 8, 128), lambda g: (g, 0, 0, 0))
    return pl.pallas_call(
        turn_kernel,
        grid=(groups,),
        in_specs=[cube, cube, flat, flat],
        out_specs=[turned, turned, pack, pack],
        out_shape=[jax.ShapeDtypeStruct((size_x, members, size_y), F32)] * 2
        + [jax.ShapeDtypeStruct((groups + 1, 3, 8, 128), F32)] * 2,
        cost_estimate=pl.CostEstimate(flops=10**7, bytes_accessed=9 * 2**20, transcendentals=0),
        name="turn",
    )(p, w, e, k)


def rows_kernel(
    flag_ref, up_ref, down_ref, top_ref, bottom_ref, left_in, right_in, above_ref, below_ref,
    left_ref, right_ref,
):
    del left_in, right_in
    first, last = flag_ref[0] > 0, flag_ref[1] > 0
    sub = lax.broadcasted_iota(jnp.int32, (8, 256), 0)

    def mirrored(block):
        out = block
        for i in range(4):
            for base in (0, 4):
                row = block[base + 3 - i : base + 4 - i, :]
                out = jnp.where(sub == base + i, jnp.broadcast_to(row, (8, 256)), out)
        return out

    for flag, got, own, out in (
        (first, up_ref, top_ref, above_ref),
        (last, down_ref, bottom_ref, below_ref),
    ):
        for f in range(2):
            for i in range(W):
                row = jnp.where(flag, own[f * W + W - 1 - i], got[f * W + i])
                out[f * W + i] = row * F32(0.5)
        block = jnp.where(flag, mirrored(own[2 * W]), got[2 * W])
        out[2 * W] = block * jnp.where(sub < 4, F32(0.5), F32(0.25))
    for f in range(2):
        left_ref[0, f], right_ref[0, f] = pack_rows(
            (half * W + i, out[f * W + i, :, 0:128], out[f * W + i, :, 128:256])
            for half, out in enumerate((above_ref, below_ref))
            for i in range(W)
        )
    above, below = above_ref[2 * W], below_ref[2 * W]
    e = jnp.where(sub < 4, above, pltpu.roll(below, 4, 0))
    k = jnp.where(sub < 4, pltpu.roll(above, 4, 0), below)
    left_ref[0, 2], right_ref[0, 2] = pack_rows(
        (slot, v[:, 0:128], v[:, 128:256]) for slot, v in ((0, e), (4, k))
    )


def halo_rows(flags, up, down, top, bottom, left, right):
    groups = left.shape[0]
    whole = pl.BlockSpec(up.shape, lambda g, s: (0, 0, 0))
    pack = pl.BlockSpec((1, 3, 8, 128), lambda g, s: (groups - 1, 0, 0, 0))
    return pl.pallas_call(
        rows_kernel,
        grid_spec=pltpu.PrefetchScalarGridSpec(
            num_scalar_prefetch=1,
            grid=(1,),
            in_specs=[whole] * 4 + [pl.BlockSpec(memory_space=pl.ANY)] * 2,
            out_specs=[whole, whole, pack, pack],
        ),
        out_shape=[jax.ShapeDtypeStruct(up.shape, F32)] * 2
        + [jax.ShapeDtypeStruct(left.shape, F32)] * 2,
        input_output_aliases={5: 2, 6: 3},
        name="rows",
    )(flags, up, down, top, bottom, left, right)


def steps_kernel(
    flag_ref, code_ref, pt_in, wt_in, e_ref, k_ref, above_ref, below_ref, fl_ref, fr_ref,
    inside_ref, out_ref, round_ref, pick_ref,
    p0, p1, w_s, fy_s, sum_s, e_s, er_s, k_s, kr_s, f_s,
    sems,
):
    size_x = pt_in.shape[0]
    lane = lanes()
    is_first, is_last = lane == 0, lane == 127
    groups = size_x // GROUP
    blocks = size_x // 8 + 2
    inner = (pl.ds(9, size_x), slice(None), pl.ds(0, 256))
    loads = [
        pltpu.make_async_copy(src, dst.at[inner], sems.at[i])
        for i, (src, dst) in enumerate(((pt_in, p0), (wt_in, w_s)))
    ]
    for c in loads:
        c.start()

    def halo(g, f, r):
        a, b = fr_ref[g, f], fl_ref[g, f]
        if r:
            a = pltpu.roll(a, 128 - W * r, 1)
            b = pltpu.roll(b, 128 - W * r, 1)
        return jnp.where(lane < 64, a, b)

    def spread(at, v, here, shifted):
        rolled = [pltpu.roll(u, 127, 1) for u in v]
        for t in range(3):
            here[at, :, 128 * t : 128 * t + 128] = v[t]
            shifted[at, :, 128 * t : 128 * t + 128] = jnp.where(
                is_last, rolled[(t + 1) % 3], rolled[t]
            )

    def unpack_group(g, _):
        for r in range(GROUP):
            for f, dst in ((0, p0), (1, w_s)):
                dst[g * GROUP + r + 9, :, 256:384] = halo(g, f, r)
        for q in range(GROUP // 8):
            rows = pl.ds(pl.multiple_of(g * GROUP + 8 * q, 8), 8)
            for base, ref, factor, here, shifted in (
                (0, e_ref, 0.5, e_s, er_s), (4, k_ref, 0.25, k_s, kr_s),
            ):
                v = [ref[rows, 128 * t : 128 * t + 128] * F32(factor) for t in range(2)]
                spread(g * (GROUP // 8) + q + 1, v + [halo(g, 2, base + q)], here, shifted)
        return 0

    lax.fori_loop(0, groups, unpack_group, 0)
    for r in range(2 * W):
        ref, y = (above_ref, 4 + r) if r < W else (below_ref, size_x + 4 + r)
        for f, dst in ((0, p0), (1, w_s)):
            dst[y + 1, :, 0:256] = ref[f * W + r % W]
            dst[y + 1, :, 256:384] = halo(groups, f, r)
    for base, here, shifted in ((0, e_s, er_s), (4, k_s, kr_s)):
        edge = pltpu.roll(halo(groups, 2, base), 4, 0)
        for at, ref, up in ((0, above_ref, base == 0), (blocks - 1, below_ref, base == 4)):
            v = ref[2 * W]
            v = pltpu.roll(v, 4, 0) if up else v
            spread(at, [v[:, 0:128], v[:, 128:256], edge], here, shifted)

    one, none = F32(1), F32(0)

    def edge_mask(flag):
        return jnp.where(is_last & (jnp.broadcast_to(flag, (8, 128)) > 0), none, one)

    mask_right, mask_left = edge_mask(flag_ref[3]), edge_mask(flag_ref[2])
    for c in loads:
        c.wait()

    def tiles(ref, at):
        return [ref[at, :, 128 * t : 128 * t + 128] for t in range(3)]

    def put(ref, at, v):
        for t in range(3):
            ref[at, :, 128 * t : 128 * t + 128] = v[t]

    def row_of(ref, b, u):
        return [wide(ref[b, u : u + 1, 128 * t : 128 * t + 128]) for t in range(3)]

    def step(src, dst):
        count = 8 * blocks // ROWS

        def body(i, carry):
            b_at = jnp.minimum(i, count - 1)
            c_at = jnp.maximum(i - 1, 0) * ROWS
            for u in range(ROWS):
                at = c_at + u
                s, fy = tiles(sum_s, at), tiles(fy_s, at)
                fr = [pltpu.roll(v, 1, 1) for v in fy]
                back = [jnp.where(is_first, fr[(t - 1) % 3], fr[t]) for t in range(3)]
                put(dst, at, [s[t] + (fy[t] - back[t]) for t in range(3)])
            p_old, h_old, c_old, fx_old = carry
            for u in range(ROWS):
                at = b_at * ROWS + u
                block = (b_at * (ROWS // 8) + u // 8, u % 8)
                p = tiles(src, at + 1)
                raw = [pltpu.roll(v, 127, 1) for v in p]
                pr = [jnp.where(is_last, raw[(t + 1) % 3], raw[t]) for t in range(3)]
                e, er = row_of(e_s, *block), row_of(er_s, *block)
                k, kr = row_of(k_s, *block), row_of(kr_s, *block)
                w = tiles(w_s, at)
                h = [p[t] + e[t] for t in range(3)]
                c = [k[t] * jnp.tanh(p[t]) + k[t] for t in range(3)]
                fy = [
                    (c[t] + (kr[t] * jnp.tanh(pr[t]) + kr[t])) * ((pr[t] + er[t]) - h[t])
                    for t in range(3)
                ]
                fy[1] = fy[1] * mask_right
                fy[2] = fy[2] * mask_left
                fx = [(c_old[t] + c[t]) * (h[t] - h_old[t]) for t in range(3)]
                put(sum_s, at, [(p_old[t] + w[t]) + (fx[t] - fx_old[t]) for t in range(3)])
                put(fy_s, at + 1, fy)
                p_old, h_old, c_old, fx_old = p, h, c, fx
            return p_old, h_old, c_old, fx_old

        zero = [jnp.zeros((8, 128), F32)] * 3
        lax.fori_loop(0, count + 1, body, (zero, zero, zero, zero))

    for s in range(SUBSTEPS):
        step(*((p0, p1) if s % 2 == 0 else (p1, p0)))
    last = p0 if SUBSTEPS % 2 == 0 else p1

    def leave(i, _):
        x = pl.multiple_of(i * 8, 8)
        for u in range(8):
            row = last[x + 9 + u, :, 0:256] * F32(2)
            out_ref[x + u] = row
            round_ref[x + u] = row.astype(BF16)
            f_s[2 * x + 2 * u] = row[:, 0:128]
            f_s[2 * x + 2 * u + 1] = row[:, 128:256]
        return 0

    lax.fori_loop(0, size_x // 8, leave, 0)

    def pick(g, _):
        acc = jnp.zeros((8, 128), F32)
        for u in range(128):
            code = code_ref[g * 128 + u]
            v = pltpu.roll(f_s[lax.shift_right_logical(code, 7)], code & 127, 1)
            acc = jnp.where(lane == u, v, acc)
        cols = pl.ds(pl.multiple_of(g * 128, 128), 128)
        keep = wide(inside_ref[0:1, cols]) > F32(0.5)
        pick_ref[:, cols] = jnp.where(keep, acc, F32(0))
        return 0

    lax.fori_loop(0, pick_ref.shape[1] // 128, pick, 0)


def run_steps(flags, code, pt, wt, e, k, above, below, from_left, from_right, inside):
    size_x, members, size_y = pt.shape
    tile = pltpu.VMEM((size_x + 17, members, size_y + 128), F32)
    flat = pltpu.VMEM((size_x // 8 + 2, 8, size_y + 128), F32)
    anywhere = pl.BlockSpec(memory_space=pl.ANY)
    return pl.pallas_call(
        steps_kernel,
        grid_spec=pltpu.PrefetchScalarGridSpec(
            num_scalar_prefetch=2,
            grid=(),
            in_specs=[anywhere] * 2 + [VMEM_SPEC] * 7,
            out_specs=[VMEM_SPEC] * 3,
            scratch_shapes=[tile] * 5 + [flat] * 4
            + [pltpu.VMEM((2 * size_x, members, 128), F32)]
            + [pltpu.SemaphoreType.DMA((2,))],
        ),
        out_shape=[
            jax.ShapeDtypeStruct((size_x, members, size_y), F32),
            jax.ShapeDtypeStruct((size_x, members, size_y), BF16),
            jax.ShapeDtypeStruct((members, code.shape[0]), F32),
        ],
        compiler_params=pltpu.CompilerParams(vmem_limit_bytes=50 * 2**20),
        name="steps",
    )(flags, code, pt, wt, e, k, above, below, from_left, from_right, inside)


def weights_kernel(near_ref, far_ref, innovation_ref, out_ref, x_s, m_s):
    half = near_ref.shape[0]
    members = 2 * half
    blocks = members // 8
    parts = [r[8 * b : 8 * b + 8, :] for r in (near_ref, far_ref) for b in range(half // 8)]
    total = parts[0]
    for part in parts[1:]:
        total = total + part
    mean = jnp.sum(total, axis=0, keepdims=True) * F32(1.0 / members)
    for b, part in enumerate(parts):
        x_s[8 * b : 8 * b + 8, :] = part - mean
    x = x_s[...]
    dims = (((1,), (1,)), ((), ()))
    dot = functools.partial(
        lax.dot_general, dimension_numbers=dims, precision=lax.Precision.HIGHEST,
        preferred_element_type=F32,
    )
    r = lax.broadcasted_iota(jnp.int32, (members, members), 0)
    c = lax.broadcasted_iota(jnp.int32, (members, members), 1)
    m_s[:, 0:members] = dot(x, x) + jnp.where(r == c, F32(members - 1), F32(0))
    m_s[:, members : 2 * members] = jnp.zeros((members, members), F32)
    m_s[:, members : members + 8] = dot(x, innovation_ref[...])
    m = [m_s[8 * b : 8 * b + 8, :] for b in range(blocks)]
    sub = sublanes()
    for kb in range(blocks):
        cols = [
            [jnp.broadcast_to(m[b][:, 8 * kb + j : 8 * kb + j + 1], (8, 128)) for j in range(8)]
            for b in range(blocks)
        ]
        rows = m[kb]
        piv = list(cols[kb])
        for j in range(8):
            inv = F32(1) / wide(piv[j][j : j + 1])
            here = sub == j
            factor = piv[j]
            top = wide(rows[j : j + 1]) * inv
            rows = jnp.where(here, top, rows - factor * top)
            for q in range(j + 1, 8):
                top = wide(piv[q][j : j + 1]) * inv
                piv[q] = jnp.where(here, top, piv[q] - factor * top)
        spread = [wide(rows[j : j + 1]) for j in range(8)]
        for b in range(blocks):
            if b == kb:
                m[b] = rows
            else:
                acc = cols[b][0] * spread[0]
                for j in range(1, 8):
                    acc = acc + cols[b][j] * spread[j]
                m[b] = m[b] - acc
    for b in range(blocks):
        m_s[8 * b : 8 * b + 8, :] = m[b]
    turned = jnp.transpose(m_s[...], (1, 0))
    out_ref[:, 0:members] = turned[members : members + 8, :]


def solve_weights(near, far, innovation):
    half, n_obs = near.shape
    members = 2 * half
    return pl.pallas_call(
        weights_kernel,
        in_specs=[VMEM_SPEC] * 3,
        out_specs=VMEM_SPEC,
        scratch_shapes=[
            pltpu.VMEM((members, n_obs), F32),
            pltpu.VMEM((members, 2 * members), F32),
        ],
        out_shape=jax.ShapeDtypeStruct((8, members), F32),
        name="weights",
    )(near, far, innovation)


def update_kernel(w_ref, *refs):
    pieces, f_ref, out_ref, row_s = refs[:10], refs[10], refs[11], refs[12]
    own, a, b, c, d, o, a2, b2, c2, d2 = pieces
    low = pl.program_id(0) < pl.num_programs(0) // 2
    w = w_ref[...].astype(BF16)
    for r in range(f_ref.shape[0]):
        parts = [
            own[r], a[r], b[r], jnp.where(low, c[r].astype(F32), d[r].astype(F32)),
            o[r], a2[r], b2[r], jnp.where(low, c2[r].astype(F32), d2[r].astype(F32)),
        ]
        rows = jnp.concatenate([v.astype(F32) for v in parts], axis=0).astype(BF16)
        row_s[r] = f_ref[r] + jnp.dot(w, rows, preferred_element_type=F32)
    out_ref[...] = jnp.swapaxes(row_s[...], 0, 1)


def update(weights, pieces, forecast):
    size_x, members, size_y = forecast.shape
    step = 32
    count = size_x // step
    shape = (step, members, size_y)
    whole = pl.BlockSpec(shape, lambda g: (g, 0, 0))
    first = pl.BlockSpec(shape, lambda g: (jnp.minimum(g, count // 2 - 1), 0, 0))
    second = pl.BlockSpec(shape, lambda g: (jnp.maximum(g - count // 2, 0), 0, 0))
    five = [whole] * 3 + [first, second]
    return pl.pallas_call(
        update_kernel,
        grid=(count,),
        in_specs=[pl.BlockSpec(weights.shape, lambda g: (0, 0))] + five + five + [whole],
        out_specs=pl.BlockSpec((members, step, size_y), lambda g: (0, g, 0)),
        out_shape=jax.ShapeDtypeStruct((members, size_x, size_y), F32),
        scratch_shapes=[pltpu.VMEM(shape, F32)],
        name="update",
    )(weights, *pieces, forecast)


def local(pressure, elevation, ks_field, melt_rate, obs_index, obs_value, obs_error, perturbation):
    members, size_x, size_y = pressure.shape
    n_x, n_y, n_m = (lax.axis_size(a) for a in ("tx", "ty", "mem"))
    tile_x, tile_y, me = (lax.axis_index(a) for a in ("tx", "ty", "mem"))
    total_y = size_y * n_y
    flags = jnp.stack([tile_x == 0, tile_x == n_x - 1, tile_y == 0, tile_y == n_y - 1])
    flags = flags.astype(jnp.int32)

    def ends(lo):
        cut = functools.partial(lax.slice_in_dim, start_index=lo, limit_index=lo + W)
        return jnp.concatenate(
            [
                jnp.swapaxes(cut(pressure, axis=1), 0, 1),
                jnp.swapaxes(cut(melt_rate, axis=1), 0, 1),
                jnp.concatenate([cut(elevation, axis=0), cut(ks_field, axis=0)])[None],
            ]
        )

    def ring(n, by):
        return [(i, (i + by) % n) for i in range(n)]

    top, bottom = ends(0), ends(size_x - W)
    up = lax.ppermute(bottom, "tx", ring(n_x, 1))
    down = lax.ppermute(top, "tx", ring(n_x, -1))
    pt, wt, left, right = turn(pressure, melt_rate, elevation, ks_field)
    above, below, left, right = halo_rows(flags, up, down, top, bottom, left, right)
    from_left = lax.ppermute(right, "ty", ring(n_y, 1))
    from_right = lax.ppermute(left, "ty", ring(n_y, -1))

    local_x = obs_index // total_y - tile_x * size_x
    local_y = obs_index % total_y - tile_y * size_y
    inside = (local_x >= 0) & (local_x < size_x) & (local_y >= 0) & (local_y < size_y)
    cx, cy = jnp.clip(local_x, 0, size_x - 1), jnp.clip(local_y, 0, size_y - 1)
    at = cx * 2 + cy // 128
    n_obs = obs_index.shape[0]
    turns = (jnp.arange(n_obs, dtype=jnp.int32) - cy) % 128
    forecast, rounded, picked = run_steps(
        flags, at * 128 + turns, pt, wt, elevation, ks_field, above, below, from_left, from_right,
        inside.astype(F32)[None],
    )

    block = n_obs // (n_x * n_y)
    tile = tile_x * n_y + tile_y
    mine = jnp.concatenate(
        [
            (obs_value[:, None] + obs_error[:, None] * perturbation).T,
            jnp.broadcast_to(obs_error[None], (8, block)),
        ]
    )
    mine = lax.dynamic_update_slice(jnp.zeros((16, n_obs), F32), mine, (0, tile * block))
    line = jnp.concatenate([picked, mine])
    for axis, n in (("ty", n_y), ("tx", n_x)):
        bit = 1
        while bit < n:
            line = line + lax.ppermute(line, axis, [(i, i ^ bit) for i in range(n)])
            bit *= 2
    observed, target, error = line[0:8], line[8:16], line[16:17]
    innovation = (target - observed) / error
    scaled = observed / error

    def chips(by):
        return [(i, (i + 2 * by) % n_m) for i in range(n_m)]

    swap = [(i, i ^ 1) for i in range(n_m)]

    def send(v, to):
        return lax.ppermute(v, "mem", to)

    half = size_x // 2
    a, b, o = send(rounded, chips(1)), send(rounded, chips(-1)), send(rounded, swap)
    c, d = send(a[:half], chips(1)), send(b[half:], chips(-1))
    pieces = (rounded, a, b, c, d, o, *(send(v, swap) for v in (a, b, c, d)))
    near = jnp.concatenate([scaled] + [send(scaled, chips(by)) for by in (1, -1, 2)])
    far = send(near, swap)
    weights = solve_weights(near, far, innovation)
    return update(weights, pieces, forecast)


def solution(mesh):
    placed = (
        P("mem", "tx", "ty"),
        P("tx", "ty"),
        P("tx", "ty"),
        P("mem", "tx", "ty"),
        P(),
        P(("tx", "ty")),
        P(("tx", "ty")),
        P(("tx", "ty"), "mem"),
    )
    return jax.shard_map(
        local, mesh=mesh, in_specs=placed, out_specs=P("mem", "tx", "ty"), check_vma=False
    )
```

```python
import functools

import jax
import jax.numpy as jnp
from jax import lax
from jax.experimental import pallas as pl
from jax.experimental.pallas import tpu as pltpu
from jax.sharding import PartitionSpec as P

SUBSTEPS = 4
W = SUBSTEPS
GROUP = 128 // W
ROWS = 16
F32 = jnp.float32
BF16 = jnp.bfloat16
VMEM_SPEC = pl.BlockSpec(memory_space=pltpu.VMEM)
HBM_SPEC = pl.BlockSpec(memory_space=pltpu.HBM)


def lanes():
    return lax.broadcasted_iota(jnp.int32, (8, 128), 1)


def sublanes():
    return lax.broadcasted_iota(jnp.int32, (8, 128), 0)


def wide(row):
    return jnp.broadcast_to(row, (8, 128))


def ends_kernel(
    obs_ref, p_ref, w_ref, e_ref, k_ref, top_ref, bottom_ref, code_ref, inside_ref,
    cubes, sems,
):
    members, size_x, size_y = p_ref.shape
    copies = []
    for i, lo in enumerate((0, size_x - 8)):
        for j, ref in enumerate((p_ref, w_ref)):
            copies.append((ref.at[:, pl.ds(lo, 8), :], cubes.at[2 * i + j]))
    copies = [pltpu.make_async_copy(a, b, sems.at[n]) for n, (a, b) in enumerate(copies)]
    for c in copies:
        c.start()
    bits_x, bits_y = size_x.bit_length() - 1, size_y.bit_length() - 1
    total_y = size_y * lax.axis_size("ty")
    obs = obs_ref[...]
    x = lax.shift_right_logical(obs, total_y.bit_length() - 1)
    y = obs & (total_y - 1)
    mine = (lax.shift_right_logical(x, bits_x) == lax.axis_index("tx")) & (
        lax.shift_right_logical(y, bits_y) == lax.axis_index("ty")
    )
    x, y = x & (size_x - 1), y & (size_y - 1)
    tile = x * (size_y // 128) + lax.shift_right_logical(y, 7)
    code_ref[...] = tile * 128 + ((lanes() - y) & 127)
    inside_ref[...] = jnp.where(mine, F32(1), F32(0))
    for c in copies:
        c.wait()
    sub = lax.broadcasted_iota(jnp.int32, (8, size_y), 0)
    for i, out in enumerate((top_ref, bottom_ref)):
        for j in range(2):
            turned = jnp.swapaxes(cubes[2 * i + j], 0, 1)
            for r in range(W):
                out[j * W + r] = turned[r if i == 0 else 8 - W + r]
        lo = (0, size_x - 8)[i]
        e, k = e_ref[lo : lo + 8, :], k_ref[lo : lo + 8, :]
        if i == 0:
            k = pltpu.roll(k, 4, 0)
        else:
            e = pltpu.roll(e, 4, 0)
        out[2 * W] = jnp.where(sub < 4, e, k)


def ends(obs, p, w, e, k):
    members, size_x, size_y = p.shape
    edge = jax.ShapeDtypeStruct((2 * W + 1, members, size_y), F32)
    return pl.pallas_call(
        ends_kernel,
        in_specs=[VMEM_SPEC] + [HBM_SPEC] * 2 + [VMEM_SPEC] * 2,
        out_specs=[VMEM_SPEC] * 4,
        out_shape=[
            edge, edge, jax.ShapeDtypeStruct(obs.shape, jnp.int32),
            jax.ShapeDtypeStruct(obs.shape, F32),
        ],
        scratch_shapes=[
            pltpu.VMEM((4, members, 8, size_y), F32),
            pltpu.SemaphoreType.DMA((4,)),
        ],
        compiler_params=pltpu.CompilerParams(vmem_limit_bytes=52 * 2**20),
        name="ends",
    )(obs, p, w, e, k)


def pack_rows(rows):
    slot = lanes() // W
    left = jnp.zeros((8, 128), F32)
    right = jnp.zeros((8, 128), F32)
    for r, a, b in rows:
        if r:
            a = pltpu.roll(a, W * r, 1)
            b = pltpu.roll(b, W * r, 1)
        left = jnp.where(slot == r, a, left)
        right = jnp.where(slot == (r - 1) % GROUP, b, right)
    return left, right


def turn_kernel(
    p_in, w_in, e_ref, k_ref, pt_out, wt_out, left_ref, right_ref,
    p_ref, w_ref, pt_ref, wt_ref, in_sems, out_sems,
):
    groups = left_ref.shape[0]

    def rows_of(g):
        return pl.ds(pl.multiple_of(g * GROUP, GROUP), GROUP)

    def fetch(g, f):
        src, dst = ((p_in, p_ref), (w_in, w_ref))[f]
        at = rows_of(g)
        return pltpu.make_async_copy(src.at[:, at, :], dst.at[:, at, :], in_sems.at[f, g])

    def leave(g, f):
        src, dst = ((pt_ref, pt_out), (wt_ref, wt_out))[f]
        at = rows_of(g)
        return pltpu.make_async_copy(src.at[at], dst.at[at], out_sems.at[f, g])

    for g in range(groups):
        for f in range(2):
            fetch(g, f).start()

    def group(g, _):
        at = rows_of(g)
        for f, (src, dst) in enumerate(((p_ref, pt_ref), (w_ref, wt_ref))):
            fetch(g, f).wait()
            rows = jnp.swapaxes(src[:, at, :] * F32(0.5), 0, 1)
            dst[at] = rows
            left_ref[g, f], right_ref[g, f] = pack_rows(
                (r, rows[r, :, 0:128], rows[r, :, 128:256]) for r in range(GROUP)
            )
            leave(g, f).start()
        fields = []
        for base, ref, factor in ((0, e_ref, 0.5), (4, k_ref, 0.25)):
            block = ref[at, :] * F32(factor)
            for q in range(GROUP // 8):
                part = block[8 * q : 8 * q + 8]
                fields.append((base + q, part[:, 0:128], part[:, 128:256]))
        left_ref[g, 2], right_ref[g, 2] = pack_rows(fields)
        return 0

    lax.fori_loop(0, groups, group, 0)
    for g in range(groups):
        for f in range(2):
            leave(g, f).wait()


def turn(p, w, e, k):
    members, size_x, size_y = p.shape
    groups = size_x // GROUP
    turned = (size_x, members, size_y)
    return pl.pallas_call(
        turn_kernel,
        in_specs=[HBM_SPEC] * 2 + [VMEM_SPEC] * 2,
        out_specs=[HBM_SPEC] * 2 + [VMEM_SPEC] * 2,
        out_shape=[jax.ShapeDtypeStruct(turned, F32)] * 2
        + [jax.ShapeDtypeStruct((groups, 3, 8, 128), F32)] * 2,
        scratch_shapes=[pltpu.VMEM(p.shape, F32)] * 2 + [pltpu.VMEM(turned, F32)] * 2
        + [pltpu.SemaphoreType.DMA((2, groups))] * 2,
        cost_estimate=pl.CostEstimate(flops=10**7, bytes_accessed=9 * 2**20, transcendentals=0),
        compiler_params=pltpu.CompilerParams(vmem_limit_bytes=52 * 2**20),
        name="turn",
    )(p, w, e, k)


def rows_kernel(
    up_ref, down_ref, top_ref, bottom_ref, left_in, right_in, above_ref, below_ref,
    left_ref, right_ref,
):
    tile, groups = lax.axis_index("tx"), left_in.shape[0]
    first, last = tile == 0, tile == lax.axis_size("tx") - 1
    left_ref[0:groups] = left_in[...]
    right_ref[0:groups] = right_in[...]
    sub = lax.broadcasted_iota(jnp.int32, (8, 256), 0)

    def mirrored(block):
        out = block
        for i in range(4):
            for base in (0, 4):
                row = block[base + 3 - i : base + 4 - i, :]
                out = jnp.where(sub == base + i, jnp.broadcast_to(row, (8, 256)), out)
        return out

    for flag, got, own, out in (
        (first, up_ref, top_ref, above_ref),
        (last, down_ref, bottom_ref, below_ref),
    ):
        for f in range(2):
            for i in range(W):
                row = jnp.where(flag, own[f * W + W - 1 - i], got[f * W + i])
                out[f * W + i] = row * F32(0.5)
        block = jnp.where(flag, mirrored(own[2 * W]), got[2 * W])
        out[2 * W] = block * jnp.where(sub < 4, F32(0.5), F32(0.25))
    for f in range(2):
        left_ref[groups, f], right_ref[groups, f] = pack_rows(
            (half * W + i, out[f * W + i, :, 0:128], out[f * W + i, :, 128:256])
            for half, out in enumerate((above_ref, below_ref))
            for i in range(W)
        )
    above, below = above_ref[2 * W], below_ref[2 * W]
    e = jnp.where(sub < 4, above, pltpu.roll(below, 4, 0))
    k = jnp.where(sub < 4, pltpu.roll(above, 4, 0), below)
    left_ref[groups, 2], right_ref[groups, 2] = pack_rows(
        (slot, v[:, 0:128], v[:, 128:256]) for slot, v in ((0, e), (4, k))
    )


def halo_rows(up, down, top, bottom, left, right):
    packs = jax.ShapeDtypeStruct((left.shape[0] + 1, *left.shape[1:]), F32)
    return pl.pallas_call(
        rows_kernel,
        in_specs=[VMEM_SPEC] * 6,
        out_specs=[VMEM_SPEC] * 4,
        out_shape=[jax.ShapeDtypeStruct(up.shape, F32)] * 2 + [packs] * 2,
        compiler_params=pltpu.CompilerParams(vmem_limit_bytes=4 * 2**20),
        name="rows",
    )(up, down, top, bottom, left, right)


def steps_kernel(
    pt_in, wt_in, e_ref, k_ref, above_ref, below_ref, fl_ref, fr_ref,
    out_ref, round_ref,
    p0, p1, w_s, fy_s, sum_s, e_s, er_s, k_s, kr_s, sems,
):
    size_x = pt_in.shape[0]
    lane = lanes()
    is_first, is_last = lane == 0, lane == 127
    groups = size_x // GROUP
    blocks = size_x // 8 + 2
    inner = (pl.ds(9, size_x), slice(None), pl.ds(0, 256))
    loads = [
        pltpu.make_async_copy(src, dst.at[inner], sems.at[i])
        for i, (src, dst) in enumerate(((pt_in, p0), (wt_in, w_s)))
    ]
    for c in loads:
        c.start()

    def halo(g, f, r):
        a, b = fr_ref[g, f], fl_ref[g, f]
        if r:
            a = pltpu.roll(a, 128 - W * r, 1)
            b = pltpu.roll(b, 128 - W * r, 1)
        return jnp.where(lane < 64, a, b)

    def spread(at, v, here, shifted):
        rolled = [pltpu.roll(u, 127, 1) for u in v]
        for t in range(3):
            here[at, :, 128 * t : 128 * t + 128] = v[t]
            shifted[at, :, 128 * t : 128 * t + 128] = jnp.where(
                is_last, rolled[(t + 1) % 3], rolled[t]
            )

    def unpack_group(g, _):
        for r in range(GROUP):
            for f, dst in ((0, p0), (1, w_s)):
                dst[g * GROUP + r + 9, :, 256:384] = halo(g, f, r)
        for q in range(GROUP // 8):
            rows = pl.ds(pl.multiple_of(g * GROUP + 8 * q, 8), 8)
            for base, ref, factor, here, shifted in (
                (0, e_ref, 0.5, e_s, er_s), (4, k_ref, 0.25, k_s, kr_s),
            ):
                v = [ref[rows, 128 * t : 128 * t + 128] * F32(factor) for t in range(2)]
                spread(g * (GROUP // 8) + q + 1, v + [halo(g, 2, base + q)], here, shifted)
        return 0

    lax.fori_loop(0, groups, unpack_group, 0)
    for r in range(2 * W):
        ref, y = (above_ref, 4 + r) if r < W else (below_ref, size_x + 4 + r)
        for f, dst in ((0, p0), (1, w_s)):
            dst[y + 1, :, 0:256] = ref[f * W + r % W]
            dst[y + 1, :, 256:384] = halo(groups, f, r)
    for base, here, shifted in ((0, e_s, er_s), (4, k_s, kr_s)):
        edge = pltpu.roll(halo(groups, 2, base), 4, 0)
        for at, ref, up in ((0, above_ref, base == 0), (blocks - 1, below_ref, base == 4)):
            v = ref[2 * W]
            v = pltpu.roll(v, 4, 0) if up else v
            spread(at, [v[:, 0:128], v[:, 128:256], edge], here, shifted)

    one, none = F32(1), F32(0)

    tile = lax.axis_index("ty")

    def edge_mask(at):
        return jnp.where(is_last & (jnp.broadcast_to(tile, (8, 128)) == at), none, one)

    mask_right, mask_left = edge_mask(lax.axis_size("ty") - 1), edge_mask(0)
    for c in loads:
        c.wait()

    def tiles(ref, at):
        return [ref[at, :, 128 * t : 128 * t + 128] for t in range(3)]

    def put(ref, at, v):
        for t in range(3):
            ref[at, :, 128 * t : 128 * t + 128] = v[t]

    def row_of(ref, b, u):
        return [wide(ref[b, u : u + 1, 128 * t : 128 * t + 128]) for t in range(3)]

    def step(src, dst):
        count = 8 * blocks // ROWS

        def body(i, carry):
            b_at = jnp.minimum(i, count - 1)
            c_at = jnp.maximum(i - 1, 0) * ROWS
            for u in range(ROWS):
                at = c_at + u
                s, fy = tiles(sum_s, at), tiles(fy_s, at)
                fr = [pltpu.roll(v, 1, 1) for v in fy]
                back = [jnp.where(is_first, fr[(t - 1) % 3], fr[t]) for t in range(3)]
                put(dst, at, [s[t] + (fy[t] - back[t]) for t in range(3)])
            p_old, h_old, c_old, fx_old = carry
            for u in range(ROWS):
                at = b_at * ROWS + u
                block = (b_at * (ROWS // 8) + u // 8, u % 8)
                p = tiles(src, at + 1)
                raw = [pltpu.roll(v, 127, 1) for v in p]
                pr = [jnp.where(is_last, raw[(t + 1) % 3], raw[t]) for t in range(3)]
                e, er = row_of(e_s, *block), row_of(er_s, *block)
                k, kr = row_of(k_s, *block), row_of(kr_s, *block)
                w = tiles(w_s, at)
                h = [p[t] + e[t] for t in range(3)]
                c = [k[t] * jnp.tanh(p[t]) + k[t] for t in range(3)]
                fy = [
                    (c[t] + (kr[t] * jnp.tanh(pr[t]) + kr[t])) * ((pr[t] + er[t]) - h[t])
                    for t in range(3)
                ]
                fy[1] = fy[1] * mask_right
                fy[2] = fy[2] * mask_left
                fx = [(c_old[t] + c[t]) * (h[t] - h_old[t]) for t in range(3)]
                put(sum_s, at, [(p_old[t] + w[t]) + (fx[t] - fx_old[t]) for t in range(3)])
                put(fy_s, at + 1, fy)
                p_old, h_old, c_old, fx_old = p, h, c, fx
            return p_old, h_old, c_old, fx_old

        zero = [jnp.zeros((8, 128), F32)] * 3
        lax.fori_loop(0, count + 1, body, (zero, zero, zero, zero))

    for s in range(SUBSTEPS):
        step(*((p0, p1) if s % 2 == 0 else (p1, p0)))
    last = p0 if SUBSTEPS % 2 == 0 else p1

    def leave(i, _):
        x = pl.multiple_of(i * 8, 8)
        for u in range(8):
            row = last[x + 9 + u, :, 0:256] * F32(2)
            out_ref[2 * x + 2 * u] = row[:, 0:128]
            out_ref[2 * x + 2 * u + 1] = row[:, 128:256]
            round_ref[x + u] = row.astype(BF16)
        return 0

    lax.fori_loop(0, size_x // 8, leave, 0)


def run_steps(pt, wt, e, k, above, below, from_left, from_right):
    size_x, members, size_y = pt.shape
    tile = pltpu.VMEM((size_x + 17, members, size_y + 128), F32)
    flat = pltpu.VMEM((size_x // 8 + 2, 8, size_y + 128), F32)
    return pl.pallas_call(
        steps_kernel,
        in_specs=[HBM_SPEC] * 2 + [VMEM_SPEC] * 6,
        out_specs=[VMEM_SPEC] * 2,
        scratch_shapes=[tile] * 5 + [flat] * 4 + [pltpu.SemaphoreType.DMA((2,))],
        out_shape=[
            jax.ShapeDtypeStruct((size_x * (size_y // 128), members, 128), F32),
            jax.ShapeDtypeStruct((size_x, members, size_y), BF16),
        ],
        compiler_params=pltpu.CompilerParams(vmem_limit_bytes=50 * 2**20),
        name="steps",
    )(pt, wt, e, k, above, below, from_left, from_right)


def pick_kernel(code_ref, f_ref, inside_ref, pick_ref):
    lane = lanes()

    def pick(g, _):
        acc = jnp.zeros((8, 128), F32)
        for u in range(128):
            code = code_ref[g, u]
            v = pltpu.roll(f_ref[lax.shift_right_logical(code, 7)], code & 127, 1)
            acc = jnp.where(lane == u, v, acc)
        keep = wide(inside_ref[pl.ds(g, 1), :]) > F32(0.5)
        pick_ref[:, pl.ds(pl.multiple_of(g * 128, 128), 128)] = jnp.where(keep, acc, F32(0))
        return 0

    lax.fori_loop(0, code_ref.shape[0], pick, 0)


def picks(code, forecast, inside):
    return pl.pallas_call(
        pick_kernel,
        grid_spec=pltpu.PrefetchScalarGridSpec(
            num_scalar_prefetch=1, grid=(), in_specs=[VMEM_SPEC] * 2, out_specs=VMEM_SPEC
        ),
        out_shape=jax.ShapeDtypeStruct((8, code.size), F32),
        compiler_params=pltpu.CompilerParams(vmem_limit_bytes=8 * 2**20),
        name="picks",
    )(code, forecast, inside)


def weights_kernel(near_ref, far_ref, innovation_ref, out_ref, x_s, m_s):
    half = near_ref.shape[0]
    members = 2 * half
    blocks = members // 8
    parts = [r[8 * b : 8 * b + 8, :] for r in (near_ref, far_ref) for b in range(half // 8)]
    total = parts[0]
    for part in parts[1:]:
        total = total + part
    mean = jnp.sum(total, axis=0, keepdims=True) * F32(1.0 / members)
    for b, part in enumerate(parts):
        x_s[8 * b : 8 * b + 8, :] = part - mean
    x = x_s[...]
    dims = (((1,), (1,)), ((), ()))
    dot = functools.partial(
        lax.dot_general, dimension_numbers=dims, precision=lax.Precision.HIGHEST,
        preferred_element_type=F32,
    )
    r = lax.broadcasted_iota(jnp.int32, (members, members), 0)
    c = lax.broadcasted_iota(jnp.int32, (members, members), 1)
    m_s[:, 0:members] = dot(x, x) + jnp.where(r == c, F32(members - 1), F32(0))
    m_s[:, members : 2 * members] = jnp.zeros((members, members), F32)
    m_s[:, members : members + 8] = dot(x, innovation_ref[...])
    m = [m_s[8 * b : 8 * b + 8, :] for b in range(blocks)]
    sub = sublanes()
    for kb in range(blocks):
        cols = [
            [jnp.broadcast_to(m[b][:, 8 * kb + j : 8 * kb + j + 1], (8, 128)) for j in range(8)]
            for b in range(blocks)
        ]
        rows = m[kb]
        piv = list(cols[kb])
        for j in range(8):
            inv = F32(1) / wide(piv[j][j : j + 1])
            here = sub == j
            factor = piv[j]
            top = wide(rows[j : j + 1]) * inv
            rows = jnp.where(here, top, rows - factor * top)
            for q in range(j + 1, 8):
                top = wide(piv[q][j : j + 1]) * inv
                piv[q] = jnp.where(here, top, piv[q] - factor * top)
        spread = [wide(rows[j : j + 1]) for j in range(8)]
        for b in range(blocks):
            if b == kb:
                m[b] = rows
            else:
                acc = cols[b][0] * spread[0]
                for j in range(1, 8):
                    acc = acc + cols[b][j] * spread[j]
                m[b] = m[b] - acc
    for b in range(blocks):
        m_s[8 * b : 8 * b + 8, :] = m[b]
    turned = jnp.transpose(m_s[...], (1, 0))
    out_ref[:, 0:members] = turned[members : members + 8, :]


def solve_weights(near, far, innovation):
    half, n_obs = near.shape
    members = 2 * half
    return pl.pallas_call(
        weights_kernel,
        in_specs=[VMEM_SPEC] * 3,
        out_specs=VMEM_SPEC,
        scratch_shapes=[
            pltpu.VMEM((members, n_obs), F32),
            pltpu.VMEM((members, 2 * members), F32),
        ],
        out_shape=jax.ShapeDtypeStruct((8, members), F32),
        name="weights",
    )(near, far, innovation)


def update_kernel(w_ref, *refs):
    pieces, f_ref, out_ref, row_s = refs[:10], refs[10], refs[11], refs[12]
    own, a, b, c, d, o, a2, b2, c2, d2 = pieces
    low = pl.program_id(0) < pl.num_programs(0) // 2
    w = w_ref[...].astype(BF16)
    for r in range(row_s.shape[0]):
        parts = [
            own[r], a[r], b[r], jnp.where(low, c[r].astype(F32), d[r].astype(F32)),
            o[r], a2[r], b2[r], jnp.where(low, c2[r].astype(F32), d2[r].astype(F32)),
        ]
        rows = jnp.concatenate([v.astype(F32) for v in parts], axis=0).astype(BF16)
        shift = jnp.dot(w, rows, preferred_element_type=F32)
        for t in range(2):
            cols = slice(128 * t, 128 * t + 128)
            row_s[r, :, cols] = f_ref[2 * r + t] + shift[:, cols]
    out_ref[...] = jnp.swapaxes(row_s[...], 0, 1)


def update(weights, pieces, forecast):
    size_x, members, size_y = pieces[0].shape
    step = 32
    count = size_x // step
    shape = (step, members, size_y)
    whole = pl.BlockSpec(shape, lambda g: (g, 0, 0))
    first = pl.BlockSpec(shape, lambda g: (jnp.minimum(g, count // 2 - 1), 0, 0))
    second = pl.BlockSpec(shape, lambda g: (jnp.maximum(g - count // 2, 0), 0, 0))
    five = [whole] * 3 + [first, second]
    return pl.pallas_call(
        update_kernel,
        grid=(count,),
        in_specs=[pl.BlockSpec(weights.shape, lambda g: (0, 0))] + five + five
        + [pl.BlockSpec((2 * step, members, 128), lambda g: (g, 0, 0))],
        out_specs=pl.BlockSpec((members, step, size_y), lambda g: (0, g, 0)),
        out_shape=jax.ShapeDtypeStruct((members, size_x, size_y), F32),
        scratch_shapes=[pltpu.VMEM(shape, F32)],
        name="update",
    )(weights, *pieces, forecast)


def local(pressure, elevation, ks_field, melt_rate, obs_index, obs_value, obs_error, perturbation):
    members, size_x, size_y = pressure.shape
    n_x, n_y, n_m = (lax.axis_size(a) for a in ("tx", "ty", "mem"))
    tile_x, tile_y = lax.axis_index("tx"), lax.axis_index("ty")
    def ring(n, by):
        return [(i, (i + by) % n) for i in range(n)]

    n_obs = obs_index.shape[0]
    top, bottom, code, inside = ends(
        obs_index.reshape(n_obs // 128, 128), pressure, melt_rate, elevation, ks_field
    )
    up = lax.ppermute(bottom, "tx", ring(n_x, 1))
    down = lax.ppermute(top, "tx", ring(n_x, -1))
    pt, wt, left, right = turn(pressure, melt_rate, elevation, ks_field)
    above, below, left, right = halo_rows(up, down, top, bottom, left, right)
    from_left = lax.ppermute(right, "ty", ring(n_y, 1))
    from_right = lax.ppermute(left, "ty", ring(n_y, -1))
    forecast, rounded = run_steps(
        pt, wt, elevation, ks_field, above, below, from_left, from_right
    )
    picked = picks(code, forecast, inside)

    block = n_obs // (n_x * n_y)
    tile = tile_x * n_y + tile_y
    mine = jnp.concatenate(
        [
            (obs_value[:, None] + obs_error[:, None] * perturbation).T,
            jnp.broadcast_to(obs_error[None], (8, block)),
        ]
    )
    mine = lax.dynamic_update_slice(jnp.zeros((16, n_obs), F32), mine, (0, tile * block))
    line = jnp.concatenate([picked, mine])
    for axis, n in (("ty", n_y), ("tx", n_x)):
        bit = 1
        while bit < n:
            line = line + lax.ppermute(line, axis, [(i, i ^ bit) for i in range(n)])
            bit *= 2
    observed, target, error = line[0:8], line[8:16], line[16:17]
    innovation = (target - observed) / error
    scaled = observed / error

    def chips(by):
        return [(i, (i + 2 * by) % n_m) for i in range(n_m)]

    swap = [(i, i ^ 1) for i in range(n_m)]

    def send(v, to):
        return lax.ppermute(v, "mem", to)

    half = size_x // 2
    a, b, o = send(rounded, chips(1)), send(rounded, chips(-1)), send(rounded, swap)
    near = jnp.concatenate([scaled] + [send(scaled, chips(by)) for by in (1, -1, 2)])
    near, a, b = lax.optimization_barrier((near, a, b))
    far = send(near, swap)
    c, d = send(a[:half], chips(1)), send(b[half:], chips(-1))
    a2, b2 = send(a, swap), send(b, swap)
    weights = solve_weights(near, far, innovation)
    weights, c, d, o, a2, b2 = lax.optimization_barrier((weights, c, d, o, a2, b2))
    pieces = (rounded, a, b, c, d, o, a2, b2, send(c, swap), send(d, swap))
    pieces = [pltpu.with_memory_space_constraint(v, pltpu.HBM) for v in pieces]
    return update(weights, pieces, forecast)


def solution(mesh):
    placed = (
        P("mem", "tx", "ty"),
        P("tx", "ty"),
        P("tx", "ty"),
        P("mem", "tx", "ty"),
        P(),
        P(("tx", "ty")),
        P(("tx", "ty")),
        P(("tx", "ty"), "mem"),
    )
    return jax.shard_map(
        local, mesh=mesh, in_specs=placed, out_specs=P("mem", "tx", "ty"), check_vma=False
    )
```

```python
import functools

import jax
import jax.numpy as jnp
from jax import lax
from jax.experimental import pallas as pl
from jax.experimental.pallas import tpu as pltpu
from jax.sharding import PartitionSpec as P

SUBSTEPS = 4
W = SUBSTEPS
GROUP = 128 // W
ROWS = 16
F32 = jnp.float32
BF16 = jnp.bfloat16
VMEM_SPEC = pl.BlockSpec(memory_space=pltpu.VMEM)
HBM_SPEC = pl.BlockSpec(memory_space=pltpu.HBM)


def lanes():
    return lax.broadcasted_iota(jnp.int32, (8, 128), 1)


def sublanes():
    return lax.broadcasted_iota(jnp.int32, (8, 128), 0)


def wide(row):
    return jnp.broadcast_to(row, (8, 128))


def ends_kernel(
    obs_ref, p_ref, w_ref, e_ref, k_ref, top_ref, bottom_ref, code_ref, inside_ref,
    cubes, sems,
):
    members, size_x, size_y = p_ref.shape
    copies = []
    for i, lo in enumerate((0, size_x - 8)):
        for j, ref in enumerate((p_ref, w_ref)):
            copies.append((ref.at[:, pl.ds(lo, 8), :], cubes.at[2 * i + j]))
    copies = [pltpu.make_async_copy(a, b, sems.at[n]) for n, (a, b) in enumerate(copies)]
    for c in copies:
        c.start()
    bits_x, bits_y = size_x.bit_length() - 1, size_y.bit_length() - 1
    total_y = size_y * lax.axis_size("ty")
    obs = obs_ref[...]
    x = lax.shift_right_logical(obs, total_y.bit_length() - 1)
    y = obs & (total_y - 1)
    mine = (lax.shift_right_logical(x, bits_x) == lax.axis_index("tx")) & (
        lax.shift_right_logical(y, bits_y) == lax.axis_index("ty")
    )
    x, y = x & (size_x - 1), y & (size_y - 1)
    tile = x * (size_y // 128) + lax.shift_right_logical(y, 7)
    code_ref[...] = tile * 128 + ((lanes() - y) & 127)
    inside_ref[...] = jnp.where(mine, F32(1), F32(0))
    for c in copies:
        c.wait()
    sub = lax.broadcasted_iota(jnp.int32, (8, size_y), 0)
    for i, out in enumerate((top_ref, bottom_ref)):
        for j in range(2):
            turned = jnp.swapaxes(cubes[2 * i + j], 0, 1)
            for r in range(W):
                out[j * W + r] = turned[r if i == 0 else 8 - W + r]
        lo = (0, size_x - 8)[i]
        e, k = e_ref[lo : lo + 8, :], k_ref[lo : lo + 8, :]
        if i == 0:
            k = pltpu.roll(k, 4, 0)
        else:
            e = pltpu.roll(e, 4, 0)
        out[2 * W] = jnp.where(sub < 4, e, k)


def ends(obs, p, w, e, k):
    members, size_x, size_y = p.shape
    edge = jax.ShapeDtypeStruct((2 * W + 1, members, size_y), F32)
    return pl.pallas_call(
        ends_kernel,
        in_specs=[VMEM_SPEC] + [HBM_SPEC] * 2 + [VMEM_SPEC] * 2,
        out_specs=[VMEM_SPEC] * 4,
        out_shape=[
            edge, edge, jax.ShapeDtypeStruct(obs.shape, jnp.int32),
            jax.ShapeDtypeStruct(obs.shape, F32),
        ],
        scratch_shapes=[
            pltpu.VMEM((4, members, 8, size_y), F32),
            pltpu.SemaphoreType.DMA((4,)),
        ],
        compiler_params=pltpu.CompilerParams(vmem_limit_bytes=56 * 2**20),
        name="ends",
    )(obs, p, w, e, k)


def pack_rows(rows):
    slot = lanes() // W
    left = jnp.zeros((8, 128), F32)
    right = jnp.zeros((8, 128), F32)
    for r, a, b in rows:
        if r:
            a = pltpu.roll(a, W * r, 1)
            b = pltpu.roll(b, W * r, 1)
        left = jnp.where(slot == r, a, left)
        right = jnp.where(slot == (r - 1) % GROUP, b, right)
    return left, right


def turn_kernel(
    p_in, w_in, e_ref, k_ref, pt_out, wt_out, left_ref, right_ref,
    p_ref, w_ref, pt_ref, wt_ref, in_sems, out_sems,
):
    groups = left_ref.shape[0]

    def rows_of(g):
        return pl.ds(pl.multiple_of(g * GROUP, GROUP), GROUP)

    def fetch(g, f):
        src, dst = ((p_in, p_ref), (w_in, w_ref))[f]
        at = rows_of(g)
        return pltpu.make_async_copy(src.at[:, at, :], dst.at[:, at, :], in_sems.at[f, g])

    def leave(g, f):
        src, dst = ((pt_ref, pt_out), (wt_ref, wt_out))[f]
        at = rows_of(g)
        return pltpu.make_async_copy(src.at[at], dst.at[at], out_sems.at[f, g])

    for g in range(groups):
        for f in range(2):
            fetch(g, f).start()

    def group(g, _):
        at = rows_of(g)
        for f, (src, dst) in enumerate(((p_ref, pt_ref), (w_ref, wt_ref))):
            fetch(g, f).wait()
            rows = jnp.swapaxes(src[:, at, :] * F32(0.5), 0, 1)
            dst[at] = rows
            left_ref[g, f], right_ref[g, f] = pack_rows(
                (r, rows[r, :, 0:128], rows[r, :, 128:256]) for r in range(GROUP)
            )
            leave(g, f).start()
        fields = []
        for base, ref, factor in ((0, e_ref, 0.5), (4, k_ref, 0.25)):
            block = ref[at, :] * F32(factor)
            for q in range(GROUP // 8):
                part = block[8 * q : 8 * q + 8]
                fields.append((base + q, part[:, 0:128], part[:, 128:256]))
        left_ref[g, 2], right_ref[g, 2] = pack_rows(fields)
        return 0

    lax.fori_loop(0, groups, group, 0)
    for g in range(groups):
        for f in range(2):
            leave(g, f).wait()


def turn(p, w, e, k):
    members, size_x, size_y = p.shape
    groups = size_x // GROUP
    turned = (size_x, members, size_y)
    return pl.pallas_call(
        turn_kernel,
        in_specs=[HBM_SPEC] * 2 + [VMEM_SPEC] * 2,
        out_specs=[HBM_SPEC] * 2 + [VMEM_SPEC] * 2,
        out_shape=[jax.ShapeDtypeStruct(turned, F32)] * 2
        + [jax.ShapeDtypeStruct((groups, 3, 8, 128), F32)] * 2,
        scratch_shapes=[pltpu.VMEM(p.shape, F32)] * 2 + [pltpu.VMEM(turned, F32)] * 2
        + [pltpu.SemaphoreType.DMA((2, groups))] * 2,
        cost_estimate=pl.CostEstimate(flops=10**7, bytes_accessed=9 * 2**20, transcendentals=0),
        compiler_params=pltpu.CompilerParams(vmem_limit_bytes=52 * 2**20),
        name="turn",
    )(p, w, e, k)


def rows_kernel(
    up_ref, down_ref, top_ref, bottom_ref, left_in, right_in, above_ref, below_ref,
    left_ref, right_ref,
):
    tile, groups = lax.axis_index("tx"), left_in.shape[0]
    first, last = tile == 0, tile == lax.axis_size("tx") - 1
    left_ref[0:groups] = left_in[...]
    right_ref[0:groups] = right_in[...]
    sub = lax.broadcasted_iota(jnp.int32, (8, 256), 0)

    def mirrored(block):
        out = block
        for i in range(4):
            for base in (0, 4):
                row = block[base + 3 - i : base + 4 - i, :]
                out = jnp.where(sub == base + i, jnp.broadcast_to(row, (8, 256)), out)
        return out

    for flag, got, own, out in (
        (first, up_ref, top_ref, above_ref),
        (last, down_ref, bottom_ref, below_ref),
    ):
        for f in range(2):
            for i in range(W):
                row = jnp.where(flag, own[f * W + W - 1 - i], got[f * W + i])
                out[f * W + i] = row * F32(0.5)
        block = jnp.where(flag, mirrored(own[2 * W]), got[2 * W])
        out[2 * W] = block * jnp.where(sub < 4, F32(0.5), F32(0.25))
    for f in range(2):
        left_ref[groups, f], right_ref[groups, f] = pack_rows(
            (half * W + i, out[f * W + i, :, 0:128], out[f * W + i, :, 128:256])
            for half, out in enumerate((above_ref, below_ref))
            for i in range(W)
        )
    above, below = above_ref[2 * W], below_ref[2 * W]
    e = jnp.where(sub < 4, above, pltpu.roll(below, 4, 0))
    k = jnp.where(sub < 4, pltpu.roll(above, 4, 0), below)
    left_ref[groups, 2], right_ref[groups, 2] = pack_rows(
        (slot, v[:, 0:128], v[:, 128:256]) for slot, v in ((0, e), (4, k))
    )


def halo_rows(up, down, top, bottom, left, right):
    packs = jax.ShapeDtypeStruct((left.shape[0] + 1, *left.shape[1:]), F32)
    return pl.pallas_call(
        rows_kernel,
        in_specs=[VMEM_SPEC] * 6,
        out_specs=[VMEM_SPEC] * 4,
        out_shape=[jax.ShapeDtypeStruct(up.shape, F32)] * 2 + [packs] * 2,
        compiler_params=pltpu.CompilerParams(vmem_limit_bytes=4 * 2**20),
        name="rows",
    )(up, down, top, bottom, left, right)


def steps_kernel(
    pt_in, wt_in, e_ref, k_ref, above_ref, below_ref, fl_ref, fr_ref,
    out_ref, round_ref,
    p0, p1, w_s, fy_s, sum_s, e_s, er_s, k_s, kr_s, sems,
):
    size_x = pt_in.shape[0]
    lane = lanes()
    is_first, is_last = lane == 0, lane == 127
    groups = size_x // GROUP
    blocks = size_x // 8 + 2
    inner = (pl.ds(9, size_x), slice(None), pl.ds(0, 256))
    loads = [
        pltpu.make_async_copy(src, dst.at[inner], sems.at[i])
        for i, (src, dst) in enumerate(((pt_in, p0), (wt_in, w_s)))
    ]
    for c in loads:
        c.start()

    def halo(g, f, r):
        a, b = fr_ref[g, f], fl_ref[g, f]
        if r:
            a = pltpu.roll(a, 128 - W * r, 1)
            b = pltpu.roll(b, 128 - W * r, 1)
        return jnp.where(lane < 64, a, b)

    def spread(at, v, here, shifted):
        rolled = [pltpu.roll(u, 127, 1) for u in v]
        for t in range(3):
            here[at, :, 128 * t : 128 * t + 128] = v[t]
            shifted[at, :, 128 * t : 128 * t + 128] = jnp.where(
                is_last, rolled[(t + 1) % 3], rolled[t]
            )

    def unpack_group(g, _):
        for r in range(GROUP):
            for f, dst in ((0, p0), (1, w_s)):
                dst[g * GROUP + r + 9, :, 256:384] = halo(g, f, r)
        for q in range(GROUP // 8):
            rows = pl.ds(pl.multiple_of(g * GROUP + 8 * q, 8), 8)
            for base, ref, factor, here, shifted in (
                (0, e_ref, 0.5, e_s, er_s), (4, k_ref, 0.25, k_s, kr_s),
            ):
                v = [ref[rows, 128 * t : 128 * t + 128] * F32(factor) for t in range(2)]
                spread(g * (GROUP // 8) + q + 1, v + [halo(g, 2, base + q)], here, shifted)
        return 0

    lax.fori_loop(0, groups, unpack_group, 0)
    for r in range(2 * W):
        ref, y = (above_ref, 4 + r) if r < W else (below_ref, size_x + 4 + r)
        for f, dst in ((0, p0), (1, w_s)):
            dst[y + 1, :, 0:256] = ref[f * W + r % W]
            dst[y + 1, :, 256:384] = halo(groups, f, r)
    for base, here, shifted in ((0, e_s, er_s), (4, k_s, kr_s)):
        edge = pltpu.roll(halo(groups, 2, base), 4, 0)
        for at, ref, up in ((0, above_ref, base == 0), (blocks - 1, below_ref, base == 4)):
            v = ref[2 * W]
            v = pltpu.roll(v, 4, 0) if up else v
            spread(at, [v[:, 0:128], v[:, 128:256], edge], here, shifted)

    one, none = F32(1), F32(0)

    tile = lax.axis_index("ty")

    def edge_mask(at):
        return jnp.where(is_last & (jnp.broadcast_to(tile, (8, 128)) == at), none, one)

    mask_right, mask_left = edge_mask(lax.axis_size("ty") - 1), edge_mask(0)
    for c in loads:
        c.wait()

    def tiles(ref, at):
        return [ref[at, :, 128 * t : 128 * t + 128] for t in range(3)]

    def put(ref, at, v):
        for t in range(3):
            ref[at, :, 128 * t : 128 * t + 128] = v[t]

    def row_of(ref, b, u):
        return [wide(ref[b, u : u + 1, 128 * t : 128 * t + 128]) for t in range(3)]

    def step(src, dst):
        count = 8 * blocks // ROWS

        def body(i, carry):
            b_at = jnp.minimum(i, count - 1)
            c_at = jnp.maximum(i - 1, 0) * ROWS
            for u in range(ROWS):
                at = c_at + u
                s, fy = tiles(sum_s, at), tiles(fy_s, at)
                fr = [pltpu.roll(v, 1, 1) for v in fy]
                back = [jnp.where(is_first, fr[(t - 1) % 3], fr[t]) for t in range(3)]
                put(dst, at, [s[t] + (fy[t] - back[t]) for t in range(3)])
            p_old, h_old, c_old, fx_old = carry
            for u in range(ROWS):
                at = b_at * ROWS + u
                block = (b_at * (ROWS // 8) + u // 8, u % 8)
                p = tiles(src, at + 1)
                raw = [pltpu.roll(v, 127, 1) for v in p]
                pr = [jnp.where(is_last, raw[(t + 1) % 3], raw[t]) for t in range(3)]
                e, er = row_of(e_s, *block), row_of(er_s, *block)
                k, kr = row_of(k_s, *block), row_of(kr_s, *block)
                w = tiles(w_s, at)
                h = [p[t] + e[t] for t in range(3)]
                c = [k[t] * jnp.tanh(p[t]) + k[t] for t in range(3)]
                fy = [
                    (c[t] + (kr[t] * jnp.tanh(pr[t]) + kr[t])) * ((pr[t] + er[t]) - h[t])
                    for t in range(3)
                ]
                fy[1] = fy[1] * mask_right
                fy[2] = fy[2] * mask_left
                fx = [(c_old[t] + c[t]) * (h[t] - h_old[t]) for t in range(3)]
                put(sum_s, at, [(p_old[t] + w[t]) + (fx[t] - fx_old[t]) for t in range(3)])
                put(fy_s, at + 1, fy)
                p_old, h_old, c_old, fx_old = p, h, c, fx
            return p_old, h_old, c_old, fx_old

        zero = [jnp.zeros((8, 128), F32)] * 3
        lax.fori_loop(0, count + 1, body, (zero, zero, zero, zero))

    for s in range(SUBSTEPS):
        step(*((p0, p1) if s % 2 == 0 else (p1, p0)))
    last = p0 if SUBSTEPS % 2 == 0 else p1

    def leave(i, _):
        x = pl.multiple_of(i * 8, 8)
        for u in range(8):
            row = last[x + 9 + u, :, 0:256] * F32(2)
            out_ref[2 * x + 2 * u] = row[:, 0:128]
            out_ref[2 * x + 2 * u + 1] = row[:, 128:256]
            round_ref[x + u] = row.astype(BF16)
        return 0

    lax.fori_loop(0, size_x // 8, leave, 0)


def run_steps(pt, wt, e, k, above, below, from_left, from_right):
    size_x, members, size_y = pt.shape
    tile = pltpu.VMEM((size_x + 17, members, size_y + 128), F32)
    flat = pltpu.VMEM((size_x // 8 + 2, 8, size_y + 128), F32)
    return pl.pallas_call(
        steps_kernel,
        in_specs=[HBM_SPEC] * 2 + [VMEM_SPEC] * 6,
        out_specs=[VMEM_SPEC] * 2,
        scratch_shapes=[tile] * 5 + [flat] * 4 + [pltpu.SemaphoreType.DMA((2,))],
        out_shape=[
            jax.ShapeDtypeStruct((size_x * (size_y // 128), members, 128), F32),
            jax.ShapeDtypeStruct((size_x, members, size_y), BF16),
        ],
        compiler_params=pltpu.CompilerParams(vmem_limit_bytes=50 * 2**20),
        name="steps",
    )(pt, wt, e, k, above, below, from_left, from_right)


def pick_kernel(code_ref, f_ref, inside_ref, pick_ref):
    lane = lanes()

    def pick(g, _):
        acc = jnp.zeros((8, 128), F32)
        for u in range(128):
            code = code_ref[g, u]
            v = pltpu.roll(f_ref[lax.shift_right_logical(code, 7)], code & 127, 1)
            acc = jnp.where(lane == u, v, acc)
        keep = wide(inside_ref[pl.ds(g, 1), :]) > F32(0.5)
        pick_ref[:, pl.ds(pl.multiple_of(g * 128, 128), 128)] = jnp.where(keep, acc, F32(0))
        return 0

    lax.fori_loop(0, code_ref.shape[0], pick, 0)


def picks(code, forecast, inside):
    return pl.pallas_call(
        pick_kernel,
        grid_spec=pltpu.PrefetchScalarGridSpec(
            num_scalar_prefetch=1, grid=(), in_specs=[VMEM_SPEC] * 2, out_specs=VMEM_SPEC
        ),
        out_shape=jax.ShapeDtypeStruct((8, code.size), F32),
        compiler_params=pltpu.CompilerParams(vmem_limit_bytes=8 * 2**20),
        name="picks",
    )(code, forecast, inside)


def weights_kernel(near_ref, far_ref, innovation_ref, first_ref, last_ref, x_s, m_s):
    half = near_ref.shape[0]
    members = 2 * half
    blocks = members // 8
    parts = [r[8 * b : 8 * b + 8, :] for r in (near_ref, far_ref) for b in range(half // 8)]
    total = parts[0]
    for part in parts[1:]:
        total = total + part
    mean = jnp.sum(total, axis=0, keepdims=True) * F32(1.0 / members)
    for b, part in enumerate(parts):
        x_s[8 * b : 8 * b + 8, :] = part - mean
    x = x_s[...]
    dims = (((1,), (1,)), ((), ()))
    dot = functools.partial(
        lax.dot_general, dimension_numbers=dims, precision=lax.Precision.HIGHEST,
        preferred_element_type=F32,
    )
    r = lax.broadcasted_iota(jnp.int32, (members, members), 0)
    c = lax.broadcasted_iota(jnp.int32, (members, members), 1)
    m_s[:, 0:members] = dot(x, x) + jnp.where(r == c, F32(members - 1), F32(0))
    m_s[:, members : 2 * members] = jnp.zeros((members, members), F32)
    m_s[:, members : members + 8] = dot(x, innovation_ref[...])
    m = [m_s[8 * b : 8 * b + 8, :] for b in range(blocks)]
    sub = sublanes()
    for kb in range(blocks):
        cols = [
            [jnp.broadcast_to(m[b][:, 8 * kb + j : 8 * kb + j + 1], (8, 128)) for j in range(8)]
            for b in range(blocks)
        ]
        rows = m[kb]
        piv = list(cols[kb])
        for j in range(8):
            inv = F32(1) / wide(piv[j][j : j + 1])
            here = sub == j
            factor = piv[j]
            top = wide(rows[j : j + 1]) * inv
            rows = jnp.where(here, top, rows - factor * top)
            for q in range(j + 1, 8):
                top = wide(piv[q][j : j + 1]) * inv
                piv[q] = jnp.where(here, top, piv[q] - factor * top)
        spread = [wide(rows[j : j + 1]) for j in range(8)]
        for b in range(blocks):
            if b == kb:
                m[b] = rows
            else:
                acc = cols[b][0] * spread[0]
                for j in range(1, 8):
                    acc = acc + cols[b][j] * spread[j]
                m[b] = m[b] - acc
    for b in range(blocks):
        m_s[8 * b : 8 * b + 8, :] = m[b]
    turned = jnp.transpose(m_s[...], (1, 0))
    turned = turned[members : members + 8, :]
    for h in range(2):
        at = h * half
        first_ref[:, h * (half - 8) : (h + 1) * (half - 8)] = turned[:, at : at + half - 8]
        last_ref[:, 8 * h : 8 * h + 8] = turned[:, at + half - 8 : at + half]


def solve_weights(near, far, innovation):
    half, n_obs = near.shape
    members = 2 * half
    return pl.pallas_call(
        weights_kernel,
        in_specs=[VMEM_SPEC] * 3,
        out_specs=[VMEM_SPEC] * 2,
        scratch_shapes=[
            pltpu.VMEM((members, n_obs), F32),
            pltpu.VMEM((members, 2 * members), F32),
        ],
        out_shape=[
            jax.ShapeDtypeStruct((8, members - 16), F32), jax.ShapeDtypeStruct((8, 16), F32),
        ],
        name="weights",
    )(near, far, innovation)


def update_kernel(last, w_ref, *refs):
    pieces, (f_ref, out_ref) = refs[: len(refs) - 2 - last], refs[-2 - last : len(refs) - last]
    w = w_ref[...].astype(BF16)
    step = f_ref.shape[0] // 2
    at = pl.program_id(0) * step if last else 0
    for r in range(step):
        rows = jnp.concatenate([v[at + r].astype(F32) for v in pieces], axis=0).astype(BF16)
        shift = jnp.dot(w, rows, preferred_element_type=F32)
        for t in range(2):
            cols = slice(128 * t, 128 * t + 128)
            new = f_ref[2 * r + t] + shift[:, cols]
            if last:
                refs[-1][r, :, cols] = new
            else:
                out_ref[2 * r + t] = new
    if last:
        out_ref[...] = jnp.swapaxes(refs[-1][...], 0, 1)


def update(weights, pieces, forecast, last):
    size_x, members, size_y = pieces[0].shape
    step = 32
    shape = (step, members, size_y)
    tiles = pl.BlockSpec((2 * step, members, 128), lambda g: (g, 0, 0))
    return pl.pallas_call(
        functools.partial(update_kernel, last),
        grid=(size_x // step,),
        in_specs=[pl.BlockSpec(weights.shape, lambda g: (0, 0))]
        + [VMEM_SPEC if last else pl.BlockSpec(shape, lambda g: (g, 0, 0))] * len(pieces)
        + [tiles],
        out_specs=pl.BlockSpec((members, step, size_y), lambda g: (0, g, 0)) if last else tiles,
        out_shape=jax.ShapeDtypeStruct(
            (members, size_x, size_y) if last else forecast.shape, F32
        ),
        scratch_shapes=[pltpu.VMEM(shape, F32)] if last else [],
        name="update" if last else "begin",
    )(weights, *pieces, forecast)


def local(pressure, elevation, ks_field, melt_rate, obs_index, obs_value, obs_error, perturbation):
    members, size_x, size_y = pressure.shape
    n_x, n_y, n_m = (lax.axis_size(a) for a in ("tx", "ty", "mem"))
    tile_x, tile_y = lax.axis_index("tx"), lax.axis_index("ty")
    def ring(n, by):
        return [(i, (i + by) % n) for i in range(n)]

    n_obs = obs_index.shape[0]
    top, bottom, code, inside = ends(
        obs_index.reshape(n_obs // 128, 128), pressure, melt_rate, elevation, ks_field
    )
    up = lax.ppermute(bottom, "tx", ring(n_x, 1))
    down = lax.ppermute(top, "tx", ring(n_x, -1))
    pt, wt, left, right = turn(pressure, melt_rate, elevation, ks_field)
    above, below, left, right = halo_rows(up, down, top, bottom, left, right)
    from_left = lax.ppermute(right, "ty", ring(n_y, 1))
    from_right = lax.ppermute(left, "ty", ring(n_y, -1))
    forecast, rounded = run_steps(
        pt, wt, elevation, ks_field, above, below, from_left, from_right
    )
    picked = picks(code, forecast, inside)

    block = n_obs // (n_x * n_y)
    tile = tile_x * n_y + tile_y
    mine = jnp.concatenate(
        [
            (obs_value[:, None] + obs_error[:, None] * perturbation).T,
            jnp.broadcast_to(obs_error[None], (8, block)),
        ]
    )
    mine = lax.dynamic_update_slice(jnp.zeros((16, n_obs), F32), mine, (0, tile * block))
    line = jnp.concatenate([picked, mine])
    for axis, n in (("ty", n_y), ("tx", n_x)):
        bit = 1
        while bit < n:
            line = line + lax.ppermute(line, axis, [(i, i ^ bit) for i in range(n)])
            bit *= 2
    observed, target, error = line[0:8], line[8:16], line[16:17]
    innovation = (target - observed) / error
    scaled = observed / error

    def send(v, by, swap=False):
        to = [(i, (i + 2 * (by if i % 2 == 0 else -by)) % n_m) for i in range(n_m)]
        return lax.ppermute(v, "mem", [(i, i ^ 1) for i in range(n_m)] if swap else to)

    a, b = send(rounded, 1), send(rounded, -1)
    scaled, a, b = lax.optimization_barrier((scaled, a, b))
    c = send(a, 1)
    near = jnp.concatenate([scaled] + [send(scaled, by) for by in (1, -1, 2)])
    near, own, a, b = lax.optimization_barrier((near, rounded, a, b))
    far = send(near, 0, True)
    others = [send(v, 0, True) for v in (own, a, b)]
    w_first, w_last = solve_weights(near, far, innovation)
    w_first, c, *others = lax.optimization_barrier((w_first, c, *others))
    d = send(c, 0, True)
    begun = update(w_first, [own, a, b, *others], forecast, False)
    return update(w_last, [c, d], begun, True)


def solution(mesh):
    placed = (
        P("mem", "tx", "ty"),
        P("tx", "ty"),
        P("tx", "ty"),
        P("mem", "tx", "ty"),
        P(),
        P(("tx", "ty")),
        P(("tx", "ty")),
        P(("tx", "ty"), "mem"),
    )
    return jax.shard_map(
        local, mesh=mesh, in_specs=placed, out_specs=P("mem", "tx", "ty"), check_vma=False
    )
```

```python
import functools

import jax
import jax.numpy as jnp
from jax import lax
from jax.experimental import pallas as pl
from jax.experimental.pallas import tpu as pltpu
from jax.sharding import PartitionSpec as P

SUBSTEPS = 4
W = SUBSTEPS
GROUP = 128 // W
ROWS = 16
F32 = jnp.float32
BF16 = jnp.bfloat16
VMEM_SPEC = pl.BlockSpec(memory_space=pltpu.VMEM)
HBM_SPEC = pl.BlockSpec(memory_space=pltpu.HBM)


def lanes():
    return lax.broadcasted_iota(jnp.int32, (8, 128), 1)


def sublanes():
    return lax.broadcasted_iota(jnp.int32, (8, 128), 0)


def wide(row):
    return jnp.broadcast_to(row, (8, 128))


def ends_kernel(
    obs_ref, p_ref, w_ref, e_ref, k_ref, top_ref, bottom_ref, code_ref, inside_ref,
    cubes, sems,
):
    _, size_x, size_y = p_ref.shape
    copies = []
    for i, lo in enumerate((0, size_x - 8)):
        for j, ref in enumerate((p_ref, w_ref)):
            copies.append((ref.at[:, pl.ds(lo, 8), :], cubes.at[2 * i + j]))
    copies = [pltpu.make_async_copy(a, b, sems.at[n]) for n, (a, b) in enumerate(copies)]
    for c in copies:
        c.start()
    bits_x, bits_y = size_x.bit_length() - 1, size_y.bit_length() - 1
    total_y = size_y * lax.axis_size("ty")
    obs = obs_ref[...]
    x = lax.shift_right_logical(obs, total_y.bit_length() - 1)
    y = obs & (total_y - 1)
    mine = (lax.shift_right_logical(x, bits_x) == lax.axis_index("tx")) & (
        lax.shift_right_logical(y, bits_y) == lax.axis_index("ty")
    )
    x, y = x & (size_x - 1), y & (size_y - 1)
    tile = x * (size_y // 128) + lax.shift_right_logical(y, 7)
    code_ref[...] = tile * 128 + ((lanes() - y) & 127)
    inside_ref[...] = jnp.where(mine, F32(1), F32(0))
    for c in copies:
        c.wait()
    sub = lax.broadcasted_iota(jnp.int32, (8, size_y), 0)
    for i, out in enumerate((top_ref, bottom_ref)):
        for j in range(2):
            turned = jnp.swapaxes(cubes[2 * i + j], 0, 1)
            for r in range(W):
                out[j * W + r] = turned[r if i == 0 else 8 - W + r]
        lo = (0, size_x - 8)[i]
        e, k = e_ref[lo : lo + 8, :], k_ref[lo : lo + 8, :]
        if i == 0:
            k = pltpu.roll(k, 4, 0)
        else:
            e = pltpu.roll(e, 4, 0)
        out[2 * W] = jnp.where(sub < 4, e, k)


def ends(obs, p, w, e, k):
    members, _, size_y = p.shape
    edge = jax.ShapeDtypeStruct((2 * W + 1, members, size_y), F32)
    return pl.pallas_call(
        ends_kernel,
        in_specs=[VMEM_SPEC] + [HBM_SPEC] * 2 + [VMEM_SPEC] * 2,
        out_specs=[VMEM_SPEC] * 4,
        out_shape=[
            edge, edge, jax.ShapeDtypeStruct(obs.shape, jnp.int32),
            jax.ShapeDtypeStruct(obs.shape, F32),
        ],
        scratch_shapes=[
            pltpu.VMEM((4, members, 8, size_y), F32),
            pltpu.SemaphoreType.DMA((4,)),
        ],
        compiler_params=pltpu.CompilerParams(vmem_limit_bytes=56 * 2**20),
        name="ends",
    )(obs, p, w, e, k)


def pack_rows(rows):
    slot = lanes() // W
    left = jnp.zeros((8, 128), F32)
    right = jnp.zeros((8, 128), F32)
    for r, a, b in rows:
        if r:
            a = pltpu.roll(a, W * r, 1)
            b = pltpu.roll(b, W * r, 1)
        left = jnp.where(slot == r, a, left)
        right = jnp.where(slot == (r - 1) % GROUP, b, right)
    return left, right


def turn_kernel(
    p_in, w_in, e_ref, k_ref, pt_out, wt_out, left_ref, right_ref,
    p_ref, w_ref, pt_ref, wt_ref, in_sems, out_sems,
):
    groups = left_ref.shape[0]

    def rows_of(g):
        return pl.ds(pl.multiple_of(g * GROUP, GROUP), GROUP)

    def fetch(g, f):
        src, dst = ((p_in, p_ref), (w_in, w_ref))[f]
        at = rows_of(g)
        return pltpu.make_async_copy(src.at[:, at, :], dst.at[:, at, :], in_sems.at[f, g])

    def leave(g, f):
        src, dst = ((pt_ref, pt_out), (wt_ref, wt_out))[f]
        at = rows_of(g)
        return pltpu.make_async_copy(src.at[at], dst.at[at], out_sems.at[f, g])

    for g in range(groups):
        for f in range(2):
            fetch(g, f).start()

    def group(g, _):
        at = rows_of(g)
        for f, (src, dst) in enumerate(((p_ref, pt_ref), (w_ref, wt_ref))):
            fetch(g, f).wait()
            rows = jnp.swapaxes(src[:, at, :] * F32(0.5), 0, 1)
            dst[at] = rows
            left_ref[g, f], right_ref[g, f] = pack_rows(
                (r, rows[r, :, 0:128], rows[r, :, 128:256]) for r in range(GROUP)
            )
            leave(g, f).start()
        fields = []
        for base, ref, factor in ((0, e_ref, 0.5), (4, k_ref, 0.25)):
            block = ref[at, :] * F32(factor)
            for q in range(GROUP // 8):
                part = block[8 * q : 8 * q + 8]
                fields.append((base + q, part[:, 0:128], part[:, 128:256]))
        left_ref[g, 2], right_ref[g, 2] = pack_rows(fields)
        return 0

    lax.fori_loop(0, groups, group, 0)
    for g in range(groups):
        for f in range(2):
            leave(g, f).wait()


def turn(p, w, e, k):
    members, size_x, size_y = p.shape
    groups = size_x // GROUP
    turned = (size_x, members, size_y)
    return pl.pallas_call(
        turn_kernel,
        in_specs=[HBM_SPEC] * 2 + [VMEM_SPEC] * 2,
        out_specs=[HBM_SPEC] * 2 + [VMEM_SPEC] * 2,
        out_shape=[jax.ShapeDtypeStruct(turned, F32)] * 2
        + [jax.ShapeDtypeStruct((groups, 3, 8, 128), F32)] * 2,
        scratch_shapes=[pltpu.VMEM(p.shape, F32)] * 2 + [pltpu.VMEM(turned, F32)] * 2
        + [pltpu.SemaphoreType.DMA((2, groups))] * 2,
        cost_estimate=pl.CostEstimate(flops=10**7, bytes_accessed=9 * 2**20, transcendentals=0),
        compiler_params=pltpu.CompilerParams(vmem_limit_bytes=52 * 2**20),
        name="turn",
    )(p, w, e, k)


def rows_kernel(
    up_ref, down_ref, top_ref, bottom_ref, left_in, right_in, above_ref, below_ref,
    left_ref, right_ref,
):
    tile, groups = lax.axis_index("tx"), left_in.shape[0]
    first, last = tile == 0, tile == lax.axis_size("tx") - 1
    left_ref[0:groups] = left_in[...]
    right_ref[0:groups] = right_in[...]
    sub = lax.broadcasted_iota(jnp.int32, (8, 256), 0)

    def mirrored(block):
        out = block
        for i in range(4):
            for base in (0, 4):
                row = block[base + 3 - i : base + 4 - i, :]
                out = jnp.where(sub == base + i, jnp.broadcast_to(row, (8, 256)), out)
        return out

    for flag, got, own, out in (
        (first, up_ref, top_ref, above_ref),
        (last, down_ref, bottom_ref, below_ref),
    ):
        for f in range(2):
            for i in range(W):
                row = jnp.where(flag, own[f * W + W - 1 - i], got[f * W + i])
                out[f * W + i] = row * F32(0.5)
        block = jnp.where(flag, mirrored(own[2 * W]), got[2 * W])
        out[2 * W] = block * jnp.where(sub < 4, F32(0.5), F32(0.25))
    for f in range(2):
        left_ref[groups, f], right_ref[groups, f] = pack_rows(
            (half * W + i, out[f * W + i, :, 0:128], out[f * W + i, :, 128:256])
            for half, out in enumerate((above_ref, below_ref))
            for i in range(W)
        )
    above, below = above_ref[2 * W], below_ref[2 * W]
    e = jnp.where(sub < 4, above, pltpu.roll(below, 4, 0))
    k = jnp.where(sub < 4, pltpu.roll(above, 4, 0), below)
    left_ref[groups, 2], right_ref[groups, 2] = pack_rows(
        (slot, v[:, 0:128], v[:, 128:256]) for slot, v in ((0, e), (4, k))
    )


def halo_rows(up, down, top, bottom, left, right):
    packs = jax.ShapeDtypeStruct((left.shape[0] + 1, *left.shape[1:]), F32)
    return pl.pallas_call(
        rows_kernel,
        in_specs=[VMEM_SPEC] * 6,
        out_specs=[VMEM_SPEC] * 4,
        out_shape=[jax.ShapeDtypeStruct(up.shape, F32)] * 2 + [packs] * 2,
        compiler_params=pltpu.CompilerParams(vmem_limit_bytes=4 * 2**20),
        name="rows",
    )(up, down, top, bottom, left, right)


def steps_kernel(
    pt_in, wt_in, e_ref, k_ref, above_ref, below_ref, fl_ref, fr_ref,
    out_ref, round_ref,
    p0, p1, w_s, fy_s, sum_s, e_s, er_s, k_s, kr_s, sems,
):
    size_x = pt_in.shape[0]
    lane = lanes()
    is_first, is_last = lane == 0, lane == 127
    groups = size_x // GROUP
    blocks = size_x // 8 + 2
    inner = (pl.ds(9, size_x), slice(None), pl.ds(0, 256))
    loads = [
        pltpu.make_async_copy(src, dst.at[inner], sems.at[i])
        for i, (src, dst) in enumerate(((pt_in, p0), (wt_in, w_s)))
    ]
    for c in loads:
        c.start()

    def halo(g, f, r):
        a, b = fr_ref[g, f], fl_ref[g, f]
        if r:
            a = pltpu.roll(a, 128 - W * r, 1)
            b = pltpu.roll(b, 128 - W * r, 1)
        return jnp.where(lane < 64, a, b)

    def spread(at, v, here, shifted):
        rolled = [pltpu.roll(u, 127, 1) for u in v]
        for t in range(3):
            here[at, :, 128 * t : 128 * t + 128] = v[t]
            shifted[at, :, 128 * t : 128 * t + 128] = jnp.where(
                is_last, rolled[(t + 1) % 3], rolled[t]
            )

    def unpack_group(g, _):
        for r in range(GROUP):
            for f, dst in ((0, p0), (1, w_s)):
                dst[g * GROUP + r + 9, :, 256:384] = halo(g, f, r)
        for q in range(GROUP // 8):
            rows = pl.ds(pl.multiple_of(g * GROUP + 8 * q, 8), 8)
            for base, ref, factor, here, shifted in (
                (0, e_ref, 0.5, e_s, er_s), (4, k_ref, 0.25, k_s, kr_s),
            ):
                v = [ref[rows, 128 * t : 128 * t + 128] * F32(factor) for t in range(2)]
                spread(g * (GROUP // 8) + q + 1, v + [halo(g, 2, base + q)], here, shifted)
        return 0

    lax.fori_loop(0, groups, unpack_group, 0)
    for r in range(2 * W):
        ref, y = (above_ref, 4 + r) if r < W else (below_ref, size_x + 4 + r)
        for f, dst in ((0, p0), (1, w_s)):
            dst[y + 1, :, 0:256] = ref[f * W + r % W]
            dst[y + 1, :, 256:384] = halo(groups, f, r)
    for base, here, shifted in ((0, e_s, er_s), (4, k_s, kr_s)):
        edge = pltpu.roll(halo(groups, 2, base), 4, 0)
        for at, ref, up in ((0, above_ref, base == 0), (blocks - 1, below_ref, base == 4)):
            v = ref[2 * W]
            v = pltpu.roll(v, 4, 0) if up else v
            spread(at, [v[:, 0:128], v[:, 128:256], edge], here, shifted)

    one, none = F32(1), F32(0)

    tile = lax.axis_index("ty")

    def edge_mask(at):
        return jnp.where(is_last & (jnp.broadcast_to(tile, (8, 128)) == at), none, one)

    mask_right, mask_left = edge_mask(lax.axis_size("ty") - 1), edge_mask(0)
    for c in loads:
        c.wait()

    def tiles(ref, at):
        return [ref[at, :, 128 * t : 128 * t + 128] for t in range(3)]

    def put(ref, at, v):
        for t in range(3):
            ref[at, :, 128 * t : 128 * t + 128] = v[t]

    def row_of(ref, b, u):
        return [wide(ref[b, u : u + 1, 128 * t : 128 * t + 128]) for t in range(3)]

    def step(src, dst):
        count = 8 * blocks // ROWS

        def body(i, carry):
            b_at = jnp.minimum(i, count - 1)
            c_at = jnp.maximum(i - 1, 0) * ROWS
            for u in range(ROWS):
                at = c_at + u
                s, fy = tiles(sum_s, at), tiles(fy_s, at)
                fr = [pltpu.roll(v, 1, 1) for v in fy]
                back = [jnp.where(is_first, fr[(t - 1) % 3], fr[t]) for t in range(3)]
                put(dst, at, [s[t] + (fy[t] - back[t]) for t in range(3)])
            p_old, h_old, c_old, fx_old = carry
            for u in range(ROWS):
                at = b_at * ROWS + u
                block = (b_at * (ROWS // 8) + u // 8, u % 8)
                p = tiles(src, at + 1)
                raw = [pltpu.roll(v, 127, 1) for v in p]
                pr = [jnp.where(is_last, raw[(t + 1) % 3], raw[t]) for t in range(3)]
                e, er = row_of(e_s, *block), row_of(er_s, *block)
                k, kr = row_of(k_s, *block), row_of(kr_s, *block)
                w = tiles(w_s, at)
                h = [p[t] + e[t] for t in range(3)]
                c = [k[t] * jnp.tanh(p[t]) + k[t] for t in range(3)]
                fy = [
                    (c[t] + (kr[t] * jnp.tanh(pr[t]) + kr[t])) * ((pr[t] + er[t]) - h[t])
                    for t in range(3)
                ]
                fy[1] = fy[1] * mask_right
                fy[2] = fy[2] * mask_left
                fx = [(c_old[t] + c[t]) * (h[t] - h_old[t]) for t in range(3)]
                put(sum_s, at, [(p_old[t] + w[t]) + (fx[t] - fx_old[t]) for t in range(3)])
                put(fy_s, at + 1, fy)
                p_old, h_old, c_old, fx_old = p, h, c, fx
            return p_old, h_old, c_old, fx_old

        zero = [jnp.zeros((8, 128), F32)] * 3
        lax.fori_loop(0, count + 1, body, (zero, zero, zero, zero))

    for s in range(SUBSTEPS):
        step(*((p0, p1) if s % 2 == 0 else (p1, p0)))
    last = p0 if SUBSTEPS % 2 == 0 else p1

    def leave(i, _):
        x = pl.multiple_of(i * 8, 8)
        for u in range(8):
            row = last[x + 9 + u, :, 0:256] * F32(2)
            out_ref[2 * x + 2 * u] = row[:, 0:128]
            out_ref[2 * x + 2 * u + 1] = row[:, 128:256]
            round_ref[x + u] = row.astype(BF16)
        return 0

    lax.fori_loop(0, size_x // 8, leave, 0)


def run_steps(pt, wt, e, k, above, below, from_left, from_right):
    size_x, members, size_y = pt.shape
    tile = pltpu.VMEM((size_x + 17, members, size_y + 128), F32)
    flat = pltpu.VMEM((size_x // 8 + 2, 8, size_y + 128), F32)
    return pl.pallas_call(
        steps_kernel,
        in_specs=[HBM_SPEC] * 2 + [VMEM_SPEC] * 6,
        out_specs=[VMEM_SPEC] * 2,
        scratch_shapes=[tile] * 5 + [flat] * 4 + [pltpu.SemaphoreType.DMA((2,))],
        out_shape=[
            jax.ShapeDtypeStruct((size_x * (size_y // 128), members, 128), F32),
            jax.ShapeDtypeStruct((size_x, members, size_y), BF16),
        ],
        compiler_params=pltpu.CompilerParams(vmem_limit_bytes=50 * 2**20),
        name="steps",
    )(pt, wt, e, k, above, below, from_left, from_right)


def pick_kernel(code_ref, f_ref, inside_ref, pick_ref):
    lane = lanes()

    def pick(g, _):
        acc = jnp.zeros((8, 128), F32)
        for u in range(128):
            code = code_ref[g, u]
            v = pltpu.roll(f_ref[lax.shift_right_logical(code, 7)], code & 127, 1)
            acc = jnp.where(lane == u, v, acc)
        keep = wide(inside_ref[pl.ds(g, 1), :]) > F32(0.5)
        pick_ref[:, pl.ds(pl.multiple_of(g * 128, 128), 128)] = jnp.where(keep, acc, F32(0))
        return 0

    lax.fori_loop(0, code_ref.shape[0], pick, 0)


def picks(code, forecast, inside):
    return pl.pallas_call(
        pick_kernel,
        grid_spec=pltpu.PrefetchScalarGridSpec(
            num_scalar_prefetch=1, grid=(), in_specs=[VMEM_SPEC] * 2, out_specs=VMEM_SPEC
        ),
        out_shape=jax.ShapeDtypeStruct((8, code.size), F32),
        compiler_params=pltpu.CompilerParams(vmem_limit_bytes=8 * 2**20),
        name="picks",
    )(code, forecast, inside)


def weights_kernel(near_ref, far_ref, innovation_ref, out_ref, x_s, m_s):
    half = near_ref.shape[0]
    members = 2 * half
    blocks = members // 8
    parts = [r[8 * b : 8 * b + 8, :] for r in (near_ref, far_ref) for b in range(half // 8)]
    total = parts[0]
    for part in parts[1:]:
        total = total + part
    mean = jnp.sum(total, axis=0, keepdims=True) * F32(1.0 / members)
    for b, part in enumerate(parts):
        x_s[8 * b : 8 * b + 8, :] = part - mean
    x = x_s[...]
    dims = (((1,), (1,)), ((), ()))
    dot = functools.partial(
        lax.dot_general, dimension_numbers=dims, precision=lax.Precision.HIGHEST,
        preferred_element_type=F32,
    )
    r = lax.broadcasted_iota(jnp.int32, (members, members), 0)
    c = lax.broadcasted_iota(jnp.int32, (members, members), 1)
    m_s[:, 0:members] = dot(x, x) + jnp.where(r == c, F32(members - 1), F32(0))
    m_s[:, members : 2 * members] = jnp.zeros((members, members), F32)
    m_s[:, members : members + 8] = dot(x, innovation_ref[...])
    m = [m_s[8 * b : 8 * b + 8, :] for b in range(blocks)]
    sub = sublanes()
    for kb in range(blocks):
        cols = [
            [jnp.broadcast_to(m[b][:, 8 * kb + j : 8 * kb + j + 1], (8, 128)) for j in range(8)]
            for b in range(blocks)
        ]
        rows = m[kb]
        piv = list(cols[kb])
        for j in range(8):
            inv = F32(1) / wide(piv[j][j : j + 1])
            here = sub == j
            factor = piv[j]
            top = wide(rows[j : j + 1]) * inv
            rows = jnp.where(here, top, rows - factor * top)
            for q in range(j + 1, 8):
                top = wide(piv[q][j : j + 1]) * inv
                piv[q] = jnp.where(here, top, piv[q] - factor * top)
        spread = [wide(rows[j : j + 1]) for j in range(8)]
        for b in range(blocks):
            if b == kb:
                m[b] = rows
            else:
                acc = cols[b][0] * spread[0]
                for j in range(1, 8):
                    acc = acc + cols[b][j] * spread[j]
                m[b] = m[b] - acc
    for b in range(blocks):
        m_s[8 * b : 8 * b + 8, :] = m[b]
    turned = jnp.transpose(m_s[...], (1, 0))
    out_ref[...] = turned[members : members + 8, 0:members]


def solve_weights(near, far, innovation):
    half, n_obs = near.shape
    members = 2 * half
    return pl.pallas_call(
        weights_kernel,
        in_specs=[VMEM_SPEC] * 3,
        out_specs=VMEM_SPEC,
        scratch_shapes=[
            pltpu.VMEM((members, n_obs), F32),
            pltpu.VMEM((members, 2 * members), F32),
        ],
        out_shape=jax.ShapeDtypeStruct((8, members), F32),
        compiler_params=pltpu.CompilerParams(vmem_limit_bytes=4 * 2**20),
        name="weights",
    )(near, far, innovation)


def update_kernel(w_ref, *refs):
    pieces, (f_ref, out_ref, row_s, done_s, sems) = refs[:-5], refs[-5:]
    step = row_s.shape[0]
    w = w_ref[...].astype(BF16)

    def leave(g):
        at = pl.ds(pl.multiple_of(g * step, step), step)
        return pltpu.make_async_copy(done_s.at[:, at, :], out_ref.at[:, at, :], sems.at[g])

    def chunk(g, _):
        x = g * step
        for r in range(step):
            rows = jnp.concatenate([v[x + r].astype(F32) for v in pieces], axis=0).astype(BF16)
            shift = jnp.dot(w, rows, preferred_element_type=F32)
            for t in range(2):
                cols = slice(128 * t, 128 * t + 128)
                row_s[r, :, cols] = f_ref[2 * (x + r) + t] + shift[:, cols]
        at = pl.ds(pl.multiple_of(x, step), step)
        done_s[:, at, :] = jnp.swapaxes(row_s[...], 0, 1)
        leave(g).start()
        return 0

    count = pieces[0].shape[0] // step
    lax.fori_loop(0, count, chunk, 0)
    for g in range(count):
        leave(g).wait()


def update(weights, pieces, forecast):
    size_x, members, size_y = pieces[0].shape
    step = 32
    whole = (members, size_x, size_y)
    return pl.pallas_call(
        update_kernel,
        in_specs=[VMEM_SPEC] * (len(pieces) + 2),
        out_specs=HBM_SPEC,
        out_shape=jax.ShapeDtypeStruct(whole, F32),
        scratch_shapes=[
            pltpu.VMEM((step, members, size_y), F32),
            pltpu.VMEM(whole, F32),
            pltpu.SemaphoreType.DMA((size_x // step,)),
        ],
        compiler_params=pltpu.CompilerParams(vmem_limit_bytes=8 * 2**20),
        name="update",
    )(weights, *pieces, forecast)


def local(pressure, elevation, ks_field, melt_rate, obs_index, obs_value, obs_error, perturbation):
    n_x, n_y, n_m = (lax.axis_size(a) for a in ("tx", "ty", "mem"))
    tile_x, tile_y = lax.axis_index("tx"), lax.axis_index("ty")

    def ring(n, by):
        return [(i, (i + by) % n) for i in range(n)]

    n_obs = obs_index.shape[0]
    top, bottom, code, inside = ends(
        obs_index.reshape(n_obs // 128, 128), pressure, melt_rate, elevation, ks_field
    )
    up = lax.ppermute(bottom, "tx", ring(n_x, 1))
    down = lax.ppermute(top, "tx", ring(n_x, -1))
    pt, wt, left, right = turn(pressure, melt_rate, elevation, ks_field)
    above, below, left, right = halo_rows(up, down, top, bottom, left, right)
    from_left = lax.ppermute(right, "ty", ring(n_y, 1))
    from_right = lax.ppermute(left, "ty", ring(n_y, -1))
    forecast, rounded = run_steps(
        pt, wt, elevation, ks_field, above, below, from_left, from_right
    )
    picked = picks(code, forecast, inside)

    def send(v, by, swap=False):
        to = [(i, (i + 2 * (by if i % 2 == 0 else -by)) % n_m) for i in range(n_m)]
        return lax.ppermute(v, "mem", [(i, i ^ 1) for i in range(n_m)] if swap else to)

    block = n_obs // (n_x * n_y)
    tile = tile_x * n_y + tile_y
    mine = jnp.concatenate(
        [
            (obs_value[:, None] + obs_error[:, None] * perturbation).T,
            jnp.broadcast_to(obs_error[None], (8, block)),
        ]
    )
    mine = lax.dynamic_update_slice(jnp.zeros((16, n_obs), F32), mine, (0, tile * block))
    line = jnp.concatenate([picked, mine])
    a, b = send(rounded, 1), send(rounded, -1)
    own_far = send(rounded, 0, True)
    for axis, n in (("ty", n_y), ("tx", n_x)):
        bit = 1
        while bit < n:
            line = line + lax.ppermute(line, axis, [(i, i ^ bit) for i in range(n)])
            if bit == 1 and axis == "ty":
                line, own_far = lax.optimization_barrier((line, own_far))
            bit *= 2
    observed, target, error = line[0:8], line[8:16], line[16:17]
    innovation = (target - observed) / error
    scaled = observed / error

    scaled, a, b = lax.optimization_barrier((scaled, a, b))
    c = send(a, 1)
    parts = [send(scaled, by) for by in (1, -1, 2)]
    near = jnp.concatenate([scaled] + parts)
    far = send(near, 0, True)
    far, a, b = lax.optimization_barrier((far, a, b))
    a_far, b_far = send(a, 0, True), send(b, 0, True)
    weights = solve_weights(near, far, innovation)
    weights, c, a_far, b_far = lax.optimization_barrier((weights, c, a_far, b_far))
    c_far = send(c, 0, True)
    return update(weights, [rounded, a, b, c, own_far, a_far, b_far, c_far], forecast)


def solution(mesh):
    placed = (
        P("mem", "tx", "ty"),
        P("tx", "ty"),
        P("tx", "ty"),
        P("mem", "tx", "ty"),
        P(),
        P(("tx", "ty")),
        P(("tx", "ty")),
        P(("tx", "ty"), "mem"),
    )
    return jax.shard_map(
        local, mesh=mesh, in_specs=placed, out_specs=P("mem", "tx", "ty"), check_vma=False
    )
```

```python
import functools

import jax
import jax.numpy as jnp
from jax import lax
from jax.experimental import pallas as pl
from jax.experimental.pallas import tpu as pltpu
from jax.sharding import PartitionSpec as P

SUBSTEPS = 4
W = SUBSTEPS
GROUP = 128 // W
ROWS = 16
F32 = jnp.float32
BF16 = jnp.bfloat16
VMEM_SPEC = pl.BlockSpec(memory_space=pltpu.VMEM)
HBM_SPEC = pl.BlockSpec(memory_space=pltpu.HBM)


def lanes():
    return lax.broadcasted_iota(jnp.int32, (8, 128), 1)


def sublanes():
    return lax.broadcasted_iota(jnp.int32, (8, 128), 0)


def wide(row):
    return jnp.broadcast_to(row, (8, 128))


def ends_kernel(
    obs_ref, p_ref, w_ref, e_ref, k_ref, top_ref, bottom_ref, code_ref, inside_ref,
    cubes, sems,
):
    _, size_x, size_y = p_ref.shape
    copies = []
    for i, lo in enumerate((0, size_x - 8)):
        for j, ref in enumerate((p_ref, w_ref)):
            copies.append((ref.at[:, pl.ds(lo, 8), :], cubes.at[2 * i + j]))
    copies = [pltpu.make_async_copy(a, b, sems.at[n]) for n, (a, b) in enumerate(copies)]
    for c in copies:
        c.start()
    bits_x, bits_y = size_x.bit_length() - 1, size_y.bit_length() - 1
    total_y = size_y * lax.axis_size("ty")
    obs = obs_ref[...]
    x = lax.shift_right_logical(obs, total_y.bit_length() - 1)
    y = obs & (total_y - 1)
    mine = (lax.shift_right_logical(x, bits_x) == lax.axis_index("tx")) & (
        lax.shift_right_logical(y, bits_y) == lax.axis_index("ty")
    )
    x, y = x & (size_x - 1), y & (size_y - 1)
    tile = x * (size_y // 128) + lax.shift_right_logical(y, 7)
    code_ref[...] = tile * 128 + ((lanes() - y) & 127)
    inside_ref[...] = jnp.where(mine, F32(1), F32(0))
    for c in copies:
        c.wait()
    sub = lax.broadcasted_iota(jnp.int32, (8, size_y), 0)
    for i, out in enumerate((top_ref, bottom_ref)):
        for j in range(2):
            turned = jnp.swapaxes(cubes[2 * i + j], 0, 1)
            for r in range(W):
                out[j * W + r] = turned[r if i == 0 else 8 - W + r]
        lo = (0, size_x - 8)[i]
        e, k = e_ref[lo : lo + 8, :], k_ref[lo : lo + 8, :]
        if i == 0:
            k = pltpu.roll(k, 4, 0)
        else:
            e = pltpu.roll(e, 4, 0)
        out[2 * W] = jnp.where(sub < 4, e, k)


def ends(obs, p, w, e, k):
    members, _, size_y = p.shape
    edge = jax.ShapeDtypeStruct((2 * W + 1, members, size_y), F32)
    return pl.pallas_call(
        ends_kernel,
        in_specs=[VMEM_SPEC] + [HBM_SPEC] * 2 + [VMEM_SPEC] * 2,
        out_specs=[VMEM_SPEC] * 4,
        out_shape=[
            edge, edge, jax.ShapeDtypeStruct(obs.shape, jnp.int32),
            jax.ShapeDtypeStruct(obs.shape, F32),
        ],
        scratch_shapes=[
            pltpu.VMEM((4, members, 8, size_y), F32),
            pltpu.SemaphoreType.DMA((4,)),
        ],
        compiler_params=pltpu.CompilerParams(vmem_limit_bytes=56 * 2**20),
        name="ends",
    )(obs, p, w, e, k)


def pack_rows(rows):
    slot = lanes() // W
    left = jnp.zeros((8, 128), F32)
    right = jnp.zeros((8, 128), F32)
    for r, a, b in rows:
        if r:
            a = pltpu.roll(a, W * r, 1)
            b = pltpu.roll(b, W * r, 1)
        left = jnp.where(slot == r, a, left)
        right = jnp.where(slot == (r - 1) % GROUP, b, right)
    return left, right


def turn_kernel(
    p_in, w_in, e_ref, k_ref, pt_out, wt_out, left_ref, right_ref,
    p_ref, w_ref, pt_ref, wt_ref, in_sems, out_sems,
):
    groups = left_ref.shape[0]

    def rows_of(g):
        return pl.ds(pl.multiple_of(g * GROUP, GROUP), GROUP)

    def fetch(g, f):
        src, dst = ((p_in, p_ref), (w_in, w_ref))[f]
        at = rows_of(g)
        return pltpu.make_async_copy(src.at[:, at, :], dst.at[:, at, :], in_sems.at[f, g])

    def leave(g, f):
        src, dst = ((pt_ref, pt_out), (wt_ref, wt_out))[f]
        at = rows_of(g)
        return pltpu.make_async_copy(src.at[at], dst.at[at], out_sems.at[f, g])

    for g in range(groups):
        for f in range(2):
            fetch(g, f).start()

    def group(g, _):
        at = rows_of(g)
        for f, (src, dst) in enumerate(((p_ref, pt_ref), (w_ref, wt_ref))):
            fetch(g, f).wait()
            rows = jnp.swapaxes(src[:, at, :] * F32(0.5), 0, 1)
            dst[at] = rows
            left_ref[g, f], right_ref[g, f] = pack_rows(
                (r, rows[r, :, 0:128], rows[r, :, 128:256]) for r in range(GROUP)
            )
            leave(g, f).start()
        fields = []
        for base, ref, factor in ((0, e_ref, 0.5), (4, k_ref, 0.25)):
            block = ref[at, :] * F32(factor)
            for q in range(GROUP // 8):
                part = block[8 * q : 8 * q + 8]
                fields.append((base + q, part[:, 0:128], part[:, 128:256]))
        left_ref[g, 2], right_ref[g, 2] = pack_rows(fields)
        return 0

    lax.fori_loop(0, groups, group, 0)
    for g in range(groups):
        for f in range(2):
            leave(g, f).wait()


def turn(p, w, e, k):
    members, size_x, size_y = p.shape
    groups = size_x // GROUP
    turned = (size_x, members, size_y)
    return pl.pallas_call(
        turn_kernel,
        in_specs=[HBM_SPEC] * 2 + [VMEM_SPEC] * 2,
        out_specs=[HBM_SPEC] * 2 + [VMEM_SPEC] * 2,
        out_shape=[jax.ShapeDtypeStruct(turned, F32)] * 2
        + [jax.ShapeDtypeStruct((groups, 3, 8, 128), F32)] * 2,
        scratch_shapes=[pltpu.VMEM(p.shape, F32)] * 2 + [pltpu.VMEM(turned, F32)] * 2
        + [pltpu.SemaphoreType.DMA((2, groups))] * 2,
        cost_estimate=pl.CostEstimate(flops=10**7, bytes_accessed=9 * 2**20, transcendentals=0),
        compiler_params=pltpu.CompilerParams(vmem_limit_bytes=52 * 2**20),
        name="turn",
    )(p, w, e, k)


def rows_kernel(
    up_ref, down_ref, top_ref, bottom_ref, left_in, right_in, above_ref, below_ref,
    left_ref, right_ref,
):
    tile, groups = lax.axis_index("tx"), left_in.shape[0]
    first, last = tile == 0, tile == lax.axis_size("tx") - 1
    left_ref[0:groups] = left_in[...]
    right_ref[0:groups] = right_in[...]
    sub = lax.broadcasted_iota(jnp.int32, (8, 256), 0)

    def mirrored(block):
        out = block
        for i in range(4):
            for base in (0, 4):
                row = block[base + 3 - i : base + 4 - i, :]
                out = jnp.where(sub == base + i, jnp.broadcast_to(row, (8, 256)), out)
        return out

    for flag, got, own, out in (
        (first, up_ref, top_ref, above_ref),
        (last, down_ref, bottom_ref, below_ref),
    ):
        for f in range(2):
            for i in range(W):
                row = jnp.where(flag, own[f * W + W - 1 - i], got[f * W + i])
                out[f * W + i] = row * F32(0.5)
        block = jnp.where(flag, mirrored(own[2 * W]), got[2 * W])
        out[2 * W] = block * jnp.where(sub < 4, F32(0.5), F32(0.25))
    for f in range(2):
        left_ref[groups, f], right_ref[groups, f] = pack_rows(
            (half * W + i, out[f * W + i, :, 0:128], out[f * W + i, :, 128:256])
            for half, out in enumerate((above_ref, below_ref))
            for i in range(W)
        )
    above, below = above_ref[2 * W], below_ref[2 * W]
    e = jnp.where(sub < 4, above, pltpu.roll(below, 4, 0))
    k = jnp.where(sub < 4, pltpu.roll(above, 4, 0), below)
    left_ref[groups, 2], right_ref[groups, 2] = pack_rows(
        (slot, v[:, 0:128], v[:, 128:256]) for slot, v in ((0, e), (4, k))
    )


def halo_rows(up, down, top, bottom, left, right):
    packs = jax.ShapeDtypeStruct((left.shape[0] + 1, *left.shape[1:]), F32)
    return pl.pallas_call(
        rows_kernel,
        in_specs=[VMEM_SPEC] * 6,
        out_specs=[VMEM_SPEC] * 4,
        out_shape=[jax.ShapeDtypeStruct(up.shape, F32)] * 2 + [packs] * 2,
        compiler_params=pltpu.CompilerParams(vmem_limit_bytes=4 * 2**20),
        name="rows",
    )(up, down, top, bottom, left, right)


def steps_kernel(
    half, pt_in, wt_in, e_ref, k_ref, outer_ref, fl_ref, fr_ref, *refs,
):
    (
        out_ref, round_ref, p0, p1, w_s, fy_s, sum_s, e_s, er_s, k_s, kr_s, sems,
    ) = refs[half:]
    size_x = pt_in.shape[0] // 2
    lane = lanes()
    is_first, is_last = lane == 0, lane == 127
    groups = 2 * size_x // GROUP
    blocks = size_x // 8 + 2
    first, start = half * (size_x - W), 9 - half * W
    inner = (pl.ds(start, size_x + W), slice(None), pl.ds(0, 256))
    loads = [
        pltpu.make_async_copy(src.at[pl.ds(first, size_x + W)], dst.at[inner], sems.at[i])
        for i, (src, dst) in enumerate(((pt_in, p0), (wt_in, w_s)))
    ]
    for c in loads:
        c.start()

    def halo(g, f, r):
        a, b = fr_ref[g, f], fl_ref[g, f]
        if r:
            a = pltpu.roll(a, 128 - W * r, 1)
            b = pltpu.roll(b, 128 - W * r, 1)
        return jnp.where(lane < 64, a, b)

    def spread(at, v, here, shifted):
        rolled = [pltpu.roll(u, 127, 1) for u in v]
        for t in range(3):
            here[at, :, 128 * t : 128 * t + 128] = v[t]
            shifted[at, :, 128 * t : 128 * t + 128] = jnp.where(
                is_last, rolled[(t + 1) % 3], rolled[t]
            )

    def columns(y, g, r):
        for f, dst in ((0, p0), (1, w_s)):
            dst[y + 1, :, 256:384] = halo(g, f, r)

    def fields(at, g, q, rows):
        for base, ref, factor, here, shifted in (
            (0, e_ref, 0.5, e_s, er_s), (4, k_ref, 0.25, k_s, kr_s),
        ):
            v = [ref[rows, 128 * t : 128 * t + 128] * F32(factor) for t in range(2)]
            spread(at, v + [halo(g, 2, base + q)], here, shifted)

    per = GROUP // 8

    def unpack_group(i, _):
        g = half * (groups // 2) + i
        for r in range(GROUP):
            columns(i * GROUP + r + 8, g, r)
        for q in range(per):
            rows = pl.ds(pl.multiple_of(g * GROUP + 8 * q, 8), 8)
            fields(i * per + q + 1, g, q, rows)
        return 0

    lax.fori_loop(0, groups // 2, unpack_group, 0)
    for r in range(W):
        if half:
            columns(4 + r, groups // 2 - 1, GROUP - W + r)
        else:
            columns(size_x + 8 + r, groups // 2, r)
    if half:
        fields(0, groups // 2 - 1, per - 1, slice(size_x - 8, size_x))
    else:
        fields(blocks - 1, groups // 2, 0, slice(size_x, size_x + 8))
    for r in range(W):
        y = size_x + 8 + r if half else 4 + r
        for f, dst in ((0, p0), (1, w_s)):
            dst[y + 1, :, 0:256] = outer_ref[f * W + r]
        columns(y, groups, half * W + r)
    for base, here, shifted in ((0, e_s, er_s), (4, k_s, kr_s)):
        edge = pltpu.roll(halo(groups, 2, base), 4, 0)
        v = outer_ref[2 * W]
        v = pltpu.roll(v, 4, 0) if (base == 0) != bool(half) else v
        spread((blocks - 1) * half, [v[:, 0:128], v[:, 128:256], edge], here, shifted)

    one, none = F32(1), F32(0)

    tile = lax.axis_index("ty")

    def edge_mask(at):
        return jnp.where(is_last & (jnp.broadcast_to(tile, (8, 128)) == at), none, one)

    mask_right, mask_left = edge_mask(lax.axis_size("ty") - 1), edge_mask(0)
    for c in loads:
        c.wait()

    def tiles(ref, at):
        return [ref[at, :, 128 * t : 128 * t + 128] for t in range(3)]

    def put(ref, at, v):
        for t in range(3):
            ref[at, :, 128 * t : 128 * t + 128] = v[t]

    def row_of(ref, b, u):
        return [wide(ref[b, u : u + 1, 128 * t : 128 * t + 128]) for t in range(3)]

    def step(src, dst):
        count = 8 * blocks // ROWS

        def body(i, carry):
            b_at = jnp.minimum(i, count - 1)
            c_at = jnp.maximum(i - 1, 0) * ROWS
            for u in range(ROWS):
                at = c_at + u
                s, fy = tiles(sum_s, at), tiles(fy_s, at)
                fr = [pltpu.roll(v, 1, 1) for v in fy]
                back = [jnp.where(is_first, fr[(t - 1) % 3], fr[t]) for t in range(3)]
                put(dst, at, [s[t] + (fy[t] - back[t]) for t in range(3)])
            p_old, h_old, c_old, fx_old = carry
            for u in range(ROWS):
                at = b_at * ROWS + u
                block = (b_at * (ROWS // 8) + u // 8, u % 8)
                p = tiles(src, at + 1)
                raw = [pltpu.roll(v, 127, 1) for v in p]
                pr = [jnp.where(is_last, raw[(t + 1) % 3], raw[t]) for t in range(3)]
                e, er = row_of(e_s, *block), row_of(er_s, *block)
                k, kr = row_of(k_s, *block), row_of(kr_s, *block)
                w = tiles(w_s, at)
                h = [p[t] + e[t] for t in range(3)]
                c = [k[t] * jnp.tanh(p[t]) + k[t] for t in range(3)]
                fy = [
                    (c[t] + (kr[t] * jnp.tanh(pr[t]) + kr[t])) * ((pr[t] + er[t]) - h[t])
                    for t in range(3)
                ]
                fy[1] = fy[1] * mask_right
                fy[2] = fy[2] * mask_left
                fx = [(c_old[t] + c[t]) * (h[t] - h_old[t]) for t in range(3)]
                put(sum_s, at, [(p_old[t] + w[t]) + (fx[t] - fx_old[t]) for t in range(3)])
                put(fy_s, at + 1, fy)
                p_old, h_old, c_old, fx_old = p, h, c, fx
            return p_old, h_old, c_old, fx_old

        zero = [jnp.zeros((8, 128), F32)] * 3
        lax.fori_loop(0, count + 1, body, (zero, zero, zero, zero))

    for s in range(SUBSTEPS):
        step(*((p0, p1) if s % 2 == 0 else (p1, p0)))
    last = p0 if SUBSTEPS % 2 == 0 else p1

    def leave(i, _):
        x = pl.multiple_of(i * 8, 8)
        for u in range(8):
            row = last[x + 9 + u, :, 0:256] * F32(2)
            to = 2 * (half * size_x + x + u)
            out_ref[to] = row[:, 0:128]
            out_ref[to + 1] = row[:, 128:256]
            round_ref[x + u] = row.astype(BF16)
        return 0

    lax.fori_loop(0, size_x // 8, leave, 0)


def run_steps(half, pt, wt, e, k, outer, from_left, from_right, *before):
    size_x, members, size_y = pt.shape
    rows = size_x // 2
    tile = pltpu.VMEM((rows + 17, members, size_y + 128), F32)
    flat = pltpu.VMEM((rows // 8 + 2, 8, size_y + 128), F32)
    return pl.pallas_call(
        functools.partial(steps_kernel, half),
        in_specs=[HBM_SPEC] * 2 + [VMEM_SPEC] * (5 + half),
        out_specs=[VMEM_SPEC] * 2,
        scratch_shapes=[tile] * 5 + [flat] * 4 + [pltpu.SemaphoreType.DMA((2,))],
        out_shape=[
            jax.ShapeDtypeStruct((size_x * (size_y // 128), members, 128), F32),
            jax.ShapeDtypeStruct((rows, members, size_y), BF16),
        ],
        input_output_aliases={7: 0} if half else {},
        compiler_params=pltpu.CompilerParams(vmem_limit_bytes=50 * 2**20),
        name="steps",
    )(pt, wt, e, k, outer, from_left, from_right, *before)


def pick_kernel(code_ref, f_ref, inside_ref, pick_ref):
    lane = lanes()

    def pick(g, _):
        acc = jnp.zeros((8, 128), F32)
        for u in range(128):
            code = code_ref[g, u]
            v = pltpu.roll(f_ref[lax.shift_right_logical(code, 7)], code & 127, 1)
            acc = jnp.where(lane == u, v, acc)
        keep = wide(inside_ref[pl.ds(g, 1), :]) > F32(0.5)
        pick_ref[:, pl.ds(pl.multiple_of(g * 128, 128), 128)] = jnp.where(keep, acc, F32(0))
        return 0

    lax.fori_loop(0, code_ref.shape[0], pick, 0)


def picks(code, forecast, inside):
    return pl.pallas_call(
        pick_kernel,
        grid_spec=pltpu.PrefetchScalarGridSpec(
            num_scalar_prefetch=1, grid=(), in_specs=[VMEM_SPEC] * 2, out_specs=VMEM_SPEC
        ),
        out_shape=jax.ShapeDtypeStruct((8, code.size), F32),
        compiler_params=pltpu.CompilerParams(vmem_limit_bytes=8 * 2**20),
        name="picks",
    )(code, forecast, inside)


def weights_kernel(near_ref, far_ref, innovation_ref, out_ref, x_s, m_s):
    half = near_ref.shape[0]
    members = 2 * half
    blocks = members // 8
    parts = [r[8 * b : 8 * b + 8, :] for r in (near_ref, far_ref) for b in range(half // 8)]
    total = parts[0]
    for part in parts[1:]:
        total = total + part
    mean = jnp.sum(total, axis=0, keepdims=True) * F32(1.0 / members)
    for b, part in enumerate(parts):
        x_s[8 * b : 8 * b + 8, :] = part - mean
    x = x_s[...]
    dims = (((1,), (1,)), ((), ()))
    dot = functools.partial(
        lax.dot_general, dimension_numbers=dims, precision=lax.Precision.HIGHEST,
        preferred_element_type=F32,
    )
    r = lax.broadcasted_iota(jnp.int32, (members, members), 0)
    c = lax.broadcasted_iota(jnp.int32, (members, members), 1)
    m_s[:, 0:members] = dot(x, x) + jnp.where(r == c, F32(members - 1), F32(0))
    m_s[:, members : 2 * members] = jnp.zeros((members, members), F32)
    m_s[:, members : members + 8] = dot(x, innovation_ref[...])
    m = [m_s[8 * b : 8 * b + 8, :] for b in range(blocks)]
    sub = sublanes()
    for kb in range(blocks):
        cols = [
            [jnp.broadcast_to(m[b][:, 8 * kb + j : 8 * kb + j + 1], (8, 128)) for j in range(8)]
            for b in range(blocks)
        ]
        rows = m[kb]
        piv = list(cols[kb])
        for j in range(8):
            inv = F32(1) / wide(piv[j][j : j + 1])
            here = sub == j
            factor = piv[j]
            top = wide(rows[j : j + 1]) * inv
            rows = jnp.where(here, top, rows - factor * top)
            for q in range(j + 1, 8):
                top = wide(piv[q][j : j + 1]) * inv
                piv[q] = jnp.where(here, top, piv[q] - factor * top)
        spread = [wide(rows[j : j + 1]) for j in range(8)]
        for b in range(blocks):
            if b == kb:
                m[b] = rows
            else:
                acc = cols[b][0] * spread[0]
                for j in range(1, 8):
                    acc = acc + cols[b][j] * spread[j]
                m[b] = m[b] - acc
    for b in range(blocks):
        m_s[8 * b : 8 * b + 8, :] = m[b]
    turned = jnp.transpose(m_s[...], (1, 0))
    out_ref[...] = turned[members : members + 8, 0:members]


def solve_weights(near, far, innovation):
    half, n_obs = near.shape
    members = 2 * half
    return pl.pallas_call(
        weights_kernel,
        in_specs=[VMEM_SPEC] * 3,
        out_specs=VMEM_SPEC,
        scratch_shapes=[
            pltpu.VMEM((members, n_obs), F32),
            pltpu.VMEM((members, 2 * members), F32),
        ],
        out_shape=jax.ShapeDtypeStruct((8, members), F32),
        compiler_params=pltpu.CompilerParams(vmem_limit_bytes=4 * 2**20),
        name="weights",
    )(near, far, innovation)


def update_kernel(w_ref, *refs):
    pieces, (f_ref, out_ref, row_s, done_s, sems) = refs[:-5], refs[-5:]
    step = row_s.shape[0]
    count = pieces[0].shape[0] // step
    w = w_ref[...].astype(BF16)

    def leave(g):
        at = pl.ds(pl.multiple_of(g * step, step), step)
        return pltpu.make_async_copy(done_s.at[:, at, :], out_ref.at[:, at, :], sems.at[g])

    def chunk(half, i, _):
        g = half * count + i
        for r in range(step):
            parts = [v[i * step + r].astype(F32) for v in pieces[half::2]]
            rows = jnp.concatenate(parts, axis=0).astype(BF16)
            shift = jnp.dot(w, rows, preferred_element_type=F32)
            for t in range(2):
                cols = slice(128 * t, 128 * t + 128)
                row_s[r, :, cols] = f_ref[2 * (g * step + r) + t] + shift[:, cols]
        at = pl.ds(pl.multiple_of(g * step, step), step)
        done_s[:, at, :] = jnp.swapaxes(row_s[...], 0, 1)
        leave(g).start()
        return 0

    for half in range(2):
        lax.fori_loop(0, count, functools.partial(chunk, half), 0)
    for g in range(2 * count):
        leave(g).wait()


def update(weights, pieces, forecast):
    rows, members, size_y = pieces[0].shape
    step = 32
    whole = (members, 2 * rows, size_y)
    return pl.pallas_call(
        update_kernel,
        in_specs=[VMEM_SPEC] * (len(pieces) + 2),
        out_specs=HBM_SPEC,
        out_shape=jax.ShapeDtypeStruct(whole, F32),
        scratch_shapes=[
            pltpu.VMEM((step, members, size_y), F32),
            pltpu.VMEM(whole, F32),
            pltpu.SemaphoreType.DMA((2 * rows // step,)),
        ],
        compiler_params=pltpu.CompilerParams(vmem_limit_bytes=8 * 2**20),
        name="update",
    )(weights, *pieces, forecast)


def local(pressure, elevation, ks_field, melt_rate, obs_index, obs_value, obs_error, perturbation):
    n_x, n_y, n_m = (lax.axis_size(a) for a in ("tx", "ty", "mem"))
    tile_x, tile_y = lax.axis_index("tx"), lax.axis_index("ty")

    def ring(n, by):
        return [(i, (i + by) % n) for i in range(n)]

    n_obs = obs_index.shape[0]
    top, bottom, code, inside = ends(
        obs_index.reshape(n_obs // 128, 128), pressure, melt_rate, elevation, ks_field
    )
    up = lax.ppermute(bottom, "tx", ring(n_x, 1))
    down = lax.ppermute(top, "tx", ring(n_x, -1))
    pt, wt, left, right = turn(pressure, melt_rate, elevation, ks_field)
    above, below, left, right = halo_rows(up, down, top, bottom, left, right)
    from_left = lax.ppermute(right, "ty", ring(n_y, 1))
    from_right = lax.ppermute(left, "ty", ring(n_y, -1))

    def send(v, by, swap=False):
        to = [(i, (i + 2 * (by if i % 2 == 0 else -by)) % n_m) for i in range(n_m)]
        return lax.ppermute(v, "mem", [(i, i ^ 1) for i in range(n_m)] if swap else to)

    columns = (from_left, from_right)
    forecast, low = run_steps(0, pt, wt, elevation, ks_field, above, *columns)
    a0, b0 = send(low, 1), send(low, -1)
    forecast, high = run_steps(1, pt, wt, elevation, ks_field, below, *columns, forecast)
    a1, b1 = send(high, 1), send(high, -1)
    own0, own1 = send(low, 0, True), send(high, 0, True)
    picked = picks(code, forecast, inside)

    block = n_obs // (n_x * n_y)
    tile = tile_x * n_y + tile_y
    mine = jnp.concatenate(
        [
            (obs_value[:, None] + obs_error[:, None] * perturbation).T,
            jnp.broadcast_to(obs_error[None], (8, block)),
        ]
    )
    mine = lax.dynamic_update_slice(jnp.zeros((16, n_obs), F32), mine, (0, tile * block))
    line = jnp.concatenate([picked, mine])
    steps = [("ty", 1), ("ty", 2), ("tx", 1), ("tx", 2)]
    for n, (axis, bit) in enumerate(steps):
        line = line + lax.ppermute(line, axis, [(i, i ^ bit) for i in range(lax.axis_size(axis))])
        if n == 0:
            line, a0, b0, own0, own1 = lax.optimization_barrier((line, a0, b0, own0, own1))
            c0 = send(a0, 1)
        if n == 1:
            line, a0, b0 = lax.optimization_barrier((line, a0, b0))
            a0_far, b0_far = send(a0, 0, True), send(b0, 0, True)
    observed, target, error = line[0:8], line[8:16], line[16:17]
    innovation = (target - observed) / error
    scaled = observed / error

    scaled, a1, b1, c0 = lax.optimization_barrier((scaled, a1, b1, c0))
    c1 = send(a1, 1)
    parts = [send(scaled, by) for by in (1, -1, 2)]
    near = jnp.concatenate([scaled] + parts)
    c0_far = send(c0, 0, True)
    far = send(near, 0, True)
    far, a1, b1 = lax.optimization_barrier((far, a1, b1))
    a1_far, b1_far = send(a1, 0, True), send(b1, 0, True)
    weights = solve_weights(near, far, innovation)
    weights, c1, a1_far, b1_far = lax.optimization_barrier((weights, c1, a1_far, b1_far))
    c1_far = send(c1, 0, True)
    pieces = [
        low, high, a0, a1, b0, b1, c0, c1,
        own0, own1, a0_far, a1_far, b0_far, b1_far, c0_far, c1_far,
    ]
    return update(weights, pieces, forecast)


def solution(mesh):
    placed = (
        P("mem", "tx", "ty"),
        P("tx", "ty"),
        P("tx", "ty"),
        P("mem", "tx", "ty"),
        P(),
        P(("tx", "ty")),
        P(("tx", "ty")),
        P(("tx", "ty"), "mem"),
    )
    return jax.shard_map(
        local, mesh=mesh, in_specs=placed, out_specs=P("mem", "tx", "ty"), check_vma=False
    )
```

```python
import functools

import jax
import jax.numpy as jnp
from jax import lax
from jax.experimental import pallas as pl
from jax.experimental.pallas import tpu as pltpu
from jax.sharding import PartitionSpec as P

SUBSTEPS = 4
W = SUBSTEPS
GROUP = 128 // W
ROWS = 16
F32 = jnp.float32
BF16 = jnp.bfloat16
VMEM_SPEC = pl.BlockSpec(memory_space=pltpu.VMEM)
HBM_SPEC = pl.BlockSpec(memory_space=pltpu.HBM)


def lanes():
    return lax.broadcasted_iota(jnp.int32, (8, 128), 1)


def sublanes():
    return lax.broadcasted_iota(jnp.int32, (8, 128), 0)


def wide(row):
    return jnp.broadcast_to(row, (8, 128))


def ends_kernel(
    obs_ref, p_ref, w_ref, e_ref, k_ref, top_ref, bottom_ref, code_ref, inside_ref,
    cubes, sems,
):
    _, size_x, size_y = p_ref.shape
    copies = []
    for i, lo in enumerate((0, size_x - 8)):
        for j, ref in enumerate((p_ref, w_ref)):
            copies.append((ref.at[:, pl.ds(lo, 8), :], cubes.at[2 * i + j]))
    copies = [pltpu.make_async_copy(a, b, sems.at[n]) for n, (a, b) in enumerate(copies)]
    for c in copies:
        c.start()
    bits_x, bits_y = size_x.bit_length() - 1, size_y.bit_length() - 1
    total_y = size_y * lax.axis_size("ty")
    obs = obs_ref[...]
    x = lax.shift_right_logical(obs, total_y.bit_length() - 1)
    y = obs & (total_y - 1)
    mine = (lax.shift_right_logical(x, bits_x) == lax.axis_index("tx")) & (
        lax.shift_right_logical(y, bits_y) == lax.axis_index("ty")
    )
    x, y = x & (size_x - 1), y & (size_y - 1)
    tile = x * (size_y // 128) + lax.shift_right_logical(y, 7)
    code_ref[...] = tile * 128 + ((lanes() - y) & 127)
    inside_ref[...] = jnp.where(mine, F32(1), F32(0))
    for c in copies:
        c.wait()
    sub = lax.broadcasted_iota(jnp.int32, (8, size_y), 0)
    for i, out in enumerate((top_ref, bottom_ref)):
        for j in range(2):
            turned = jnp.swapaxes(cubes[2 * i + j], 0, 1)
            for r in range(W):
                out[j * W + r] = turned[r if i == 0 else 8 - W + r]
        lo = (0, size_x - 8)[i]
        e, k = e_ref[lo : lo + 8, :], k_ref[lo : lo + 8, :]
        if i == 0:
            k = pltpu.roll(k, 4, 0)
        else:
            e = pltpu.roll(e, 4, 0)
        out[2 * W] = jnp.where(sub < 4, e, k)


def ends(obs, p, w, e, k):
    members, _, size_y = p.shape
    edge = jax.ShapeDtypeStruct((2 * W + 1, members, size_y), F32)
    return pl.pallas_call(
        ends_kernel,
        in_specs=[VMEM_SPEC] + [HBM_SPEC] * 2 + [VMEM_SPEC] * 2,
        out_specs=[VMEM_SPEC] * 4,
        out_shape=[
            edge, edge, jax.ShapeDtypeStruct(obs.shape, jnp.int32),
            jax.ShapeDtypeStruct(obs.shape, F32),
        ],
        scratch_shapes=[
            pltpu.VMEM((4, members, 8, size_y), F32),
            pltpu.SemaphoreType.DMA((4,)),
        ],
        compiler_params=pltpu.CompilerParams(vmem_limit_bytes=56 * 2**20),
        name="ends",
    )(obs, p, w, e, k)


def pack_rows(rows):
    slot = lanes() // W
    left = jnp.zeros((8, 128), F32)
    right = jnp.zeros((8, 128), F32)
    for r, a, b in rows:
        if r:
            a = pltpu.roll(a, W * r, 1)
            b = pltpu.roll(b, W * r, 1)
        left = jnp.where(slot == r, a, left)
        right = jnp.where(slot == (r - 1) % GROUP, b, right)
    return left, right


def turn_kernel(
    p_in, w_in, e_ref, k_ref, pt_out, wt_out, left_ref, right_ref,
    p_ref, w_ref, pt_ref, wt_ref, in_sems, out_sems,
):
    groups = left_ref.shape[0]

    def rows_of(g):
        return pl.ds(pl.multiple_of(g * GROUP, GROUP), GROUP)

    def fetch(g, f):
        src, dst = ((p_in, p_ref), (w_in, w_ref))[f]
        at = rows_of(g)
        return pltpu.make_async_copy(src.at[:, at, :], dst.at[:, at, :], in_sems.at[f, g])

    def leave(g, f):
        src, dst = ((pt_ref, pt_out), (wt_ref, wt_out))[f]
        at = rows_of(g)
        return pltpu.make_async_copy(src.at[at], dst.at[at], out_sems.at[f, g])

    for g in range(groups):
        for f in range(2):
            fetch(g, f).start()

    def group(g, _):
        at = rows_of(g)
        for f, (src, dst) in enumerate(((p_ref, pt_ref), (w_ref, wt_ref))):
            fetch(g, f).wait()
            rows = jnp.swapaxes(src[:, at, :] * F32(0.5), 0, 1)
            dst[at] = rows
            left_ref[g, f], right_ref[g, f] = pack_rows(
                (r, rows[r, :, 0:128], rows[r, :, 128:256]) for r in range(GROUP)
            )
            leave(g, f).start()
        fields = []
        for base, ref, factor in ((0, e_ref, 0.5), (4, k_ref, 0.25)):
            block = ref[at, :] * F32(factor)
            for q in range(GROUP // 8):
                part = block[8 * q : 8 * q + 8]
                fields.append((base + q, part[:, 0:128], part[:, 128:256]))
        left_ref[g, 2], right_ref[g, 2] = pack_rows(fields)
        return 0

    lax.fori_loop(0, groups, group, 0)
    for g in range(groups):
        for f in range(2):
            leave(g, f).wait()


def turn(p, w, e, k):
    members, size_x, size_y = p.shape
    groups = size_x // GROUP
    turned = (size_x, members, size_y)
    return pl.pallas_call(
        turn_kernel,
        in_specs=[HBM_SPEC] * 2 + [VMEM_SPEC] * 2,
        out_specs=[HBM_SPEC] * 2 + [VMEM_SPEC] * 2,
        out_shape=[jax.ShapeDtypeStruct(turned, F32)] * 2
        + [jax.ShapeDtypeStruct((groups, 3, 8, 128), F32)] * 2,
        scratch_shapes=[pltpu.VMEM(p.shape, F32)] * 2 + [pltpu.VMEM(turned, F32)] * 2
        + [pltpu.SemaphoreType.DMA((2, groups))] * 2,
        cost_estimate=pl.CostEstimate(flops=10**7, bytes_accessed=9 * 2**20, transcendentals=0),
        compiler_params=pltpu.CompilerParams(vmem_limit_bytes=52 * 2**20),
        name="turn",
    )(p, w, e, k)


def rows_kernel(
    up_ref, down_ref, top_ref, bottom_ref, left_in, right_in, above_ref, below_ref,
    left_ref, right_ref,
):
    tile, groups = lax.axis_index("tx"), left_in.shape[0]
    first, last = tile == 0, tile == lax.axis_size("tx") - 1
    left_ref[0:groups] = left_in[...]
    right_ref[0:groups] = right_in[...]
    sub = lax.broadcasted_iota(jnp.int32, (8, 256), 0)

    def mirrored(block):
        out = block
        for i in range(4):
            for base in (0, 4):
                row = block[base + 3 - i : base + 4 - i, :]
                out = jnp.where(sub == base + i, jnp.broadcast_to(row, (8, 256)), out)
        return out

    for flag, got, own, out in (
        (first, up_ref, top_ref, above_ref),
        (last, down_ref, bottom_ref, below_ref),
    ):
        for f in range(2):
            for i in range(W):
                row = jnp.where(flag, own[f * W + W - 1 - i], got[f * W + i])
                out[f * W + i] = row * F32(0.5)
        block = jnp.where(flag, mirrored(own[2 * W]), got[2 * W])
        out[2 * W] = block * jnp.where(sub < 4, F32(0.5), F32(0.25))
    for f in range(2):
        left_ref[groups, f], right_ref[groups, f] = pack_rows(
            (half * W + i, out[f * W + i, :, 0:128], out[f * W + i, :, 128:256])
            for half, out in enumerate((above_ref, below_ref))
            for i in range(W)
        )
    above, below = above_ref[2 * W], below_ref[2 * W]
    e = jnp.where(sub < 4, above, pltpu.roll(below, 4, 0))
    k = jnp.where(sub < 4, pltpu.roll(above, 4, 0), below)
    left_ref[groups, 2], right_ref[groups, 2] = pack_rows(
        (slot, v[:, 0:128], v[:, 128:256]) for slot, v in ((0, e), (4, k))
    )


def halo_rows(up, down, top, bottom, left, right):
    packs = jax.ShapeDtypeStruct((left.shape[0] + 1, *left.shape[1:]), F32)
    return pl.pallas_call(
        rows_kernel,
        in_specs=[VMEM_SPEC] * 6,
        out_specs=[VMEM_SPEC] * 4,
        out_shape=[jax.ShapeDtypeStruct(up.shape, F32)] * 2 + [packs] * 2,
        compiler_params=pltpu.CompilerParams(vmem_limit_bytes=4 * 2**20),
        name="rows",
    )(up, down, top, bottom, left, right)


def steps_kernel(
    pt_in, wt_in, e_ref, k_ref, above_ref, below_ref, fl_ref, fr_ref,
    out_ref, round_ref,
    p0, p1, w_s, fy_s, sum_s, e_s, er_s, k_s, kr_s, sems,
):
    size_x = pt_in.shape[0]
    lane = lanes()
    is_first, is_last = lane == 0, lane == 127
    groups = size_x // GROUP
    blocks = size_x // 8 + 2
    inner = (pl.ds(9, size_x), slice(None), pl.ds(0, 256))
    loads = [
        pltpu.make_async_copy(src, dst.at[inner], sems.at[i])
        for i, (src, dst) in enumerate(((pt_in, p0), (wt_in, w_s)))
    ]
    for c in loads:
        c.start()

    def halo(g, f, r):
        a, b = fr_ref[g, f], fl_ref[g, f]
        if r:
            a = pltpu.roll(a, 128 - W * r, 1)
            b = pltpu.roll(b, 128 - W * r, 1)
        return jnp.where(lane < 64, a, b)

    def spread(at, v, here, shifted):
        rolled = [pltpu.roll(u, 127, 1) for u in v]
        for t in range(3):
            here[at, :, 128 * t : 128 * t + 128] = v[t]
            shifted[at, :, 128 * t : 128 * t + 128] = jnp.where(
                is_last, rolled[(t + 1) % 3], rolled[t]
            )

    def unpack_group(g, _):
        for r in range(GROUP):
            for f, dst in ((0, p0), (1, w_s)):
                dst[g * GROUP + r + 9, :, 256:384] = halo(g, f, r)
        for q in range(GROUP // 8):
            rows = pl.ds(pl.multiple_of(g * GROUP + 8 * q, 8), 8)
            for base, ref, factor, here, shifted in (
                (0, e_ref, 0.5, e_s, er_s), (4, k_ref, 0.25, k_s, kr_s),
            ):
                v = [ref[rows, 128 * t : 128 * t + 128] * F32(factor) for t in range(2)]
                spread(g * (GROUP // 8) + q + 1, v + [halo(g, 2, base + q)], here, shifted)
        return 0

    lax.fori_loop(0, groups, unpack_group, 0)
    for r in range(2 * W):
        ref, y = (above_ref, 4 + r) if r < W else (below_ref, size_x + 4 + r)
        for f, dst in ((0, p0), (1, w_s)):
            dst[y + 1, :, 0:256] = ref[f * W + r % W]
            dst[y + 1, :, 256:384] = halo(groups, f, r)
    for base, here, shifted in ((0, e_s, er_s), (4, k_s, kr_s)):
        edge = pltpu.roll(halo(groups, 2, base), 4, 0)
        for at, ref, up in ((0, above_ref, base == 0), (blocks - 1, below_ref, base == 4)):
            v = ref[2 * W]
            v = pltpu.roll(v, 4, 0) if up else v
            spread(at, [v[:, 0:128], v[:, 128:256], edge], here, shifted)

    one, none = F32(1), F32(0)

    tile = lax.axis_index("ty")

    def edge_mask(at):
        return jnp.where(is_last & (jnp.broadcast_to(tile, (8, 128)) == at), none, one)

    mask_right, mask_left = edge_mask(lax.axis_size("ty") - 1), edge_mask(0)
    for c in loads:
        c.wait()

    def tiles(ref, at):
        return [ref[at, :, 128 * t : 128 * t + 128] for t in range(3)]

    def put(ref, at, v):
        for t in range(3):
            ref[at, :, 128 * t : 128 * t + 128] = v[t]

    def row_of(ref, b, u):
        return [wide(ref[b, u : u + 1, 128 * t : 128 * t + 128]) for t in range(3)]

    def step(src, dst):
        count = 8 * blocks // ROWS

        def body(i, carry):
            b_at = jnp.minimum(i, count - 1)
            c_at = jnp.maximum(i - 1, 0) * ROWS
            for u in range(ROWS):
                at = c_at + u
                s, fy = tiles(sum_s, at), tiles(fy_s, at)
                fr = [pltpu.roll(v, 1, 1) for v in fy]
                back = [jnp.where(is_first, fr[(t - 1) % 3], fr[t]) for t in range(3)]
                put(dst, at, [s[t] + (fy[t] - back[t]) for t in range(3)])
            p_old, h_old, c_old, fx_old = carry
            for u in range(ROWS):
                at = b_at * ROWS + u
                block = (b_at * (ROWS // 8) + u // 8, u % 8)
                p = tiles(src, at + 1)
                raw = [pltpu.roll(v, 127, 1) for v in p]
                pr = [jnp.where(is_last, raw[(t + 1) % 3], raw[t]) for t in range(3)]
                e, er = row_of(e_s, *block), row_of(er_s, *block)
                k, kr = row_of(k_s, *block), row_of(kr_s, *block)
                w = tiles(w_s, at)
                h = [p[t] + e[t] for t in range(3)]
                c = [k[t] * jnp.tanh(p[t]) + k[t] for t in range(3)]
                fy = [
                    (c[t] + (kr[t] * jnp.tanh(pr[t]) + kr[t])) * ((pr[t] + er[t]) - h[t])
                    for t in range(3)
                ]
                fy[1] = fy[1] * mask_right
                fy[2] = fy[2] * mask_left
                fx = [(c_old[t] + c[t]) * (h[t] - h_old[t]) for t in range(3)]
                put(sum_s, at, [(p_old[t] + w[t]) + (fx[t] - fx_old[t]) for t in range(3)])
                put(fy_s, at + 1, fy)
                p_old, h_old, c_old, fx_old = p, h, c, fx
            return p_old, h_old, c_old, fx_old

        zero = [jnp.zeros((8, 128), F32)] * 3
        lax.fori_loop(0, count + 1, body, (zero, zero, zero, zero))

    for s in range(SUBSTEPS):
        step(*((p0, p1) if s % 2 == 0 else (p1, p0)))
    last = p0 if SUBSTEPS % 2 == 0 else p1

    def leave(i, _):
        x = pl.multiple_of(i * 8, 8)
        for u in range(8):
            row = last[x + 9 + u, :, 0:256] * F32(2)
            out_ref[2 * x + 2 * u] = row[:, 0:128]
            out_ref[2 * x + 2 * u + 1] = row[:, 128:256]
            round_ref[x + u] = row.astype(BF16)
        return 0

    lax.fori_loop(0, size_x // 8, leave, 0)


def run_steps(pt, wt, e, k, above, below, from_left, from_right):
    size_x, members, size_y = pt.shape
    tile = pltpu.VMEM((size_x + 17, members, size_y + 128), F32)
    flat = pltpu.VMEM((size_x // 8 + 2, 8, size_y + 128), F32)
    return pl.pallas_call(
        steps_kernel,
        in_specs=[HBM_SPEC] * 2 + [VMEM_SPEC] * 6,
        out_specs=[VMEM_SPEC] * 2,
        scratch_shapes=[tile] * 5 + [flat] * 4 + [pltpu.SemaphoreType.DMA((2,))],
        out_shape=[
            jax.ShapeDtypeStruct((size_x * (size_y // 128), members, 128), F32),
            jax.ShapeDtypeStruct((size_x, members, size_y), BF16),
        ],
        compiler_params=pltpu.CompilerParams(vmem_limit_bytes=50 * 2**20),
        name="steps",
    )(pt, wt, e, k, above, below, from_left, from_right)


def pick_kernel(code_ref, f_ref, inside_ref, pick_ref):
    lane = lanes()

    def pick(g, _):
        acc = jnp.zeros((8, 128), F32)
        for u in range(128):
            code = code_ref[g, u]
            v = pltpu.roll(f_ref[lax.shift_right_logical(code, 7)], code & 127, 1)
            acc = jnp.where(lane == u, v, acc)
        keep = wide(inside_ref[pl.ds(g, 1), :]) > F32(0.5)
        pick_ref[:, pl.ds(pl.multiple_of(g * 128, 128), 128)] = jnp.where(keep, acc, F32(0))
        return 0

    lax.fori_loop(0, code_ref.shape[0], pick, 0)


def picks(code, forecast, inside):
    return pl.pallas_call(
        pick_kernel,
        grid_spec=pltpu.PrefetchScalarGridSpec(
            num_scalar_prefetch=1, grid=(), in_specs=[VMEM_SPEC] * 2, out_specs=VMEM_SPEC
        ),
        out_shape=jax.ShapeDtypeStruct((8, code.size), F32),
        compiler_params=pltpu.CompilerParams(vmem_limit_bytes=8 * 2**20),
        name="picks",
    )(code, forecast, inside)


def weights_kernel(near_ref, far_ref, target_ref, error_ref, first_ref, last_ref, x_s, m_s):
    half = near_ref.shape[0]
    members = 2 * half
    blocks = members // 8
    parts = [r[8 * b : 8 * b + 8, :] for r in (near_ref, far_ref) for b in range(half // 8)]
    total = parts[0]
    for part in parts[1:]:
        total = total + part
    mean = jnp.sum(total, axis=0, keepdims=True) * F32(1.0 / members)
    error = jnp.concatenate([error_ref[r : r + 1, :] for r in range(error_ref.shape[0])], axis=1)
    inverse = F32(1) / error
    for b, part in enumerate(parts):
        x_s[8 * b : 8 * b + 8, :] = (part - mean) * inverse
    innovation = (target_ref[...] - parts[0]) * inverse
    x = x_s[...]
    dims = (((1,), (1,)), ((), ()))
    dot = functools.partial(
        lax.dot_general, dimension_numbers=dims, precision=lax.Precision.HIGHEST,
        preferred_element_type=F32,
    )
    r = lax.broadcasted_iota(jnp.int32, (members, members), 0)
    c = lax.broadcasted_iota(jnp.int32, (members, members), 1)
    m_s[:, 0:members] = dot(x, x) + jnp.where(r == c, F32(members - 1), F32(0))
    m_s[:, members : 2 * members] = jnp.zeros((members, members), F32)
    m_s[:, members : members + 8] = dot(x, innovation)
    m = [m_s[8 * b : 8 * b + 8, :] for b in range(blocks)]
    sub = sublanes()
    for kb in range(blocks):
        cols = [
            [jnp.broadcast_to(m[b][:, 8 * kb + j : 8 * kb + j + 1], (8, 128)) for j in range(8)]
            for b in range(blocks)
        ]
        rows = m[kb]
        piv = list(cols[kb])
        for j in range(8):
            inv = F32(1) / wide(piv[j][j : j + 1])
            here = sub == j
            factor = piv[j]
            top = wide(rows[j : j + 1]) * inv
            rows = jnp.where(here, top, rows - factor * top)
            for q in range(j + 1, 8):
                top = wide(piv[q][j : j + 1]) * inv
                piv[q] = jnp.where(here, top, piv[q] - factor * top)
        spread = [wide(rows[j : j + 1]) for j in range(8)]
        for b in range(blocks):
            if b == kb:
                m[b] = rows
            else:
                acc = cols[b][0] * spread[0]
                for j in range(1, 8):
                    acc = acc + cols[b][j] * spread[j]
                m[b] = m[b] - acc
    for b in range(blocks):
        m_s[8 * b : 8 * b + 8, :] = m[b]
    turned = jnp.transpose(m_s[...], (1, 0))
    turned = turned[members : members + 8, :]
    for h in range(2):
        at = h * half
        first_ref[:, h * (half - 8) : (h + 1) * (half - 8)] = turned[:, at : at + half - 8]
        last_ref[:, 8 * h : 8 * h + 8] = turned[:, at + half - 8 : at + half]


def solve_weights(near, far, target, error):
    half, n_obs = near.shape
    members = 2 * half
    return pl.pallas_call(
        weights_kernel,
        in_specs=[VMEM_SPEC] * 4,
        out_specs=[VMEM_SPEC] * 2,
        scratch_shapes=[
            pltpu.VMEM((members, n_obs), F32),
            pltpu.VMEM((members, 2 * members), F32),
        ],
        out_shape=[
            jax.ShapeDtypeStruct((8, members - 16), F32), jax.ShapeDtypeStruct((8, 16), F32),
        ],
        compiler_params=pltpu.CompilerParams(vmem_limit_bytes=4 * 2**20),
        name="weights",
    )(near, far, target, error)


def shifted(w, pieces, f_ref, x):
    rows = jnp.concatenate([v[x].astype(F32) for v in pieces], axis=0).astype(BF16)
    shift = jnp.dot(w, rows, preferred_element_type=F32)
    return [f_ref[2 * x + t] + shift[:, 128 * t : 128 * t + 128] for t in range(2)]


def begin_kernel(w_ref, *refs):
    pieces, (f_ref, out_ref) = refs[:-2], refs[-2:]
    w = w_ref[...].astype(BF16)

    def chunk(g, _):
        for r in range(16):
            x = g * 16 + r
            for t, v in enumerate(shifted(w, pieces, f_ref, x)):
                out_ref[2 * x + t] = v
        return 0

    lax.fori_loop(0, pieces[0].shape[0] // 16, chunk, 0)


def update_kernel(w_ref, *refs):
    pieces, (f_ref, out_ref, row_s, done_s, sems) = refs[:-5], refs[-5:]
    step = row_s.shape[0]
    w = w_ref[...].astype(BF16)

    def leave(g):
        at = pl.ds(pl.multiple_of(g * step, step), step)
        return pltpu.make_async_copy(done_s.at[:, at, :], out_ref.at[:, at, :], sems.at[g])

    def chunk(g, _):
        for r in range(step):
            for t, v in enumerate(shifted(w, pieces, f_ref, g * step + r)):
                row_s[r, :, 128 * t : 128 * t + 128] = v
        at = pl.ds(pl.multiple_of(g * step, step), step)
        done_s[:, at, :] = jnp.swapaxes(row_s[...], 0, 1)
        leave(g).start()
        return 0

    count = pieces[0].shape[0] // step
    lax.fori_loop(0, count, chunk, 0)
    for g in range(count):
        leave(g).wait()


def begin(weights, pieces, forecast):
    return pl.pallas_call(
        begin_kernel,
        in_specs=[VMEM_SPEC] * (len(pieces) + 2),
        out_specs=VMEM_SPEC,
        out_shape=jax.ShapeDtypeStruct(forecast.shape, F32),
        compiler_params=pltpu.CompilerParams(vmem_limit_bytes=12 * 2**20),
        name="begin",
    )(weights, *pieces, forecast)


def update(weights, pieces, forecast):
    size_x, members, size_y = pieces[0].shape
    step = 32
    whole = (members, size_x, size_y)
    return pl.pallas_call(
        update_kernel,
        in_specs=[VMEM_SPEC] * (len(pieces) + 2),
        out_specs=HBM_SPEC,
        out_shape=jax.ShapeDtypeStruct(whole, F32),
        scratch_shapes=[
            pltpu.VMEM((step, members, size_y), F32),
            pltpu.VMEM(whole, F32),
            pltpu.SemaphoreType.DMA((size_x // step,)),
        ],
        compiler_params=pltpu.CompilerParams(vmem_limit_bytes=8 * 2**20),
        name="update",
    )(weights, *pieces, forecast)


def local(pressure, elevation, ks_field, melt_rate, obs_index, obs_value, obs_error, perturbation):
    n_x, n_y, n_m = (lax.axis_size(a) for a in ("tx", "ty", "mem"))
    tile_x, tile_y = lax.axis_index("tx"), lax.axis_index("ty")

    def ring(n, by):
        return [(i, (i + by) % n) for i in range(n)]

    n_obs = obs_index.shape[0]
    top, bottom, code, inside = ends(
        obs_index.reshape(n_obs // 128, 128), pressure, melt_rate, elevation, ks_field
    )
    up = lax.ppermute(bottom, "tx", ring(n_x, 1))
    down = lax.ppermute(top, "tx", ring(n_x, -1))
    pt, wt, left, right = turn(pressure, melt_rate, elevation, ks_field)
    above, below, left, right = halo_rows(up, down, top, bottom, left, right)
    from_left = lax.ppermute(right, "ty", ring(n_y, 1))
    from_right = lax.ppermute(left, "ty", ring(n_y, -1))
    forecast, rounded = run_steps(
        pt, wt, elevation, ks_field, above, below, from_left, from_right
    )
    picked = picks(code, forecast, inside)

    def send(v, by, swap=False):
        to = [(i, (i + 2 * (by if i % 2 == 0 else -by)) % n_m) for i in range(n_m)]
        return lax.ppermute(v, "mem", [(i, i ^ 1) for i in range(n_m)] if swap else to)

    block = n_obs // (n_x * n_y)
    tile = tile_x * n_y + tile_y
    target = (obs_value[:, None] + obs_error[:, None] * perturbation).T
    target = lax.dynamic_update_slice(jnp.zeros((8, n_obs), F32), target, (0, tile * block))
    per_row = 128 // block
    error = lax.dynamic_update_slice(
        jnp.zeros((n_obs // 128, 128), F32), obs_error[None],
        (tile // per_row, tile % per_row * block),
    )
    line = jnp.concatenate([picked, target, error], axis=1)
    a, b = send(rounded, 1), send(rounded, -1)
    own_far = send(rounded, 0, True)
    for axis, n in (("ty", n_y), ("tx", n_x)):
        bit = 1
        while bit < n:
            line = line + lax.ppermute(line, axis, [(i, i ^ bit) for i in range(n)])
            if bit == 1 and axis == "ty":
                line, own_far = lax.optimization_barrier((line, own_far))
            bit *= 2
    observed, target, error = (
        line[:, 0:n_obs], line[:, n_obs : 2 * n_obs], line[:, 2 * n_obs :]
    )
    observed, a, b = lax.optimization_barrier((observed, a, b))
    c = send(a, 1)
    parts = [send(observed, by) for by in (1, -1, 2)]
    near = jnp.concatenate([observed] + parts)
    far = send(near, 0, True)
    far, a, b = lax.optimization_barrier((far, a, b))
    a_far, b_far = send(a, 0, True), send(b, 0, True)
    w_first, w_last = solve_weights(near, far, target, error)
    begun = begin(w_first, [rounded, a, b, own_far, a_far, b_far], forecast)
    c_far = send(c, 0, True)
    return update(w_last, [c, c_far], begun)


def solution(mesh):
    placed = (
        P("mem", "tx", "ty"),
        P("tx", "ty"),
        P("tx", "ty"),
        P("mem", "tx", "ty"),
        P(),
        P(("tx", "ty")),
        P(("tx", "ty")),
        P(("tx", "ty"), "mem"),
    )
    return jax.shard_map(
        local, mesh=mesh, in_specs=placed, out_specs=P("mem", "tx", "ty"), check_vma=False
    )
```

```python
import functools

import jax
import jax.numpy as jnp
from jax import lax
from jax.experimental import pallas as pl
from jax.experimental.pallas import tpu as pltpu
from jax.sharding import PartitionSpec as P

SUBSTEPS = 4
W = SUBSTEPS
GROUP = 128 // W
ROWS = 16
F32 = jnp.float32
BF16 = jnp.bfloat16
VMEM_SPEC = pl.BlockSpec(memory_space=pltpu.VMEM)
HBM_SPEC = pl.BlockSpec(memory_space=pltpu.HBM)


def lanes():
    return lax.broadcasted_iota(jnp.int32, (8, 128), 1)


def sublanes():
    return lax.broadcasted_iota(jnp.int32, (8, 128), 0)


def wide(row):
    return jnp.broadcast_to(row, (8, 128))


def ends_kernel(
    obs_ref, p_ref, w_ref, e_ref, k_ref, top_ref, bottom_ref, code_ref, inside_ref,
    cubes, sems,
):
    _, size_x, size_y = p_ref.shape
    copies = []
    for i, lo in enumerate((0, size_x - 8)):
        for j, ref in enumerate((p_ref, w_ref)):
            copies.append((ref.at[:, pl.ds(lo, 8), :], cubes.at[2 * i + j]))
    copies = [pltpu.make_async_copy(a, b, sems.at[n]) for n, (a, b) in enumerate(copies)]
    for c in copies:
        c.start()
    bits_x, bits_y = size_x.bit_length() - 1, size_y.bit_length() - 1
    total_y = size_y * lax.axis_size("ty")
    obs = obs_ref[...]
    x = lax.shift_right_logical(obs, total_y.bit_length() - 1)
    y = obs & (total_y - 1)
    mine = (lax.shift_right_logical(x, bits_x) == lax.axis_index("tx")) & (
        lax.shift_right_logical(y, bits_y) == lax.axis_index("ty")
    )
    x, y = x & (size_x - 1), y & (size_y - 1)
    tile = x * (size_y // 128) + lax.shift_right_logical(y, 7)
    code_ref[...] = tile * 128 + ((lanes() - y) & 127)
    inside_ref[...] = jnp.where(mine, F32(1), F32(0))
    for c in copies:
        c.wait()
    sub = lax.broadcasted_iota(jnp.int32, (8, size_y), 0)
    for i, out in enumerate((top_ref, bottom_ref)):
        for j in range(2):
            turned = jnp.swapaxes(cubes[2 * i + j], 0, 1)
            for r in range(W):
                out[j * W + r] = turned[r if i == 0 else 8 - W + r]
        lo = (0, size_x - 8)[i]
        e, k = e_ref[lo : lo + 8, :], k_ref[lo : lo + 8, :]
        if i == 0:
            k = pltpu.roll(k, 4, 0)
        else:
            e = pltpu.roll(e, 4, 0)
        out[2 * W] = jnp.where(sub < 4, e, k)


def ends(obs, p, w, e, k):
    members, _, size_y = p.shape
    edge = jax.ShapeDtypeStruct((2 * W + 1, members, size_y), F32)
    return pl.pallas_call(
        ends_kernel,
        in_specs=[VMEM_SPEC] + [HBM_SPEC] * 2 + [VMEM_SPEC] * 2,
        out_specs=[VMEM_SPEC] * 4,
        out_shape=[
            edge, edge, jax.ShapeDtypeStruct(obs.shape, jnp.int32),
            jax.ShapeDtypeStruct(obs.shape, F32),
        ],
        scratch_shapes=[
            pltpu.VMEM((4, members, 8, size_y), F32),
            pltpu.SemaphoreType.DMA((4,)),
        ],
        compiler_params=pltpu.CompilerParams(vmem_limit_bytes=56 * 2**20),
        name="ends",
    )(obs, p, w, e, k)


def pack_rows(rows):
    slot = lanes() // W
    left = jnp.zeros((8, 128), F32)
    right = jnp.zeros((8, 128), F32)
    for r, a, b in rows:
        if r:
            a = pltpu.roll(a, W * r, 1)
            b = pltpu.roll(b, W * r, 1)
        left = jnp.where(slot == r, a, left)
        right = jnp.where(slot == (r - 1) % GROUP, b, right)
    return left, right


def turn_kernel(
    p_in, w_in, e_ref, k_ref, pt_out, wt_out, left_ref, right_ref,
    p_ref, w_ref, pt_ref, wt_ref, in_sems, out_sems,
):
    groups = left_ref.shape[0]

    def rows_of(g):
        return pl.ds(pl.multiple_of(g * GROUP, GROUP), GROUP)

    def fetch(g, f):
        src, dst = ((p_in, p_ref), (w_in, w_ref))[f]
        at = rows_of(g)
        return pltpu.make_async_copy(src.at[:, at, :], dst.at[:, at, :], in_sems.at[f, g])

    def leave(g, f):
        src, dst = ((pt_ref, pt_out), (wt_ref, wt_out))[f]
        at = rows_of(g)
        return pltpu.make_async_copy(src.at[at], dst.at[at], out_sems.at[f, g])

    for g in range(groups):
        for f in range(2):
            fetch(g, f).start()

    def group(g, _):
        at = rows_of(g)
        for f, (src, dst) in enumerate(((p_ref, pt_ref), (w_ref, wt_ref))):
            fetch(g, f).wait()
            rows = jnp.swapaxes(src[:, at, :] * F32(0.5), 0, 1)
            dst[at] = rows
            left_ref[g, f], right_ref[g, f] = pack_rows(
                (r, rows[r, :, 0:128], rows[r, :, 128:256]) for r in range(GROUP)
            )
            leave(g, f).start()
        fields = []
        for base, ref, factor in ((0, e_ref, 0.5), (4, k_ref, 0.25)):
            block = ref[at, :] * F32(factor)
            for q in range(GROUP // 8):
                part = block[8 * q : 8 * q + 8]
                fields.append((base + q, part[:, 0:128], part[:, 128:256]))
        left_ref[g, 2], right_ref[g, 2] = pack_rows(fields)
        return 0

    lax.fori_loop(0, groups, group, 0)
    for g in range(groups):
        for f in range(2):
            leave(g, f).wait()


def turn(p, w, e, k):
    members, size_x, size_y = p.shape
    groups = size_x // GROUP
    turned = (size_x, members, size_y)
    return pl.pallas_call(
        turn_kernel,
        in_specs=[HBM_SPEC] * 2 + [VMEM_SPEC] * 2,
        out_specs=[HBM_SPEC] * 2 + [VMEM_SPEC] * 2,
        out_shape=[jax.ShapeDtypeStruct(turned, F32)] * 2
        + [jax.ShapeDtypeStruct((groups, 3, 8, 128), F32)] * 2,
        scratch_shapes=[pltpu.VMEM(p.shape, F32)] * 2 + [pltpu.VMEM(turned, F32)] * 2
        + [pltpu.SemaphoreType.DMA((2, groups))] * 2,
        cost_estimate=pl.CostEstimate(flops=10**7, bytes_accessed=9 * 2**20, transcendentals=0),
        compiler_params=pltpu.CompilerParams(vmem_limit_bytes=52 * 2**20),
        name="turn",
    )(p, w, e, k)


def rows_kernel(
    up_ref, down_ref, top_ref, bottom_ref, left_in, right_in, above_ref, below_ref,
    left_ref, right_ref,
):
    tile, groups = lax.axis_index("tx"), left_in.shape[0]
    first, last = tile == 0, tile == lax.axis_size("tx") - 1
    left_ref[0:groups] = left_in[...]
    right_ref[0:groups] = right_in[...]
    sub = lax.broadcasted_iota(jnp.int32, (8, 256), 0)

    def mirrored(block):
        out = block
        for i in range(4):
            for base in (0, 4):
                row = block[base + 3 - i : base + 4 - i, :]
                out = jnp.where(sub == base + i, jnp.broadcast_to(row, (8, 256)), out)
        return out

    for flag, got, own, out in (
        (first, up_ref, top_ref, above_ref),
        (last, down_ref, bottom_ref, below_ref),
    ):
        for f in range(2):
            for i in range(W):
                row = jnp.where(flag, own[f * W + W - 1 - i], got[f * W + i])
                out[f * W + i] = row * F32(0.5)
        block = jnp.where(flag, mirrored(own[2 * W]), got[2 * W])
        out[2 * W] = block * jnp.where(sub < 4, F32(0.5), F32(0.25))
    for f in range(2):
        left_ref[groups, f], right_ref[groups, f] = pack_rows(
            (half * W + i, out[f * W + i, :, 0:128], out[f * W + i, :, 128:256])
            for half, out in enumerate((above_ref, below_ref))
            for i in range(W)
        )
    above, below = above_ref[2 * W], below_ref[2 * W]
    e = jnp.where(sub < 4, above, pltpu.roll(below, 4, 0))
    k = jnp.where(sub < 4, pltpu.roll(above, 4, 0), below)
    left_ref[groups, 2], right_ref[groups, 2] = pack_rows(
        (slot, v[:, 0:128], v[:, 128:256]) for slot, v in ((0, e), (4, k))
    )


def halo_rows(up, down, top, bottom, left, right):
    packs = jax.ShapeDtypeStruct((left.shape[0] + 1, *left.shape[1:]), F32)
    return pl.pallas_call(
        rows_kernel,
        in_specs=[VMEM_SPEC] * 6,
        out_specs=[VMEM_SPEC] * 4,
        out_shape=[jax.ShapeDtypeStruct(up.shape, F32)] * 2 + [packs] * 2,
        compiler_params=pltpu.CompilerParams(vmem_limit_bytes=4 * 2**20),
        name="rows",
    )(up, down, top, bottom, left, right)


def steps_kernel(
    pt_in, wt_in, e_ref, k_ref, above_ref, below_ref, fl_ref, fr_ref,
    out_ref, round_ref,
    p0, p1, w_s, fy_s, sum_s, e_s, er_s, k_s, kr_s, sems,
):
    size_x = pt_in.shape[0]
    lane = lanes()
    is_first, is_last = lane == 0, lane == 127
    groups = size_x // GROUP
    blocks = size_x // 8 + 2
    inner = (pl.ds(9, size_x), slice(None), pl.ds(0, 256))
    loads = [
        pltpu.make_async_copy(src, dst.at[inner], sems.at[i])
        for i, (src, dst) in enumerate(((pt_in, p0), (wt_in, w_s)))
    ]
    for c in loads:
        c.start()

    def halo(g, f, r):
        a, b = fr_ref[g, f], fl_ref[g, f]
        if r:
            a = pltpu.roll(a, 128 - W * r, 1)
            b = pltpu.roll(b, 128 - W * r, 1)
        return jnp.where(lane < 64, a, b)

    def spread(at, v, here, shifted):
        rolled = [pltpu.roll(u, 127, 1) for u in v]
        for t in range(3):
            here[at, :, 128 * t : 128 * t + 128] = v[t]
            shifted[at, :, 128 * t : 128 * t + 128] = jnp.where(
                is_last, rolled[(t + 1) % 3], rolled[t]
            )

    def unpack_group(g, _):
        for r in range(GROUP):
            for f, dst in ((0, p0), (1, w_s)):
                dst[g * GROUP + r + 9, :, 256:384] = halo(g, f, r)
        for q in range(GROUP // 8):
            rows = pl.ds(pl.multiple_of(g * GROUP + 8 * q, 8), 8)
            for base, ref, factor, here, shifted in (
                (0, e_ref, 0.5, e_s, er_s), (4, k_ref, 0.25, k_s, kr_s),
            ):
                v = [ref[rows, 128 * t : 128 * t + 128] * F32(factor) for t in range(2)]
                spread(g * (GROUP // 8) + q + 1, v + [halo(g, 2, base + q)], here, shifted)
        return 0

    lax.fori_loop(0, groups, unpack_group, 0)
    for r in range(2 * W):
        ref, y = (above_ref, 4 + r) if r < W else (below_ref, size_x + 4 + r)
        for f, dst in ((0, p0), (1, w_s)):
            dst[y + 1, :, 0:256] = ref[f * W + r % W]
            dst[y + 1, :, 256:384] = halo(groups, f, r)
    for base, here, shifted in ((0, e_s, er_s), (4, k_s, kr_s)):
        edge = pltpu.roll(halo(groups, 2, base), 4, 0)
        for at, ref, up in ((0, above_ref, base == 0), (blocks - 1, below_ref, base == 4)):
            v = ref[2 * W]
            v = pltpu.roll(v, 4, 0) if up else v
            spread(at, [v[:, 0:128], v[:, 128:256], edge], here, shifted)

    one, none = F32(1), F32(0)

    tile = lax.axis_index("ty")

    def edge_mask(at):
        return jnp.where(is_last & (jnp.broadcast_to(tile, (8, 128)) == at), none, one)

    mask_right, mask_left = edge_mask(lax.axis_size("ty") - 1), edge_mask(0)
    for c in loads:
        c.wait()

    def tiles(ref, at):
        return [ref[at, :, 128 * t : 128 * t + 128] for t in range(3)]

    def put(ref, at, v):
        for t in range(3):
            ref[at, :, 128 * t : 128 * t + 128] = v[t]

    def row_of(ref, b, u):
        return [wide(ref[b, u : u + 1, 128 * t : 128 * t + 128]) for t in range(3)]

    def step(src, dst):
        count = 8 * blocks // ROWS

        def body(i, carry):
            b_at = jnp.minimum(i, count - 1)
            c_at = jnp.maximum(i - 1, 0) * ROWS
            for u in range(ROWS):
                at = c_at + u
                s, fy = tiles(sum_s, at), tiles(fy_s, at)
                fr = [pltpu.roll(v, 1, 1) for v in fy]
                back = [jnp.where(is_first, fr[(t - 1) % 3], fr[t]) for t in range(3)]
                put(dst, at, [s[t] + (fy[t] - back[t]) for t in range(3)])
            p_old, h_old, c_old, fx_old = carry
            for u in range(ROWS):
                at = b_at * ROWS + u
                block = (b_at * (ROWS // 8) + u // 8, u % 8)
                p = tiles(src, at + 1)
                raw = [pltpu.roll(v, 127, 1) for v in p]
                pr = [jnp.where(is_last, raw[(t + 1) % 3], raw[t]) for t in range(3)]
                e, er = row_of(e_s, *block), row_of(er_s, *block)
                k, kr = row_of(k_s, *block), row_of(kr_s, *block)
                w = tiles(w_s, at)
                h = [p[t] + e[t] for t in range(3)]
                c = [k[t] * jnp.tanh(p[t]) + k[t] for t in range(3)]
                fy = [
                    (c[t] + (kr[t] * jnp.tanh(pr[t]) + kr[t])) * ((pr[t] + er[t]) - h[t])
                    for t in range(3)
                ]
                fy[1] = fy[1] * mask_right
                fy[2] = fy[2] * mask_left
                fx = [(c_old[t] + c[t]) * (h[t] - h_old[t]) for t in range(3)]
                put(sum_s, at, [(p_old[t] + w[t]) + (fx[t] - fx_old[t]) for t in range(3)])
                put(fy_s, at + 1, fy)
                p_old, h_old, c_old, fx_old = p, h, c, fx
            return p_old, h_old, c_old, fx_old

        zero = [jnp.zeros((8, 128), F32)] * 3
        lax.fori_loop(0, count + 1, body, (zero, zero, zero, zero))

    for s in range(SUBSTEPS):
        step(*((p0, p1) if s % 2 == 0 else (p1, p0)))
    last = p0 if SUBSTEPS % 2 == 0 else p1

    def leave(i, _):
        x = pl.multiple_of(i * 8, 8)
        for u in range(8):
            row = last[x + 9 + u, :, 0:256] * F32(2)
            out_ref[2 * x + 2 * u] = row[:, 0:128]
            out_ref[2 * x + 2 * u + 1] = row[:, 128:256]
            round_ref[x + u] = row.astype(BF16)
        return 0

    lax.fori_loop(0, size_x // 8, leave, 0)


def run_steps(pt, wt, e, k, above, below, from_left, from_right):
    size_x, members, size_y = pt.shape
    tile = pltpu.VMEM((size_x + 17, members, size_y + 128), F32)
    flat = pltpu.VMEM((size_x // 8 + 2, 8, size_y + 128), F32)
    return pl.pallas_call(
        steps_kernel,
        in_specs=[HBM_SPEC] * 2 + [VMEM_SPEC] * 6,
        out_specs=[VMEM_SPEC] * 2,
        scratch_shapes=[tile] * 5 + [flat] * 4 + [pltpu.SemaphoreType.DMA((2,))],
        out_shape=[
            jax.ShapeDtypeStruct((size_x * (size_y // 128), members, 128), F32),
            jax.ShapeDtypeStruct((size_x, members, size_y), BF16),
        ],
        compiler_params=pltpu.CompilerParams(vmem_limit_bytes=50 * 2**20),
        name="steps",
    )(pt, wt, e, k, above, below, from_left, from_right)


def pick_kernel(code_ref, f_ref, inside_ref, pick_ref):
    lane = lanes()

    def pick(g, _):
        acc = jnp.zeros((8, 128), F32)
        for u in range(128):
            code = code_ref[g, u]
            v = pltpu.roll(f_ref[lax.shift_right_logical(code, 7)], code & 127, 1)
            acc = jnp.where(lane == u, v, acc)
        keep = wide(inside_ref[pl.ds(g, 1), :]) > F32(0.5)
        pick_ref[:, pl.ds(pl.multiple_of(g * 128, 128), 128)] = jnp.where(keep, acc, F32(0))
        return 0

    lax.fori_loop(0, code_ref.shape[0], pick, 0)


def picks(code, forecast, inside):
    return pl.pallas_call(
        pick_kernel,
        grid_spec=pltpu.PrefetchScalarGridSpec(
            num_scalar_prefetch=1, grid=(), in_specs=[VMEM_SPEC] * 2, out_specs=VMEM_SPEC
        ),
        out_shape=jax.ShapeDtypeStruct((8, code.size), F32),
        compiler_params=pltpu.CompilerParams(vmem_limit_bytes=8 * 2**20),
        name="picks",
    )(code, forecast, inside)


def weights_kernel(near_ref, far_ref, target_ref, error_ref, first_ref, last_ref, x_s, m_s):
    half = near_ref.shape[0]
    members = 2 * half
    blocks = members // 8
    parts = [r[8 * b : 8 * b + 8, :] for r in (near_ref, far_ref) for b in range(half // 8)]
    total = parts[0]
    for part in parts[1:]:
        total = total + part
    mean = jnp.sum(total, axis=0, keepdims=True) * F32(1.0 / members)
    error = jnp.concatenate([error_ref[r : r + 1, :] for r in range(error_ref.shape[0])], axis=1)
    inverse = F32(1) / error
    for b, part in enumerate(parts):
        x_s[8 * b : 8 * b + 8, :] = (part - mean) * inverse
    innovation = (target_ref[...] - parts[0]) * inverse
    x = x_s[...]
    dims = (((1,), (1,)), ((), ()))
    dot = functools.partial(
        lax.dot_general, dimension_numbers=dims, precision=lax.Precision.HIGHEST,
        preferred_element_type=F32,
    )
    r = lax.broadcasted_iota(jnp.int32, (members, members), 0)
    c = lax.broadcasted_iota(jnp.int32, (members, members), 1)
    m_s[:, 0:members] = dot(x, x) + jnp.where(r == c, F32(members - 1), F32(0))
    m_s[:, members : 2 * members] = jnp.zeros((members, members), F32)
    m_s[:, members : members + 8] = dot(x, innovation)
    m = [m_s[8 * b : 8 * b + 8, :] for b in range(blocks)]
    sub = sublanes()
    for kb in range(blocks):
        cols = [
            [jnp.broadcast_to(m[b][:, 8 * kb + j : 8 * kb + j + 1], (8, 128)) for j in range(8)]
            for b in range(blocks)
        ]
        rows = m[kb]
        piv = list(cols[kb])
        for j in range(8):
            inv = F32(1) / wide(piv[j][j : j + 1])
            here = sub == j
            factor = piv[j]
            top = wide(rows[j : j + 1]) * inv
            rows = jnp.where(here, top, rows - factor * top)
            for q in range(j + 1, 8):
                top = wide(piv[q][j : j + 1]) * inv
                piv[q] = jnp.where(here, top, piv[q] - factor * top)
        spread = [wide(rows[j : j + 1]) for j in range(8)]
        for b in range(blocks):
            if b == kb:
                m[b] = rows
            else:
                acc = cols[b][0] * spread[0]
                for j in range(1, 8):
                    acc = acc + cols[b][j] * spread[j]
                m[b] = m[b] - acc
    for b in range(blocks):
        m_s[8 * b : 8 * b + 8, :] = m[b]
    turned = jnp.transpose(m_s[...], (1, 0))
    turned = turned[members : members + 8, :]
    for h in range(2):
        at = h * half
        first_ref[:, h * (half - 8) : (h + 1) * (half - 8)] = turned[:, at : at + half - 8]
        last_ref[:, 8 * h : 8 * h + 8] = turned[:, at + half - 8 : at + half]


def solve_weights(near, far, target, error):
    half, n_obs = near.shape
    members = 2 * half
    return pl.pallas_call(
        weights_kernel,
        in_specs=[VMEM_SPEC] * 4,
        out_specs=[VMEM_SPEC] * 2,
        scratch_shapes=[
            pltpu.VMEM((members, n_obs), F32),
            pltpu.VMEM((members, 2 * members), F32),
        ],
        out_shape=[
            jax.ShapeDtypeStruct((8, members - 16), F32), jax.ShapeDtypeStruct((8, 16), F32),
        ],
        compiler_params=pltpu.CompilerParams(vmem_limit_bytes=4 * 2**20),
        name="weights",
    )(near, far, target, error)


def shifted(w, pieces, f_ref, x, to):
    rows = jnp.concatenate([v[x].astype(F32) for v in pieces], axis=0).astype(BF16)
    shift = jnp.dot(w, rows, preferred_element_type=F32)
    return [f_ref[2 * to + t] + shift[:, 128 * t : 128 * t + 128] for t in range(2)]


def begin_kernel(w_ref, *refs):
    pieces, (f_ref, out_ref) = refs[:-2], refs[-2:]
    w = w_ref[...].astype(BF16)

    def chunk(g, _):
        for r in range(16):
            x = g * 16 + r
            for t, v in enumerate(shifted(w, pieces, f_ref, x, x)):
                out_ref[2 * x + t] = v
        return 0

    lax.fori_loop(0, pieces[0].shape[0] // 16, chunk, 0)


def update_kernel(w_ref, *refs):
    pieces, (f_ref, out_ref, row_s, done_s, sems) = refs[:-5], refs[-5:]
    step = row_s.shape[0]
    w = w_ref[...].astype(BF16)

    def leave(g):
        at = pl.ds(pl.multiple_of(g * step, step), step)
        return pltpu.make_async_copy(done_s.at[:, at, :], out_ref.at[:, at, :], sems.at[g])

    count = pieces[0].shape[0] // step

    def chunk(half, i, _):
        g = half * count + i
        for r in range(step):
            at = (i * step + r, g * step + r)
            for t, v in enumerate(shifted(w, pieces[half::2], f_ref, *at)):
                row_s[r, :, 128 * t : 128 * t + 128] = v
        at = pl.ds(pl.multiple_of(g * step, step), step)
        done_s[:, at, :] = jnp.swapaxes(row_s[...], 0, 1)
        leave(g).start()
        return 0

    for half in range(2):
        lax.fori_loop(0, count, functools.partial(chunk, half), 0)
    for g in range(2 * count):
        leave(g).wait()


def begin(weights, pieces, forecast):
    return pl.pallas_call(
        begin_kernel,
        in_specs=[VMEM_SPEC] * (len(pieces) + 2),
        out_specs=VMEM_SPEC,
        out_shape=jax.ShapeDtypeStruct(forecast.shape, F32),
        compiler_params=pltpu.CompilerParams(vmem_limit_bytes=12 * 2**20),
        name="begin",
    )(weights, *pieces, forecast)


def update(weights, pieces, forecast):
    rows, members, size_y = pieces[0].shape
    size_x = 2 * rows
    step = 32
    whole = (members, size_x, size_y)
    return pl.pallas_call(
        update_kernel,
        in_specs=[VMEM_SPEC] * (len(pieces) + 2),
        out_specs=HBM_SPEC,
        out_shape=jax.ShapeDtypeStruct(whole, F32),
        scratch_shapes=[
            pltpu.VMEM((step, members, size_y), F32),
            pltpu.VMEM(whole, F32),
            pltpu.SemaphoreType.DMA((size_x // step,)),
        ],
        compiler_params=pltpu.CompilerParams(vmem_limit_bytes=8 * 2**20),
        name="update",
    )(weights, *pieces, forecast)


def local(pressure, elevation, ks_field, melt_rate, obs_index, obs_value, obs_error, perturbation):
    _, size_x, _ = pressure.shape
    n_x, n_y, n_m = (lax.axis_size(a) for a in ("tx", "ty", "mem"))
    tile_x, tile_y = lax.axis_index("tx"), lax.axis_index("ty")

    def ring(n, by):
        return [(i, (i + by) % n) for i in range(n)]

    n_obs = obs_index.shape[0]
    top, bottom, code, inside = ends(
        obs_index.reshape(n_obs // 128, 128), pressure, melt_rate, elevation, ks_field
    )
    up = lax.ppermute(bottom, "tx", ring(n_x, 1))
    down = lax.ppermute(top, "tx", ring(n_x, -1))
    pt, wt, left, right = turn(pressure, melt_rate, elevation, ks_field)
    above, below, left, right = halo_rows(up, down, top, bottom, left, right)
    from_left = lax.ppermute(right, "ty", ring(n_y, 1))
    from_right = lax.ppermute(left, "ty", ring(n_y, -1))
    forecast, rounded = run_steps(
        pt, wt, elevation, ks_field, above, below, from_left, from_right
    )
    picked = picks(code, forecast, inside)

    def send(v, by, swap=False):
        to = [(i, (i + 2 * (by if i % 2 == 0 else -by)) % n_m) for i in range(n_m)]
        return lax.ppermute(v, "mem", [(i, i ^ 1) for i in range(n_m)] if swap else to)

    block = n_obs // (n_x * n_y)
    tile = tile_x * n_y + tile_y
    target = (obs_value[:, None] + obs_error[:, None] * perturbation).T
    target = lax.dynamic_update_slice(jnp.zeros((8, n_obs), F32), target, (0, tile * block))
    per_row = 128 // block
    error = lax.dynamic_update_slice(
        jnp.zeros((n_obs // 128, 128), F32), obs_error[None],
        (tile // per_row, tile % per_row * block),
    )
    line = jnp.concatenate([picked, target, error], axis=1)
    a, b = send(rounded, 1), send(rounded, -1)
    own_far = send(rounded, 0, True)
    for axis, n in (("ty", n_y), ("tx", n_x)):
        bit = 1
        while bit < n:
            line = line + lax.ppermute(line, axis, [(i, i ^ bit) for i in range(n)])
            if bit == 1 and axis == "ty":
                line, own_far = lax.optimization_barrier((line, own_far))
            bit *= 2
    observed, target, error = (
        line[:, 0:n_obs], line[:, n_obs : 2 * n_obs], line[:, 2 * n_obs :]
    )
    observed, a, b = lax.optimization_barrier((observed, a, b))
    half = size_x // 2
    c0, c1 = send(a[:half], 1), send(b[half:], -1)
    parts = [send(observed, by) for by in (1, -1, 2)]
    near = jnp.concatenate([observed] + parts)
    far = send(near, 0, True)
    far, a, b = lax.optimization_barrier((far, a, b))
    a_far, b_far = send(a, 0, True), send(b, 0, True)
    w_first, w_last = solve_weights(near, far, target, error)
    begun = begin(w_first, [rounded, a, b, own_far, a_far, b_far], forecast)
    return update(w_last, [c0, c1, send(c0, 0, True), send(c1, 0, True)], begun)


def solution(mesh):
    placed = (
        P("mem", "tx", "ty"),
        P("tx", "ty"),
        P("tx", "ty"),
        P("mem", "tx", "ty"),
        P(),
        P(("tx", "ty")),
        P(("tx", "ty")),
        P(("tx", "ty"), "mem"),
    )
    return jax.shard_map(
        local, mesh=mesh, in_specs=placed, out_specs=P("mem", "tx", "ty"), check_vma=False
    )
```

```python
import functools

import jax
import jax.numpy as jnp
from jax import lax
from jax.experimental import pallas as pl
from jax.experimental.pallas import tpu as pltpu
from jax.sharding import PartitionSpec as P

SUBSTEPS = 4
W = SUBSTEPS
GROUP = 128 // W
F32 = jnp.float32
BF16 = jnp.bfloat16
VMEM_SPEC = pl.BlockSpec(memory_space=pltpu.VMEM)
HBM_SPEC = pl.BlockSpec(memory_space=pltpu.HBM)


def lanes():
    return lax.broadcasted_iota(jnp.int32, (8, 128), 1)


def sublanes():
    return lax.broadcasted_iota(jnp.int32, (8, 128), 0)


def wide(row):
    return jnp.broadcast_to(row, (8, 128))


def ends_kernel(
    obs_ref, p_ref, w_ref, e_ref, k_ref, top_ref, bottom_ref, code_ref, inside_ref,
    cubes, sems,
):
    _, size_x, size_y = p_ref.shape
    copies = []
    for i, lo in enumerate((0, size_x - 8)):
        for j, ref in enumerate((p_ref, w_ref)):
            copies.append((ref.at[:, pl.ds(lo, 8), :], cubes.at[2 * i + j]))
    copies = [pltpu.make_async_copy(a, b, sems.at[n]) for n, (a, b) in enumerate(copies)]
    for c in copies:
        c.start()
    bits_x, bits_y = size_x.bit_length() - 1, size_y.bit_length() - 1
    total_y = size_y * lax.axis_size("ty")
    obs = obs_ref[...]
    x = lax.shift_right_logical(obs, total_y.bit_length() - 1)
    y = obs & (total_y - 1)
    mine = (lax.shift_right_logical(x, bits_x) == lax.axis_index("tx")) & (
        lax.shift_right_logical(y, bits_y) == lax.axis_index("ty")
    )
    x, y = x & (size_x - 1), y & (size_y - 1)
    tile = x * (size_y // 128) + lax.shift_right_logical(y, 7)
    code_ref[...] = tile * 128 + ((lanes() - y) & 127)
    inside_ref[...] = jnp.where(mine, F32(1), F32(0))
    for c in copies:
        c.wait()
    sub = lax.broadcasted_iota(jnp.int32, (8, size_y), 0)
    for i, out in enumerate((top_ref, bottom_ref)):
        for j in range(2):
            turned = jnp.swapaxes(cubes[2 * i + j], 0, 1)
            for r in range(W):
                out[j * W + r] = turned[r if i == 0 else 8 - W + r]
        lo = (0, size_x - 8)[i]
        e, k = e_ref[lo : lo + 8, :], k_ref[lo : lo + 8, :]
        if i == 0:
            k = pltpu.roll(k, 4, 0)
        else:
            e = pltpu.roll(e, 4, 0)
        out[2 * W] = jnp.where(sub < 4, e, k)


def ends(obs, p, w, e, k):
    members, _, size_y = p.shape
    edge = jax.ShapeDtypeStruct((2 * W + 1, members, size_y), F32)
    return pl.pallas_call(
        ends_kernel,
        in_specs=[VMEM_SPEC] + [HBM_SPEC] * 2 + [VMEM_SPEC] * 2,
        out_specs=[VMEM_SPEC] * 4,
        out_shape=[
            edge, edge, jax.ShapeDtypeStruct(obs.shape, jnp.int32),
            jax.ShapeDtypeStruct(obs.shape, F32),
        ],
        scratch_shapes=[
            pltpu.VMEM((4, members, 8, size_y), F32),
            pltpu.SemaphoreType.DMA((4,)),
        ],
        compiler_params=pltpu.CompilerParams(vmem_limit_bytes=56 * 2**20),
        name="ends",
    )(obs, p, w, e, k)


def pack_rows(rows):
    slot = lanes() // W
    left = jnp.zeros((8, 128), F32)
    right = jnp.zeros((8, 128), F32)
    for r, a, b in rows:
        if r:
            a = pltpu.roll(a, W * r, 1)
            b = pltpu.roll(b, W * r, 1)
        left = jnp.where(slot == r, a, left)
        right = jnp.where(slot == (r - 1) % GROUP, b, right)
    return left, right


def turn_kernel(
    p_in, w_in, e_ref, k_ref, pt_out, wt_out, left_ref, right_ref,
    p_ref, w_ref, pt_ref, wt_ref, in_sems, out_sems,
):
    groups = left_ref.shape[0]

    def rows_of(g):
        return pl.ds(pl.multiple_of(g * GROUP, GROUP), GROUP)

    def fetch(g, f):
        src, dst = ((p_in, p_ref), (w_in, w_ref))[f]
        at = rows_of(g)
        return pltpu.make_async_copy(src.at[:, at, :], dst.at[:, at, :], in_sems.at[f, g])

    def leave(g, f):
        src, dst = ((pt_ref, pt_out), (wt_ref, wt_out))[f]
        at = rows_of(g)
        return pltpu.make_async_copy(src.at[at], dst.at[at], out_sems.at[f, g])

    for g in range(groups):
        for f in range(2):
            fetch(g, f).start()

    def group(g, _):
        at = rows_of(g)
        for f, (src, dst) in enumerate(((p_ref, pt_ref), (w_ref, wt_ref))):
            fetch(g, f).wait()
            rows = jnp.swapaxes(src[:, at, :] * F32(0.5), 0, 1)
            dst[at] = rows
            left_ref[g, f], right_ref[g, f] = pack_rows(
                (r, rows[r, :, 0:128], rows[r, :, 128:256]) for r in range(GROUP)
            )
            leave(g, f).start()
        fields = []
        for base, ref, factor in ((0, e_ref, 0.5), (4, k_ref, 0.25)):
            block = ref[at, :] * F32(factor)
            for q in range(GROUP // 8):
                part = block[8 * q : 8 * q + 8]
                fields.append((base + q, part[:, 0:128], part[:, 128:256]))
        left_ref[g, 2], right_ref[g, 2] = pack_rows(fields)
        return 0

    lax.fori_loop(0, groups, group, 0)
    for g in range(groups):
        for f in range(2):
            leave(g, f).wait()


def turn(p, w, e, k):
    members, size_x, size_y = p.shape
    groups = size_x // GROUP
    turned = (size_x, members, size_y)
    return pl.pallas_call(
        turn_kernel,
        in_specs=[HBM_SPEC] * 2 + [VMEM_SPEC] * 2,
        out_specs=[HBM_SPEC] * 2 + [VMEM_SPEC] * 2,
        out_shape=[jax.ShapeDtypeStruct(turned, F32)] * 2
        + [jax.ShapeDtypeStruct((groups, 3, 8, 128), F32)] * 2,
        scratch_shapes=[pltpu.VMEM(p.shape, F32)] * 2 + [pltpu.VMEM(turned, F32)] * 2
        + [pltpu.SemaphoreType.DMA((2, groups))] * 2,
        cost_estimate=pl.CostEstimate(flops=10**7, bytes_accessed=9 * 2**20, transcendentals=0),
        compiler_params=pltpu.CompilerParams(vmem_limit_bytes=52 * 2**20),
        name="turn",
    )(p, w, e, k)


def rows_kernel(
    up_ref, down_ref, top_ref, bottom_ref, left_in, right_in, above_ref, below_ref,
    left_ref, right_ref,
):
    tile, groups = lax.axis_index("tx"), left_in.shape[0]
    first, last = tile == 0, tile == lax.axis_size("tx") - 1
    left_ref[0:groups] = left_in[...]
    right_ref[0:groups] = right_in[...]
    sub = lax.broadcasted_iota(jnp.int32, (8, 256), 0)

    def mirrored(block):
        out = block
        for i in range(4):
            for base in (0, 4):
                row = block[base + 3 - i : base + 4 - i, :]
                out = jnp.where(sub == base + i, jnp.broadcast_to(row, (8, 256)), out)
        return out

    for flag, got, own, out in (
        (first, up_ref, top_ref, above_ref),
        (last, down_ref, bottom_ref, below_ref),
    ):
        for f in range(2):
            for i in range(W):
                row = jnp.where(flag, own[f * W + W - 1 - i], got[f * W + i])
                out[f * W + i] = row * F32(0.5)
        block = jnp.where(flag, mirrored(own[2 * W]), got[2 * W])
        out[2 * W] = block * jnp.where(sub < 4, F32(0.5), F32(0.25))
    for f in range(2):
        left_ref[groups, f], right_ref[groups, f] = pack_rows(
            (half * W + i, out[f * W + i, :, 0:128], out[f * W + i, :, 128:256])
            for half, out in enumerate((above_ref, below_ref))
            for i in range(W)
        )
    above, below = above_ref[2 * W], below_ref[2 * W]
    e = jnp.where(sub < 4, above, pltpu.roll(below, 4, 0))
    k = jnp.where(sub < 4, pltpu.roll(above, 4, 0), below)
    left_ref[groups, 2], right_ref[groups, 2] = pack_rows(
        (slot, v[:, 0:128], v[:, 128:256]) for slot, v in ((0, e), (4, k))
    )


def halo_rows(up, down, top, bottom, left, right):
    packs = jax.ShapeDtypeStruct((left.shape[0] + 1, *left.shape[1:]), F32)
    return pl.pallas_call(
        rows_kernel,
        in_specs=[VMEM_SPEC] * 6,
        out_specs=[VMEM_SPEC] * 4,
        out_shape=[jax.ShapeDtypeStruct(up.shape, F32)] * 2 + [packs] * 2,
        compiler_params=pltpu.CompilerParams(vmem_limit_bytes=4 * 2**20),
        name="rows",
    )(up, down, top, bottom, left, right)


def steps_kernel(
    pt_in, wt_in, e_ref, k_ref, above_ref, below_ref, fl_ref, fr_ref,
    out_ref, round_ref,
    p0, p1, w_s, fy_s, sum_s, fy2_s, sum2_s, e_s, er_s, k_s, kr_s, sems,
):
    size_x = pt_in.shape[0]
    lane = lanes()
    is_first, is_last = lane == 0, lane == 127
    groups = size_x // GROUP
    blocks = size_x // 8 + 2
    inner = (pl.ds(9, size_x), slice(None), pl.ds(0, 256))
    loads = [
        pltpu.make_async_copy(src, dst.at[inner], sems.at[i])
        for i, (src, dst) in enumerate(((pt_in, p0), (wt_in, w_s)))
    ]
    for c in loads:
        c.start()

    def halo(g, f, r):
        a, b = fr_ref[g, f], fl_ref[g, f]
        if r:
            a = pltpu.roll(a, 128 - W * r, 1)
            b = pltpu.roll(b, 128 - W * r, 1)
        return jnp.where(lane < 64, a, b)

    def spread(at, v, here, shifted):
        rolled = [pltpu.roll(u, 127, 1) for u in v]
        for t in range(3):
            here[at, :, 128 * t : 128 * t + 128] = v[t]
            shifted[at, :, 128 * t : 128 * t + 128] = jnp.where(
                is_last, rolled[(t + 1) % 3], rolled[t]
            )

    def unpack_group(g, _):
        for r in range(GROUP):
            for f, dst in ((0, p0), (1, w_s)):
                dst[g * GROUP + r + 9, :, 256:384] = halo(g, f, r)
        for q in range(GROUP // 8):
            rows = pl.ds(pl.multiple_of(g * GROUP + 8 * q, 8), 8)
            for base, ref, factor, here, shifted in (
                (0, e_ref, 0.5, e_s, er_s), (4, k_ref, 0.25, k_s, kr_s),
            ):
                v = [ref[rows, 128 * t : 128 * t + 128] * F32(factor) for t in range(2)]
                spread(g * (GROUP // 8) + q + 1, v + [halo(g, 2, base + q)], here, shifted)
        return 0

    lax.fori_loop(0, groups, unpack_group, 0)
    for r in range(2 * W):
        ref, y = (above_ref, 4 + r) if r < W else (below_ref, size_x + 4 + r)
        for f, dst in ((0, p0), (1, w_s)):
            dst[y + 1, :, 0:256] = ref[f * W + r % W]
            dst[y + 1, :, 256:384] = halo(groups, f, r)
    for base, here, shifted in ((0, e_s, er_s), (4, k_s, kr_s)):
        edge = pltpu.roll(halo(groups, 2, base), 4, 0)
        for at, ref, up in ((0, above_ref, base == 0), (blocks - 1, below_ref, base == 4)):
            v = ref[2 * W]
            v = pltpu.roll(v, 4, 0) if up else v
            spread(at, [v[:, 0:128], v[:, 128:256], edge], here, shifted)

    one, none = F32(1), F32(0)

    tile = lax.axis_index("ty")

    def edge_mask(at):
        return jnp.where(is_last & (jnp.broadcast_to(tile, (8, 128)) == at), none, one)

    mask_right, mask_left = edge_mask(lax.axis_size("ty") - 1), edge_mask(0)
    for c in loads:
        c.wait()

    def tiles(ref, at):
        return [ref[at, :, 128 * t : 128 * t + 128] for t in range(3)]

    def put(ref, at, v):
        for t in range(3):
            ref[at, :, 128 * t : 128 * t + 128] = v[t]

    def row_of(ref, b, u):
        return [wide(ref[b, u : u + 1, 128 * t : 128 * t + 128]) for t in range(3)]

    def finish(dst, at, sums, fluxes):
        for u in range(8):
            fy = tiles(fluxes, u)
            fr = [pltpu.roll(v, 1, 1) for v in fy]
            s = tiles(sums, u)
            back = [jnp.where(is_first, fr[(t - 1) % 3], fr[t]) for t in range(3)]
            put(dst, at * 8 + u, [s[t] + (fy[t] - back[t]) for t in range(3)])

    def fluxes_of(src, at, sums, fluxes, carry):
        p_old, h_old, c_old, fx_old, fy_old = carry
        for u in range(8):
            p = tiles(src, at * 8 + u + 1)
            raw = [pltpu.roll(v, 127, 1) for v in p]
            pr = [jnp.where(is_last, raw[(t + 1) % 3], raw[t]) for t in range(3)]
            e, er = row_of(e_s, at, u), row_of(er_s, at, u)
            k, kr = row_of(k_s, at, u), row_of(kr_s, at, u)
            w = tiles(w_s, at * 8 + u)
            h = [p[t] + e[t] for t in range(3)]
            c = [k[t] * jnp.tanh(p[t]) + k[t] for t in range(3)]
            fy = [
                (c[t] + (kr[t] * jnp.tanh(pr[t]) + kr[t])) * ((pr[t] + er[t]) - h[t])
                for t in range(3)
            ]
            fy[1] = fy[1] * mask_right
            fy[2] = fy[2] * mask_left
            fx = [(c_old[t] + c[t]) * (h[t] - h_old[t]) for t in range(3)]
            put(sums, u, [(p_old[t] + w[t]) + (fx[t] - fx_old[t]) for t in range(3)])
            put(fluxes, u, fy_old)
            p_old, h_old, c_old, fx_old, fy_old = p, h, c, fx, fy
        return p_old, h_old, c_old, fx_old, fy_old

    def step(src, dst):
        def body(i, carry):
            carry = fluxes_of(src, 2 * i, sum_s, fy_s, carry)
            finish(dst, jnp.maximum(2 * i - 1, 0), sum2_s, fy2_s)
            carry = fluxes_of(src, 2 * i + 1, sum2_s, fy2_s, carry)
            finish(dst, 2 * i, sum_s, fy_s)
            return carry

        zero = [jnp.zeros((8, 128), F32)] * 3
        lax.fori_loop(0, blocks // 2, body, (zero,) * 5)
        finish(dst, blocks - 1, sum2_s, fy2_s)

    for s in range(SUBSTEPS):
        step(*((p0, p1) if s % 2 == 0 else (p1, p0)))
    last = p0 if SUBSTEPS % 2 == 0 else p1

    def leave(i, _):
        x = pl.multiple_of(i * 8, 8)
        for u in range(8):
            row = last[x + 9 + u, :, 0:256] * F32(2)
            out_ref[2 * x + 2 * u] = row[:, 0:128]
            out_ref[2 * x + 2 * u + 1] = row[:, 128:256]
            round_ref[x + u] = row.astype(BF16)
        return 0

    lax.fori_loop(0, size_x // 8, leave, 0)


def run_steps(pt, wt, e, k, above, below, from_left, from_right):
    size_x, members, size_y = pt.shape
    tile = pltpu.VMEM((size_x + 17, members, size_y + 128), F32)
    flat = pltpu.VMEM((size_x // 8 + 2, 8, size_y + 128), F32)
    few = pltpu.VMEM((8, members, size_y + 128), F32)
    return pl.pallas_call(
        steps_kernel,
        in_specs=[HBM_SPEC] * 2 + [VMEM_SPEC] * 6,
        out_specs=[VMEM_SPEC] * 2,
        scratch_shapes=[tile] * 3 + [few] * 4 + [flat] * 4 + [pltpu.SemaphoreType.DMA((2,))],
        out_shape=[
            jax.ShapeDtypeStruct((size_x * (size_y // 128), members, 128), F32),
            jax.ShapeDtypeStruct((size_x, members, size_y), BF16),
        ],
        compiler_params=pltpu.CompilerParams(vmem_limit_bytes=50 * 2**20),
        name="steps",
    )(pt, wt, e, k, above, below, from_left, from_right)


def pick_kernel(code_ref, f_ref, inside_ref, pick_ref):
    lane = lanes()

    def pick(g, _):
        acc = jnp.zeros((8, 128), F32)
        for u in range(128):
            code = code_ref[g, u]
            v = pltpu.roll(f_ref[lax.shift_right_logical(code, 7)], code, 1)
            acc = jnp.where(lane == u, v, acc)
        keep = wide(inside_ref[pl.ds(g, 1), :]) > F32(0.5)
        pick_ref[:, pl.ds(pl.multiple_of(g * 128, 128), 128)] = jnp.where(keep, acc, F32(0))
        return 0

    lax.fori_loop(0, code_ref.shape[0], pick, 0)


def picks(code, forecast, inside):
    return pl.pallas_call(
        pick_kernel,
        grid_spec=pltpu.PrefetchScalarGridSpec(
            num_scalar_prefetch=1, grid=(), in_specs=[VMEM_SPEC] * 2, out_specs=VMEM_SPEC
        ),
        out_shape=jax.ShapeDtypeStruct((8, code.size), F32),
        compiler_params=pltpu.CompilerParams(vmem_limit_bytes=8 * 2**20),
        name="picks",
    )(code, forecast, inside)


def weights_kernel(near_ref, far_ref, target_ref, error_ref, first_ref, last_ref, x_s, m_s):
    half = near_ref.shape[0]
    members = 2 * half
    blocks = members // 8
    parts = [r[8 * b : 8 * b + 8, :] for r in (near_ref, far_ref) for b in range(half // 8)]
    total = parts[0]
    for part in parts[1:]:
        total = total + part
    mean = jnp.sum(total, axis=0, keepdims=True) * F32(1.0 / members)
    error = jnp.concatenate([error_ref[r : r + 1, :] for r in range(error_ref.shape[0])], axis=1)
    inverse = F32(1) / error
    for b, part in enumerate(parts):
        x_s[8 * b : 8 * b + 8, :] = (part - mean) * inverse
    innovation = (target_ref[...] - parts[0]) * inverse
    x = x_s[...]
    dims = (((1,), (1,)), ((), ()))
    dot = functools.partial(
        lax.dot_general, dimension_numbers=dims, precision=lax.Precision.HIGHEST,
        preferred_element_type=F32,
    )
    r = lax.broadcasted_iota(jnp.int32, (members, members), 0)
    c = lax.broadcasted_iota(jnp.int32, (members, members), 1)
    m_s[:, 0:members] = dot(x, x) + jnp.where(r == c, F32(members - 1), F32(0))
    m_s[:, members : 2 * members] = jnp.zeros((members, members), F32)
    m_s[:, members : members + 8] = dot(x, innovation)
    m = [m_s[8 * b : 8 * b + 8, :] for b in range(blocks)]
    sub = sublanes()
    for kb in range(blocks):
        cols = [
            [jnp.broadcast_to(m[b][:, 8 * kb + j : 8 * kb + j + 1], (8, 128)) for j in range(8)]
            for b in range(blocks)
        ]
        rows = m[kb]
        piv = list(cols[kb])
        for j in range(8):
            inv = F32(1) / wide(piv[j][j : j + 1])
            here = sub == j
            factor = piv[j]
            top = wide(rows[j : j + 1]) * inv
            rows = jnp.where(here, top, rows - factor * top)
            for q in range(j + 1, 8):
                top = wide(piv[q][j : j + 1]) * inv
                piv[q] = jnp.where(here, top, piv[q] - factor * top)
        spread = [wide(rows[j : j + 1]) for j in range(8)]
        for b in range(blocks):
            if b == kb:
                m[b] = rows
            else:
                acc = cols[b][0] * spread[0]
                for j in range(1, 8):
                    acc = acc + cols[b][j] * spread[j]
                m[b] = m[b] - acc
    for b in range(blocks):
        m_s[8 * b : 8 * b + 8, :] = m[b]
    turned = jnp.transpose(m_s[...], (1, 0))
    turned = turned[members : members + 8, :]
    for h in range(2):
        at = h * half
        first_ref[:, h * (half - 8) : (h + 1) * (half - 8)] = turned[:, at : at + half - 8]
        last_ref[:, 8 * h : 8 * h + 8] = turned[:, at + half - 8 : at + half]


def solve_weights(near, far, target, error):
    half, n_obs = near.shape
    members = 2 * half
    return pl.pallas_call(
        weights_kernel,
        in_specs=[VMEM_SPEC] * 4,
        out_specs=[VMEM_SPEC] * 2,
        scratch_shapes=[
            pltpu.VMEM((members, n_obs), F32),
            pltpu.VMEM((members, 2 * members), F32),
        ],
        out_shape=[
            jax.ShapeDtypeStruct((8, members - 16), F32), jax.ShapeDtypeStruct((8, 16), F32),
        ],
        compiler_params=pltpu.CompilerParams(vmem_limit_bytes=4 * 2**20),
        name="weights",
    )(near, far, target, error)


def shifted(w, pieces, f_ref, x, to):
    rows = jnp.concatenate([v[x].astype(F32) for v in pieces], axis=0).astype(BF16)
    shift = jnp.dot(w, rows, preferred_element_type=F32)
    return [f_ref[2 * to + t] + shift[:, 128 * t : 128 * t + 128] for t in range(2)]


def begin_kernel(w_ref, *refs):
    pieces, (f_ref, out_ref) = refs[:-2], refs[-2:]
    w = w_ref[...].astype(BF16)

    def chunk(g, _):
        for r in range(16):
            x = g * 16 + r
            for t, v in enumerate(shifted(w, pieces, f_ref, x, x)):
                out_ref[2 * x + t] = v
        return 0

    lax.fori_loop(0, pieces[0].shape[0] // 16, chunk, 0)


def update_kernel(w_ref, *refs):
    pieces, (f_ref, out_ref, row_s, done_s, sems) = refs[:-5], refs[-5:]
    step = row_s.shape[0]
    w = w_ref[...].astype(BF16)

    def leave(g):
        at = pl.ds(pl.multiple_of(g * step, step), step)
        return pltpu.make_async_copy(done_s.at[:, at, :], out_ref.at[:, at, :], sems.at[g])

    count = pieces[0].shape[0] // step

    def chunk(half, i, _):
        g = half * count + i
        for r in range(step):
            at = (i * step + r, g * step + r)
            for t, v in enumerate(shifted(w, pieces[half::2], f_ref, *at)):
                row_s[r, :, 128 * t : 128 * t + 128] = v
        at = pl.ds(pl.multiple_of(g * step, step), step)
        done_s[:, at, :] = jnp.swapaxes(row_s[...], 0, 1)
        leave(g).start()
        return 0

    for half in range(2):
        lax.fori_loop(0, count, functools.partial(chunk, half), 0)
    for g in range(2 * count):
        leave(g).wait()


def begin(weights, pieces, forecast):
    return pl.pallas_call(
        begin_kernel,
        in_specs=[VMEM_SPEC] * (len(pieces) + 2),
        out_specs=VMEM_SPEC,
        out_shape=jax.ShapeDtypeStruct(forecast.shape, F32),
        compiler_params=pltpu.CompilerParams(vmem_limit_bytes=12 * 2**20),
        name="begin",
    )(weights, *pieces, forecast)


def update(weights, pieces, forecast):
    rows, members, size_y = pieces[0].shape
    size_x = 2 * rows
    step = 32
    whole = (members, size_x, size_y)
    return pl.pallas_call(
        update_kernel,
        in_specs=[VMEM_SPEC] * (len(pieces) + 2),
        out_specs=HBM_SPEC,
        out_shape=jax.ShapeDtypeStruct(whole, F32),
        scratch_shapes=[
            pltpu.VMEM((step, members, size_y), F32),
            pltpu.VMEM(whole, F32),
            pltpu.SemaphoreType.DMA((size_x // step,)),
        ],
        compiler_params=pltpu.CompilerParams(vmem_limit_bytes=8 * 2**20),
        name="update",
    )(weights, *pieces, forecast)


def local(pressure, elevation, ks_field, melt_rate, obs_index, obs_value, obs_error, perturbation):
    _, size_x, _ = pressure.shape
    n_x, n_y, n_m = (lax.axis_size(a) for a in ("tx", "ty", "mem"))
    tile_x, tile_y = lax.axis_index("tx"), lax.axis_index("ty")

    def ring(n, by):
        return [(i, (i + by) % n) for i in range(n)]

    n_obs = obs_index.shape[0]
    top, bottom, code, inside = ends(
        obs_index.reshape(n_obs // 128, 128), pressure, melt_rate, elevation, ks_field
    )
    up = lax.ppermute(bottom, "tx", ring(n_x, 1))
    down = lax.ppermute(top, "tx", ring(n_x, -1))
    pt, wt, left, right = turn(pressure, melt_rate, elevation, ks_field)
    above, below, left, right = halo_rows(up, down, top, bottom, left, right)
    from_left = lax.ppermute(right, "ty", ring(n_y, 1))
    from_right = lax.ppermute(left, "ty", ring(n_y, -1))
    forecast, rounded = run_steps(
        pt, wt, elevation, ks_field, above, below, from_left, from_right
    )
    picked = picks(code, forecast, inside)

    def send(v, by, swap=False):
        to = [(i, (i + 2 * (by if i % 2 == 0 else -by)) % n_m) for i in range(n_m)]
        return lax.ppermute(v, "mem", [(i, i ^ 1) for i in range(n_m)] if swap else to)

    block = n_obs // (n_x * n_y)
    tile = tile_x * n_y + tile_y
    target = (obs_value[:, None] + obs_error[:, None] * perturbation).T
    target = lax.dynamic_update_slice(jnp.zeros((8, n_obs), F32), target, (0, tile * block))
    per_row = 128 // block
    error = lax.dynamic_update_slice(
        jnp.zeros((n_obs // 128, 128), F32), obs_error[None],
        (tile // per_row, tile % per_row * block),
    )
    line = jnp.concatenate([picked, target, error], axis=1)
    a, b = send(rounded, 1), send(rounded, -1)
    own_far = send(rounded, 0, True)
    for axis, n in (("ty", n_y), ("tx", n_x)):
        bit = 1
        while bit < n:
            line = line + lax.ppermute(line, axis, [(i, i ^ bit) for i in range(n)])
            if bit == 1 and axis == "ty":
                line, own_far = lax.optimization_barrier((line, own_far))
            bit *= 2
    observed, target, error = (
        line[:, 0:n_obs], line[:, n_obs : 2 * n_obs], line[:, 2 * n_obs :]
    )
    observed, a, b = lax.optimization_barrier((observed, a, b))
    half = size_x // 2
    c0, c1 = send(a[:half], 1), send(b[half:], -1)
    parts = [send(observed, by) for by in (1, -1, 2)]
    near = jnp.concatenate([observed] + parts)
    far = send(near, 0, True)
    far, a, b = lax.optimization_barrier((far, a, b))
    a_far, b_far = send(a, 0, True), send(b, 0, True)
    w_first, w_last = solve_weights(near, far, target, error)
    begun = begin(w_first, [rounded, a, b, own_far, a_far, b_far], forecast)
    return update(w_last, [c0, c1, send(c0, 0, True), send(c1, 0, True)], begun)


def solution(mesh):
    placed = (
        P("mem", "tx", "ty"),
        P("tx", "ty"),
        P("tx", "ty"),
        P("mem", "tx", "ty"),
        P(),
        P(("tx", "ty")),
        P(("tx", "ty")),
        P(("tx", "ty"), "mem"),
    )
    return jax.shard_map(
        local, mesh=mesh, in_specs=placed, out_specs=P("mem", "tx", "ty"), check_vma=False
    )
```

```python
import functools

import jax
import jax.numpy as jnp
from jax import lax
from jax.experimental import pallas as pl
from jax.experimental.pallas import tpu as pltpu
from jax.sharding import PartitionSpec as P

SUBSTEPS = 4
W = SUBSTEPS
GROUP = 128 // W
F32 = jnp.float32
BF16 = jnp.bfloat16
VMEM_SPEC = pl.BlockSpec(memory_space=pltpu.VMEM)
HBM_SPEC = pl.BlockSpec(memory_space=pltpu.HBM)


def lanes():
    return lax.broadcasted_iota(jnp.int32, (8, 128), 1)


def sublanes():
    return lax.broadcasted_iota(jnp.int32, (8, 128), 0)


def wide(row):
    return jnp.broadcast_to(row, (8, 128))


def ends_kernel(
    obs_ref, p_ref, w_ref, e_ref, k_ref, top_ref, bottom_ref, code_ref, inside_ref,
    cubes, sems,
):
    _, size_x, size_y = p_ref.shape
    copies = []
    for i, lo in enumerate((0, size_x - 8)):
        for j, ref in enumerate((p_ref, w_ref)):
            copies.append((ref.at[:, pl.ds(lo, 8), :], cubes.at[2 * i + j]))
    copies = [pltpu.make_async_copy(a, b, sems.at[n]) for n, (a, b) in enumerate(copies)]
    for c in copies:
        c.start()
    bits_x, bits_y = size_x.bit_length() - 1, size_y.bit_length() - 1
    total_y = size_y * lax.axis_size("ty")
    obs = obs_ref[...]
    x = lax.shift_right_logical(obs, total_y.bit_length() - 1)
    y = obs & (total_y - 1)
    mine = (lax.shift_right_logical(x, bits_x) == lax.axis_index("tx")) & (
        lax.shift_right_logical(y, bits_y) == lax.axis_index("ty")
    )
    x, y = x & (size_x - 1), y & (size_y - 1)
    tile = x * (size_y // 128) + lax.shift_right_logical(y, 7)
    code_ref[...] = tile * 128 + ((lanes() - y) & 127)
    inside_ref[...] = jnp.where(mine, F32(1), F32(0))
    for c in copies:
        c.wait()
    sub = lax.broadcasted_iota(jnp.int32, (8, size_y), 0)
    for i, out in enumerate((top_ref, bottom_ref)):
        for j in range(2):
            turned = jnp.swapaxes(cubes[2 * i + j], 0, 1)
            for r in range(W):
                out[j * W + r] = turned[r if i == 0 else 8 - W + r]
        lo = (0, size_x - 8)[i]
        e, k = e_ref[lo : lo + 8, :], k_ref[lo : lo + 8, :]
        if i == 0:
            k = pltpu.roll(k, 4, 0)
        else:
            e = pltpu.roll(e, 4, 0)
        out[2 * W] = jnp.where(sub < 4, e, k)


def ends(obs, p, w, e, k):
    members, _, size_y = p.shape
    edge = jax.ShapeDtypeStruct((2 * W + 1, members, size_y), F32)
    return pl.pallas_call(
        ends_kernel,
        in_specs=[VMEM_SPEC] + [HBM_SPEC] * 2 + [VMEM_SPEC] * 2,
        out_specs=[VMEM_SPEC] * 4,
        out_shape=[
            edge, edge, jax.ShapeDtypeStruct(obs.shape, jnp.int32),
            jax.ShapeDtypeStruct(obs.shape, F32),
        ],
        scratch_shapes=[
            pltpu.VMEM((4, members, 8, size_y), F32),
            pltpu.SemaphoreType.DMA((4,)),
        ],
        compiler_params=pltpu.CompilerParams(vmem_limit_bytes=56 * 2**20),
        name="ends",
    )(obs, p, w, e, k)


def pack_rows(rows):
    slot = lanes() // W
    left = jnp.zeros((8, 128), F32)
    right = jnp.zeros((8, 128), F32)
    for r, a, b in rows:
        if r:
            a = pltpu.roll(a, W * r, 1)
            b = pltpu.roll(b, W * r, 1)
        left = jnp.where(slot == r, a, left)
        right = jnp.where(slot == (r - 1) % GROUP, b, right)
    return left, right


def turn_kernel(
    p_in, w_in, e_ref, k_ref, pt_out, wt_out, left_ref, right_ref,
    p_ref, w_ref, pt_ref, wt_ref, in_sems, out_sems,
):
    groups = left_ref.shape[0]

    def rows_of(g):
        return pl.ds(pl.multiple_of(g * GROUP, GROUP), GROUP)

    def fetch(g, f):
        src, dst = ((p_in, p_ref), (w_in, w_ref))[f]
        at = rows_of(g)
        return pltpu.make_async_copy(src.at[:, at, :], dst.at[:, at, :], in_sems.at[f, g])

    def leave(g, f):
        src, dst = ((pt_ref, pt_out), (wt_ref, wt_out))[f]
        at = rows_of(g)
        return pltpu.make_async_copy(src.at[at], dst.at[at], out_sems.at[f, g])

    for g in range(groups):
        for f in range(2):
            fetch(g, f).start()

    def group(g, _):
        at = rows_of(g)
        for f, (src, dst) in enumerate(((p_ref, pt_ref), (w_ref, wt_ref))):
            fetch(g, f).wait()
            rows = jnp.swapaxes(src[:, at, :] * F32(0.5), 0, 1)
            dst[at] = rows
            left_ref[g, f], right_ref[g, f] = pack_rows(
                (r, rows[r, :, 0:128], rows[r, :, 128:256]) for r in range(GROUP)
            )
            leave(g, f).start()
        fields = []
        for base, ref, factor in ((0, e_ref, 0.5), (4, k_ref, 0.25)):
            block = ref[at, :] * F32(factor)
            for q in range(GROUP // 8):
                part = block[8 * q : 8 * q + 8]
                fields.append((base + q, part[:, 0:128], part[:, 128:256]))
        left_ref[g, 2], right_ref[g, 2] = pack_rows(fields)
        return 0

    lax.fori_loop(0, groups, group, 0)
    for g in range(groups):
        for f in range(2):
            leave(g, f).wait()


def turn(p, w, e, k):
    members, size_x, size_y = p.shape
    groups = size_x // GROUP
    turned = (size_x, members, size_y)
    return pl.pallas_call(
        turn_kernel,
        in_specs=[HBM_SPEC] * 2 + [VMEM_SPEC] * 2,
        out_specs=[HBM_SPEC] * 2 + [VMEM_SPEC] * 2,
        out_shape=[jax.ShapeDtypeStruct(turned, F32)] * 2
        + [jax.ShapeDtypeStruct((groups, 3, 8, 128), F32)] * 2,
        scratch_shapes=[pltpu.VMEM(p.shape, F32)] * 2 + [pltpu.VMEM(turned, F32)] * 2
        + [pltpu.SemaphoreType.DMA((2, groups))] * 2,
        cost_estimate=pl.CostEstimate(flops=10**7, bytes_accessed=9 * 2**20, transcendentals=0),
        compiler_params=pltpu.CompilerParams(vmem_limit_bytes=52 * 2**20),
        name="turn",
    )(p, w, e, k)


def rows_kernel(
    up_ref, down_ref, top_ref, bottom_ref, left_in, right_in, above_ref, below_ref,
    left_ref, right_ref,
):
    tile, groups = lax.axis_index("tx"), left_in.shape[0]
    first, last = tile == 0, tile == lax.axis_size("tx") - 1
    left_ref[0:groups] = left_in[...]
    right_ref[0:groups] = right_in[...]
    sub = lax.broadcasted_iota(jnp.int32, (8, 256), 0)

    def mirrored(block):
        out = block
        for i in range(4):
            for base in (0, 4):
                row = block[base + 3 - i : base + 4 - i, :]
                out = jnp.where(sub == base + i, jnp.broadcast_to(row, (8, 256)), out)
        return out

    for flag, got, own, out in (
        (first, up_ref, top_ref, above_ref),
        (last, down_ref, bottom_ref, below_ref),
    ):
        for f in range(2):
            for i in range(W):
                row = jnp.where(flag, own[f * W + W - 1 - i], got[f * W + i])
                out[f * W + i] = row * F32(0.5)
        block = jnp.where(flag, mirrored(own[2 * W]), got[2 * W])
        out[2 * W] = block * jnp.where(sub < 4, F32(0.5), F32(0.25))
    for f in range(2):
        left_ref[groups, f], right_ref[groups, f] = pack_rows(
            (half * W + i, out[f * W + i, :, 0:128], out[f * W + i, :, 128:256])
            for half, out in enumerate((above_ref, below_ref))
            for i in range(W)
        )
    above, below = above_ref[2 * W], below_ref[2 * W]
    e = jnp.where(sub < 4, above, pltpu.roll(below, 4, 0))
    k = jnp.where(sub < 4, pltpu.roll(above, 4, 0), below)
    left_ref[groups, 2], right_ref[groups, 2] = pack_rows(
        (slot, v[:, 0:128], v[:, 128:256]) for slot, v in ((0, e), (4, k))
    )


def halo_rows(up, down, top, bottom, left, right):
    packs = jax.ShapeDtypeStruct((left.shape[0] + 1, *left.shape[1:]), F32)
    return pl.pallas_call(
        rows_kernel,
        in_specs=[VMEM_SPEC] * 6,
        out_specs=[VMEM_SPEC] * 4,
        out_shape=[jax.ShapeDtypeStruct(up.shape, F32)] * 2 + [packs] * 2,
        compiler_params=pltpu.CompilerParams(vmem_limit_bytes=4 * 2**20),
        name="rows",
    )(up, down, top, bottom, left, right)


def steps_kernel(
    pt_in, wt_in, e_ref, k_ref, above_ref, below_ref, fl_ref, fr_ref,
    out_ref, round_ref,
    p0, p1, w_s, fy_s, sum_s, fy2_s, sum2_s, e_s, er_s, k_s, kr_s, sems,
):
    size_x = pt_in.shape[0]
    lane = lanes()
    is_first, is_last = lane == 0, lane == 127
    groups = size_x // GROUP
    blocks = size_x // 8 + 2
    inner = (pl.ds(9, size_x), slice(None), pl.ds(0, 256))
    loads = [
        pltpu.make_async_copy(src, dst.at[inner], sems.at[i])
        for i, (src, dst) in enumerate(((pt_in, p0), (wt_in, w_s)))
    ]
    for c in loads:
        c.start()

    def halo(g, f, r):
        a, b = fr_ref[g, f], fl_ref[g, f]
        if r:
            a = pltpu.roll(a, 128 - W * r, 1)
            b = pltpu.roll(b, 128 - W * r, 1)
        return jnp.where(lane < 64, a, b)

    def spread(at, v, here, shifted):
        rolled = [pltpu.roll(u, 127, 1) for u in v]
        for t in range(3):
            here[at, :, 128 * t : 128 * t + 128] = v[t]
            shifted[at, :, 128 * t : 128 * t + 128] = jnp.where(
                is_last, rolled[(t + 1) % 3], rolled[t]
            )

    def unpack_group(g, _):
        for r in range(GROUP):
            for f, dst in ((0, p0), (1, w_s)):
                dst[g * GROUP + r + 9, :, 256:384] = halo(g, f, r)
        for q in range(GROUP // 8):
            rows = pl.ds(pl.multiple_of(g * GROUP + 8 * q, 8), 8)
            for base, ref, factor, here, shifted in (
                (0, e_ref, 0.5, e_s, er_s), (4, k_ref, 0.25, k_s, kr_s),
            ):
                v = [ref[rows, 128 * t : 128 * t + 128] * F32(factor) for t in range(2)]
                spread(g * (GROUP // 8) + q + 1, v + [halo(g, 2, base + q)], here, shifted)
        return 0

    lax.fori_loop(0, groups, unpack_group, 0)
    for r in range(2 * W):
        ref, y = (above_ref, 4 + r) if r < W else (below_ref, size_x + 4 + r)
        for f, dst in ((0, p0), (1, w_s)):
            dst[y + 1, :, 0:256] = ref[f * W + r % W]
            dst[y + 1, :, 256:384] = halo(groups, f, r)
    for base, here, shifted in ((0, e_s, er_s), (4, k_s, kr_s)):
        edge = pltpu.roll(halo(groups, 2, base), 4, 0)
        for at, ref, up in ((0, above_ref, base == 0), (blocks - 1, below_ref, base == 4)):
            v = ref[2 * W]
            v = pltpu.roll(v, 4, 0) if up else v
            spread(at, [v[:, 0:128], v[:, 128:256], edge], here, shifted)

    one, none = F32(1), F32(0)

    tile = lax.axis_index("ty")

    def edge_mask(at):
        return jnp.where(is_last & (jnp.broadcast_to(tile, (8, 128)) == at), none, one)

    mask_right, mask_left = edge_mask(lax.axis_size("ty") - 1), edge_mask(0)
    for c in loads:
        c.wait()

    def tiles(ref, at):
        return [ref[at, :, 128 * t : 128 * t + 128] for t in range(3)]

    def put(ref, at, v):
        for t in range(3):
            ref[at, :, 128 * t : 128 * t + 128] = v[t]

    def row_of(ref, b, u):
        return [wide(ref[b, u : u + 1, 128 * t : 128 * t + 128]) for t in range(3)]

    def finish(dst, at, sums, fluxes):
        for u in range(8):
            fy = tiles(fluxes, u)
            fr = [pltpu.roll(v, 1, 1) for v in fy]
            s = tiles(sums, u)
            back = [jnp.where(is_first, fr[(t - 1) % 3], fr[t]) for t in range(3)]
            put(dst, at * 8 + u, [s[t] + (fy[t] - back[t]) for t in range(3)])

    def fluxes_of(src, at, sums, fluxes, carry):
        p_old, h_old, c_old, fx_old, fy_old = carry
        for u in range(8):
            p = tiles(src, at * 8 + u + 1)
            raw = [pltpu.roll(v, 127, 1) for v in p]
            pr = [jnp.where(is_last, raw[(t + 1) % 3], raw[t]) for t in range(3)]
            e, er = row_of(e_s, at, u), row_of(er_s, at, u)
            k, kr = row_of(k_s, at, u), row_of(kr_s, at, u)
            w = tiles(w_s, at * 8 + u)
            h = [p[t] + e[t] for t in range(3)]
            c = [k[t] * jnp.tanh(p[t]) + k[t] for t in range(3)]
            fy = [
                (c[t] + (kr[t] * jnp.tanh(pr[t]) + kr[t])) * ((pr[t] + er[t]) - h[t])
                for t in range(3)
            ]
            fy[1] = fy[1] * mask_right
            fy[2] = fy[2] * mask_left
            fx = [(c_old[t] + c[t]) * (h[t] - h_old[t]) for t in range(3)]
            put(sums, u, [(p_old[t] + w[t]) + (fx[t] - fx_old[t]) for t in range(3)])
            put(fluxes, u, fy_old)
            p_old, h_old, c_old, fx_old, fy_old = p, h, c, fx, fy
        return p_old, h_old, c_old, fx_old, fy_old

    def step(src, dst):
        def body(i, carry):
            carry = fluxes_of(src, 2 * i, sum_s, fy_s, carry)
            finish(dst, jnp.maximum(2 * i - 1, 0), sum2_s, fy2_s)
            carry = fluxes_of(src, 2 * i + 1, sum2_s, fy2_s, carry)
            finish(dst, 2 * i, sum_s, fy_s)
            return carry

        zero = [jnp.zeros((8, 128), F32)] * 3
        lax.fori_loop(0, blocks // 2, body, (zero,) * 5)
        finish(dst, blocks - 1, sum2_s, fy2_s)

    for s in range(SUBSTEPS):
        step(*((p0, p1) if s % 2 == 0 else (p1, p0)))
    last = p0 if SUBSTEPS % 2 == 0 else p1

    def leave(i, _):
        x = pl.multiple_of(i * 8, 8)
        for u in range(8):
            row = last[x + 9 + u, :, 0:256] * F32(2)
            out_ref[2 * x + 2 * u] = row[:, 0:128]
            out_ref[2 * x + 2 * u + 1] = row[:, 128:256]
            round_ref[x + u] = row.astype(BF16)
        return 0

    lax.fori_loop(0, size_x // 8, leave, 0)


def run_steps(pt, wt, e, k, above, below, from_left, from_right):
    size_x, members, size_y = pt.shape
    tile = pltpu.VMEM((size_x + 17, members, size_y + 128), F32)
    flat = pltpu.VMEM((size_x // 8 + 2, 8, size_y + 128), F32)
    few = pltpu.VMEM((8, members, size_y + 128), F32)
    return pl.pallas_call(
        steps_kernel,
        in_specs=[HBM_SPEC] * 2 + [VMEM_SPEC] * 6,
        out_specs=[VMEM_SPEC] * 2,
        scratch_shapes=[tile] * 3 + [few] * 4 + [flat] * 4 + [pltpu.SemaphoreType.DMA((2,))],
        out_shape=[
            jax.ShapeDtypeStruct((size_x * (size_y // 128), members, 128), F32),
            jax.ShapeDtypeStruct((size_x, members, size_y), BF16),
        ],
        compiler_params=pltpu.CompilerParams(vmem_limit_bytes=50 * 2**20),
        name="steps",
    )(pt, wt, e, k, above, below, from_left, from_right)


def pick_kernel(code_ref, f_ref, inside_ref, pick_ref):
    lane = lanes()

    def pick(g, _):
        acc = jnp.zeros((8, 128), F32)
        for u in range(128):
            code = code_ref[g, u]
            v = pltpu.roll(f_ref[lax.shift_right_logical(code, 7)], code, 1)
            acc = jnp.where(lane == u, v, acc)
        keep = wide(inside_ref[pl.ds(g, 1), :]) > F32(0.5)
        pick_ref[:, pl.ds(pl.multiple_of(g * 128, 128), 128)] = jnp.where(keep, acc, F32(0))
        return 0

    lax.fori_loop(0, code_ref.shape[0], pick, 0)


def picks(code, forecast, inside):
    return pl.pallas_call(
        pick_kernel,
        grid_spec=pltpu.PrefetchScalarGridSpec(
            num_scalar_prefetch=1, grid=(), in_specs=[VMEM_SPEC] * 2, out_specs=VMEM_SPEC
        ),
        out_shape=jax.ShapeDtypeStruct((8, code.size), F32),
        compiler_params=pltpu.CompilerParams(vmem_limit_bytes=8 * 2**20),
        name="picks",
    )(code, forecast, inside)


def weights_kernel(near_ref, far_ref, target_ref, error_ref, first_ref, last_ref, x_s, m_s):
    half = near_ref.shape[0]
    members = 2 * half
    blocks = members // 8
    parts = [r[8 * b : 8 * b + 8, :] for r in (near_ref, far_ref) for b in range(half // 8)]
    total = parts[0]
    for part in parts[1:]:
        total = total + part
    mean = jnp.sum(total, axis=0, keepdims=True) * F32(1.0 / members)
    error = jnp.concatenate([error_ref[r : r + 1, :] for r in range(error_ref.shape[0])], axis=1)
    inverse = F32(1) / error
    for b, part in enumerate(parts):
        x_s[8 * b : 8 * b + 8, :] = (part - mean) * inverse
    innovation = (target_ref[...] - parts[0]) * inverse
    x = x_s[...]
    dims = (((1,), (1,)), ((), ()))
    dot = functools.partial(
        lax.dot_general, dimension_numbers=dims, precision=lax.Precision.HIGHEST,
        preferred_element_type=F32,
    )
    r = lax.broadcasted_iota(jnp.int32, (members, members), 0)
    c = lax.broadcasted_iota(jnp.int32, (members, members), 1)
    m_s[:, 0:members] = dot(x, x) + jnp.where(r == c, F32(members - 1), F32(0))
    m_s[:, members : 2 * members] = jnp.zeros((members, members), F32)
    m_s[:, members : members + 8] = dot(x, innovation)
    m = [m_s[8 * b : 8 * b + 8, :] for b in range(blocks)]
    sub = sublanes()
    for kb in range(blocks):
        cols = [
            [jnp.broadcast_to(m[b][:, 8 * kb + j : 8 * kb + j + 1], (8, 128)) for j in range(8)]
            for b in range(blocks)
        ]
        rows = m[kb]
        piv = list(cols[kb])
        for j in range(8):
            inv = F32(1) / wide(piv[j][j : j + 1])
            here = sub == j
            factor = piv[j]
            top = wide(rows[j : j + 1]) * inv
            rows = jnp.where(here, top, rows - factor * top)
            for q in range(j + 1, 8):
                top = wide(piv[q][j : j + 1]) * inv
                piv[q] = jnp.where(here, top, piv[q] - factor * top)
        spread = [wide(rows[j : j + 1]) for j in range(8)]
        for b in range(blocks):
            if b == kb:
                m[b] = rows
            else:
                acc = cols[b][0] * spread[0]
                for j in range(1, 8):
                    acc = acc + cols[b][j] * spread[j]
                m[b] = m[b] - acc
    for b in range(blocks):
        m_s[8 * b : 8 * b + 8, :] = m[b]
    turned = jnp.transpose(m_s[...], (1, 0))
    turned = turned[members : members + 8, :]
    for h in range(2):
        at = h * half
        first_ref[:, h * (half - 8) : (h + 1) * (half - 8)] = turned[:, at : at + half - 8]
        last_ref[:, 8 * h : 8 * h + 8] = turned[:, at + half - 8 : at + half]


def solve_weights(near, far, target, error):
    half, n_obs = near.shape
    members = 2 * half
    return pl.pallas_call(
        weights_kernel,
        in_specs=[VMEM_SPEC] * 4,
        out_specs=[VMEM_SPEC] * 2,
        scratch_shapes=[
            pltpu.VMEM((members, n_obs), F32),
            pltpu.VMEM((members, 2 * members), F32),
        ],
        out_shape=[
            jax.ShapeDtypeStruct((8, members - 16), F32), jax.ShapeDtypeStruct((8, 16), F32),
        ],
        compiler_params=pltpu.CompilerParams(vmem_limit_bytes=4 * 2**20),
        name="weights",
    )(near, far, target, error)


def shifted(w, pieces, f_ref, x, to):
    rows = jnp.concatenate([v[x].astype(F32) for v in pieces], axis=0).astype(BF16)
    shift = jnp.dot(w, rows, preferred_element_type=F32)
    return [f_ref[2 * to + t] + shift[:, 128 * t : 128 * t + 128] for t in range(2)]


def begin_kernel(w_ref, *refs):
    pieces, (f_ref, out_ref) = refs[:-2], refs[-2:]
    w = w_ref[...].astype(BF16)

    def chunk(g, _):
        for r in range(16):
            x = g * 16 + r
            for t, v in enumerate(shifted(w, pieces, f_ref, x, x)):
                out_ref[2 * x + t] = v
        return 0

    lax.fori_loop(0, pieces[0].shape[0] // 16, chunk, 0)


def update_kernel(w_ref, *refs):
    pieces, (f_ref, out_ref, row_s, done_s, sems) = refs[:-5], refs[-5:]
    step = row_s.shape[0]
    w = w_ref[...].astype(BF16)

    def leave(g):
        at = pl.ds(pl.multiple_of(g * step, step), step)
        return pltpu.make_async_copy(done_s.at[:, at, :], out_ref.at[:, at, :], sems.at[g])

    count = pieces[0].shape[0] // step

    def chunk(half, i, _):
        g = half * count + i
        for r in range(step):
            at = (i * step + r, g * step + r)
            for t, v in enumerate(shifted(w, pieces[half::2], f_ref, *at)):
                row_s[r, :, 128 * t : 128 * t + 128] = v
        at = pl.ds(pl.multiple_of(g * step, step), step)
        done_s[:, at, :] = jnp.swapaxes(row_s[...], 0, 1)
        leave(g).start()
        return 0

    for half in range(2):
        lax.fori_loop(0, count, functools.partial(chunk, half), 0)
    for g in range(2 * count):
        leave(g).wait()


def begin(weights, pieces, forecast):
    return pl.pallas_call(
        begin_kernel,
        in_specs=[VMEM_SPEC] * (len(pieces) + 2),
        out_specs=VMEM_SPEC,
        out_shape=jax.ShapeDtypeStruct(forecast.shape, F32),
        compiler_params=pltpu.CompilerParams(vmem_limit_bytes=12 * 2**20),
        name="begin",
    )(weights, *pieces, forecast)


def update(weights, pieces, forecast):
    rows, members, size_y = pieces[0].shape
    size_x = 2 * rows
    step = 32
    whole = (members, size_x, size_y)
    return pl.pallas_call(
        update_kernel,
        in_specs=[VMEM_SPEC] * (len(pieces) + 2),
        out_specs=HBM_SPEC,
        out_shape=jax.ShapeDtypeStruct(whole, F32),
        scratch_shapes=[
            pltpu.VMEM((step, members, size_y), F32),
            pltpu.VMEM(whole, F32),
            pltpu.SemaphoreType.DMA((size_x // step,)),
        ],
        compiler_params=pltpu.CompilerParams(vmem_limit_bytes=8 * 2**20),
        name="update",
    )(weights, *pieces, forecast)


def local(pressure, elevation, ks_field, melt_rate, obs_index, obs_value, obs_error, perturbation):
    _, size_x, _ = pressure.shape
    n_x, n_y, n_m = (lax.axis_size(a) for a in ("tx", "ty", "mem"))
    tile_x, tile_y = lax.axis_index("tx"), lax.axis_index("ty")

    def ring(n, by):
        return [(i, (i + by) % n) for i in range(n)]

    n_obs = obs_index.shape[0]
    top, bottom, code, inside = ends(
        obs_index.reshape(n_obs // 128, 128), pressure, melt_rate, elevation, ks_field
    )
    up = lax.ppermute(bottom, "tx", ring(n_x, 1))
    down = lax.ppermute(top, "tx", ring(n_x, -1))
    pt, wt, left, right = turn(pressure, melt_rate, elevation, ks_field)
    above, below, left, right = halo_rows(up, down, top, bottom, left, right)
    from_left = lax.ppermute(right, "ty", ring(n_y, 1))
    from_right = lax.ppermute(left, "ty", ring(n_y, -1))
    forecast, rounded = run_steps(
        pt, wt, elevation, ks_field, above, below, from_left, from_right
    )
    picked = picks(code, forecast, inside)

    def send(v, by, swap=False):
        to = [(i, (i + 2 * (by if i % 2 == 0 else -by)) % n_m) for i in range(n_m)]
        return lax.ppermute(v, "mem", [(i, i ^ 1) for i in range(n_m)] if swap else to)

    block = n_obs // (n_x * n_y)
    tile = tile_x * n_y + tile_y
    target = (obs_value[:, None] + obs_error[:, None] * perturbation).T
    target = lax.dynamic_update_slice(jnp.zeros((8, n_obs), F32), target, (0, tile * block))
    per_row = 128 // block
    error = lax.dynamic_update_slice(
        jnp.zeros((n_obs // 128, 128), F32), obs_error[None],
        (tile // per_row, tile % per_row * block),
    )
    line = jnp.concatenate([picked, target, error], axis=1)
    a, b = send(rounded, 1), send(rounded, -1)
    own_far = send(rounded, 0, True)
    for axis, n in (("ty", n_y), ("tx", n_x)):
        span = 2
        while span <= n:
            line = line + lax.ppermute(line, axis, [(i, i ^ (span - 1)) for i in range(n)])
            if span == 2 and axis == "ty":
                line, own_far = lax.optimization_barrier((line, own_far))
            span *= 2
    observed, target, error = (
        line[:, 0:n_obs], line[:, n_obs : 2 * n_obs], line[:, 2 * n_obs :]
    )
    observed, a, b = lax.optimization_barrier((observed, a, b))
    half = size_x // 2
    c0, c1 = send(a[:half], 1), send(b[half:], -1)
    parts = [send(observed, by) for by in (1, -1, 2)]
    near = jnp.concatenate([observed] + parts)
    far = send(near, 0, True)
    far, a, b = lax.optimization_barrier((far, a, b))
    a_far, b_far = send(a, 0, True), send(b, 0, True)
    w_first, w_last = solve_weights(near, far, target, error)
    begun = begin(w_first, [rounded, a, b, own_far, a_far, b_far], forecast)
    return update(w_last, [c0, c1, send(c0, 0, True), send(c1, 0, True)], begun)


def solution(mesh):
    placed = (
        P("mem", "tx", "ty"),
        P("tx", "ty"),
        P("tx", "ty"),
        P("mem", "tx", "ty"),
        P(),
        P(("tx", "ty")),
        P(("tx", "ty")),
        P(("tx", "ty"), "mem"),
    )
    return jax.shard_map(
        local, mesh=mesh, in_specs=placed, out_specs=P("mem", "tx", "ty"), check_vma=False
    )
```

```python
import functools

import jax
import jax.numpy as jnp
from jax import lax
from jax.experimental import pallas as pl
from jax.experimental.pallas import tpu as pltpu
from jax.sharding import PartitionSpec as P

SUBSTEPS = 4
W = SUBSTEPS
GROUP = 128 // W
F32 = jnp.float32
BF16 = jnp.bfloat16
VMEM_SPEC = pl.BlockSpec(memory_space=pltpu.VMEM)
HBM_SPEC = pl.BlockSpec(memory_space=pltpu.HBM)


def lanes():
    return lax.broadcasted_iota(jnp.int32, (8, 128), 1)


def sublanes():
    return lax.broadcasted_iota(jnp.int32, (8, 128), 0)


def wide(row):
    return jnp.broadcast_to(row, (8, 128))


def ends_kernel(
    obs_ref, p_ref, w_ref, e_ref, k_ref, top_ref, bottom_ref, code_ref, inside_ref,
    cubes, sems,
):
    _, size_x, size_y = p_ref.shape
    copies = []
    for i, lo in enumerate((0, size_x - 8)):
        for j, ref in enumerate((p_ref, w_ref)):
            copies.append((ref.at[:, pl.ds(lo, 8), :], cubes.at[2 * i + j]))
    copies = [pltpu.make_async_copy(a, b, sems.at[n]) for n, (a, b) in enumerate(copies)]
    for c in copies:
        c.start()
    bits_x, bits_y = size_x.bit_length() - 1, size_y.bit_length() - 1
    total_y = size_y * lax.axis_size("ty")
    obs = obs_ref[...]
    x = lax.shift_right_logical(obs, total_y.bit_length() - 1)
    y = obs & (total_y - 1)
    mine = (lax.shift_right_logical(x, bits_x) == lax.axis_index("tx")) & (
        lax.shift_right_logical(y, bits_y) == lax.axis_index("ty")
    )
    x, y = x & (size_x - 1), y & (size_y - 1)
    tile = x * (size_y // 128) + lax.shift_right_logical(y, 7)
    code_ref[...] = tile * 128 + ((lanes() - y) & 127)
    inside_ref[...] = jnp.where(mine, F32(1), F32(0))
    for c in copies:
        c.wait()
    sub = lax.broadcasted_iota(jnp.int32, (8, size_y), 0)
    for i, out in enumerate((top_ref, bottom_ref)):
        for j in range(2):
            turned = jnp.swapaxes(cubes[2 * i + j], 0, 1)
            for r in range(W):
                out[j * W + r] = turned[r if i == 0 else 8 - W + r]
        lo = (0, size_x - 8)[i]
        e, k = e_ref[lo : lo + 8, :], k_ref[lo : lo + 8, :]
        if i == 0:
            k = pltpu.roll(k, 4, 0)
        else:
            e = pltpu.roll(e, 4, 0)
        out[2 * W] = jnp.where(sub < 4, e, k)


def ends(obs, p, w, e, k):
    members, _, size_y = p.shape
    edge = jax.ShapeDtypeStruct((2 * W + 1, members, size_y), F32)
    return pl.pallas_call(
        ends_kernel,
        in_specs=[VMEM_SPEC] + [HBM_SPEC] * 2 + [VMEM_SPEC] * 2,
        out_specs=[VMEM_SPEC] * 4,
        out_shape=[
            edge, edge, jax.ShapeDtypeStruct(obs.shape, jnp.int32),
            jax.ShapeDtypeStruct(obs.shape, F32),
        ],
        scratch_shapes=[
            pltpu.VMEM((4, members, 8, size_y), F32),
            pltpu.SemaphoreType.DMA((4,)),
        ],
        compiler_params=pltpu.CompilerParams(vmem_limit_bytes=56 * 2**20),
        name="ends",
    )(obs, p, w, e, k)


def pack_rows(rows):
    slot = lanes() // W
    left = jnp.zeros((8, 128), F32)
    right = jnp.zeros((8, 128), F32)
    for r, a, b in rows:
        if r:
            a = pltpu.roll(a, W * r, 1)
            b = pltpu.roll(b, W * r, 1)
        left = jnp.where(slot == r, a, left)
        right = jnp.where(slot == (r - 1) % GROUP, b, right)
    return left, right


def turn_kernel(
    p_in, w_in, e_ref, k_ref, pt_out, wt_out, left_ref, right_ref,
    p_ref, w_ref, pt_ref, wt_ref, in_sems, out_sems,
):
    groups = left_ref.shape[0]

    def rows_of(g):
        return pl.ds(pl.multiple_of(g * GROUP, GROUP), GROUP)

    def fetch(g, f):
        src, dst = ((p_in, p_ref), (w_in, w_ref))[f]
        at = rows_of(g)
        return pltpu.make_async_copy(src.at[:, at, :], dst.at[:, at, :], in_sems.at[f, g])

    def leave(g, f):
        src, dst = ((pt_ref, pt_out), (wt_ref, wt_out))[f]
        at = rows_of(g)
        return pltpu.make_async_copy(src.at[at], dst.at[at], out_sems.at[f, g])

    for g in range(groups):
        for f in range(2):
            fetch(g, f).start()

    def group(g, _):
        at = rows_of(g)
        for f, (src, dst) in enumerate(((p_ref, pt_ref), (w_ref, wt_ref))):
            fetch(g, f).wait()
            rows = jnp.swapaxes(src[:, at, :] * F32(0.5), 0, 1)
            dst[at] = rows
            left_ref[g, f], right_ref[g, f] = pack_rows(
                (r, rows[r, :, 0:128], rows[r, :, 128:256]) for r in range(GROUP)
            )
            leave(g, f).start()
        fields = []
        for base, ref, factor in ((0, e_ref, 0.5), (4, k_ref, 0.25)):
            block = ref[at, :] * F32(factor)
            for q in range(GROUP // 8):
                part = block[8 * q : 8 * q + 8]
                fields.append((base + q, part[:, 0:128], part[:, 128:256]))
        left_ref[g, 2], right_ref[g, 2] = pack_rows(fields)
        return 0

    lax.fori_loop(0, groups, group, 0)
    for g in range(groups):
        for f in range(2):
            leave(g, f).wait()


def turn(p, w, e, k):
    members, size_x, size_y = p.shape
    groups = size_x // GROUP
    turned = (size_x, members, size_y)
    return pl.pallas_call(
        turn_kernel,
        in_specs=[HBM_SPEC] * 2 + [VMEM_SPEC] * 2,
        out_specs=[HBM_SPEC] * 2 + [VMEM_SPEC] * 2,
        out_shape=[jax.ShapeDtypeStruct(turned, F32)] * 2
        + [jax.ShapeDtypeStruct((groups, 3, 8, 128), F32)] * 2,
        scratch_shapes=[pltpu.VMEM(p.shape, F32)] * 2 + [pltpu.VMEM(turned, F32)] * 2
        + [pltpu.SemaphoreType.DMA((2, groups))] * 2,
        cost_estimate=pl.CostEstimate(flops=10**7, bytes_accessed=9 * 2**20, transcendentals=0),
        compiler_params=pltpu.CompilerParams(vmem_limit_bytes=52 * 2**20),
        name="turn",
    )(p, w, e, k)


def rows_kernel(
    up_ref, down_ref, top_ref, bottom_ref, left_in, right_in, above_ref, below_ref,
    left_ref, right_ref,
):
    tile, groups = lax.axis_index("tx"), left_in.shape[0]
    first, last = tile == 0, tile == lax.axis_size("tx") - 1
    left_ref[0:groups] = left_in[...]
    right_ref[0:groups] = right_in[...]
    sub = lax.broadcasted_iota(jnp.int32, (8, 256), 0)

    def mirrored(block):
        out = block
        for i in range(4):
            for base in (0, 4):
                row = block[base + 3 - i : base + 4 - i, :]
                out = jnp.where(sub == base + i, jnp.broadcast_to(row, (8, 256)), out)
        return out

    for flag, got, own, out in (
        (first, up_ref, top_ref, above_ref),
        (last, down_ref, bottom_ref, below_ref),
    ):
        for f in range(2):
            for i in range(W):
                row = jnp.where(flag, own[f * W + W - 1 - i], got[f * W + i])
                out[f * W + i] = row * F32(0.5)
        block = jnp.where(flag, mirrored(own[2 * W]), got[2 * W])
        out[2 * W] = block * jnp.where(sub < 4, F32(0.5), F32(0.25))
    for f in range(2):
        left_ref[groups, f], right_ref[groups, f] = pack_rows(
            (half * W + i, out[f * W + i, :, 0:128], out[f * W + i, :, 128:256])
            for half, out in enumerate((above_ref, below_ref))
            for i in range(W)
        )
    above, below = above_ref[2 * W], below_ref[2 * W]
    e = jnp.where(sub < 4, above, pltpu.roll(below, 4, 0))
    k = jnp.where(sub < 4, pltpu.roll(above, 4, 0), below)
    left_ref[groups, 2], right_ref[groups, 2] = pack_rows(
        (slot, v[:, 0:128], v[:, 128:256]) for slot, v in ((0, e), (4, k))
    )


def halo_rows(up, down, top, bottom, left, right):
    packs = jax.ShapeDtypeStruct((left.shape[0] + 1, *left.shape[1:]), F32)
    return pl.pallas_call(
        rows_kernel,
        in_specs=[VMEM_SPEC] * 6,
        out_specs=[VMEM_SPEC] * 4,
        out_shape=[jax.ShapeDtypeStruct(up.shape, F32)] * 2 + [packs] * 2,
        compiler_params=pltpu.CompilerParams(vmem_limit_bytes=4 * 2**20),
        name="rows",
    )(up, down, top, bottom, left, right)


def steps_kernel(
    pt_in, wt_in, e_ref, k_ref, above_ref, below_ref, fl_ref, fr_ref,
    out_ref, round_ref,
    p0, p1, w_s, fy_s, sum_s, fy2_s, sum2_s, e_s, er_s, k_s, kr_s, sems,
):
    size_x = pt_in.shape[0]
    lane = lanes()
    is_first, is_last = lane == 0, lane == 127
    groups = size_x // GROUP
    blocks = size_x // 8 + 2
    inner = (pl.ds(9, size_x), slice(None), pl.ds(0, 256))
    loads = [
        pltpu.make_async_copy(src, dst.at[inner], sems.at[i])
        for i, (src, dst) in enumerate(((pt_in, p0), (wt_in, w_s)))
    ]
    for c in loads:
        c.start()

    def halo(g, f, r):
        a, b = fr_ref[g, f], fl_ref[g, f]
        if r:
            a = pltpu.roll(a, 128 - W * r, 1)
            b = pltpu.roll(b, 128 - W * r, 1)
        return jnp.where(lane < 64, a, b)

    def spread(at, v, here, shifted):
        rolled = [pltpu.roll(u, 127, 1) for u in v]
        for t in range(3):
            here[at, :, 128 * t : 128 * t + 128] = v[t]
            shifted[at, :, 128 * t : 128 * t + 128] = jnp.where(
                is_last, rolled[(t + 1) % 3], rolled[t]
            )

    def unpack_group(g, _):
        for r in range(GROUP):
            for f, dst in ((0, p0), (1, w_s)):
                dst[g * GROUP + r + 9, :, 256:384] = halo(g, f, r)
        for q in range(GROUP // 8):
            rows = pl.ds(pl.multiple_of(g * GROUP + 8 * q, 8), 8)
            for base, ref, factor, here, shifted in (
                (0, e_ref, 0.5, e_s, er_s), (4, k_ref, 0.25, k_s, kr_s),
            ):
                v = [ref[rows, 128 * t : 128 * t + 128] * F32(factor) for t in range(2)]
                spread(g * (GROUP // 8) + q + 1, v + [halo(g, 2, base + q)], here, shifted)
        return 0

    lax.fori_loop(0, groups, unpack_group, 0)
    for r in range(2 * W):
        ref, y = (above_ref, 4 + r) if r < W else (below_ref, size_x + 4 + r)
        for f, dst in ((0, p0), (1, w_s)):
            dst[y + 1, :, 0:256] = ref[f * W + r % W]
            dst[y + 1, :, 256:384] = halo(groups, f, r)
    for base, here, shifted in ((0, e_s, er_s), (4, k_s, kr_s)):
        edge = pltpu.roll(halo(groups, 2, base), 4, 0)
        for at, ref, up in ((0, above_ref, base == 0), (blocks - 1, below_ref, base == 4)):
            v = ref[2 * W]
            v = pltpu.roll(v, 4, 0) if up else v
            spread(at, [v[:, 0:128], v[:, 128:256], edge], here, shifted)

    one, none = F32(1), F32(0)

    tile = lax.axis_index("ty")

    def edge_mask(at):
        return jnp.where(is_last & (jnp.broadcast_to(tile, (8, 128)) == at), none, one)

    mask_right, mask_left = edge_mask(lax.axis_size("ty") - 1), edge_mask(0)
    for c in loads:
        c.wait()

    def tiles(ref, at):
        return [ref[at, :, 128 * t : 128 * t + 128] for t in range(3)]

    def put(ref, at, v):
        for t in range(3):
            ref[at, :, 128 * t : 128 * t + 128] = v[t]

    def row_of(ref, b, u):
        return [wide(ref[b, u : u + 1, 128 * t : 128 * t + 128]) for t in range(3)]

    def finish(dst, at, sums, fluxes):
        for u in range(8):
            fy = tiles(fluxes, u)
            fr = [pltpu.roll(v, 1, 1) for v in fy]
            s = tiles(sums, u)
            back = [jnp.where(is_first, fr[(t - 1) % 3], fr[t]) for t in range(3)]
            put(dst, at * 8 + u, [s[t] + (fy[t] - back[t]) for t in range(3)])

    def fluxes_of(src, at, sums, fluxes, carry):
        p_old, h_old, c_old, fx_old, fy_old = carry
        for u in range(8):
            p = tiles(src, at * 8 + u + 1)
            raw = [pltpu.roll(v, 127, 1) for v in p]
            pr = [jnp.where(is_last, raw[(t + 1) % 3], raw[t]) for t in range(3)]
            e, er = row_of(e_s, at, u), row_of(er_s, at, u)
            k, kr = row_of(k_s, at, u), row_of(kr_s, at, u)
            w = tiles(w_s, at * 8 + u)
            h = [p[t] + e[t] for t in range(3)]
            c = [k[t] * jnp.tanh(p[t]) + k[t] for t in range(3)]
            fy = [
                (c[t] + (kr[t] * jnp.tanh(pr[t]) + kr[t])) * ((pr[t] + er[t]) - h[t])
                for t in range(3)
            ]
            fy[1] = fy[1] * mask_right
            fy[2] = fy[2] * mask_left
            fx = [(c_old[t] + c[t]) * (h[t] - h_old[t]) for t in range(3)]
            put(sums, u, [(p_old[t] + w[t]) + (fx[t] - fx_old[t]) for t in range(3)])
            put(fluxes, u, fy_old)
            p_old, h_old, c_old, fx_old, fy_old = p, h, c, fx, fy
        return p_old, h_old, c_old, fx_old, fy_old

    def step(src, dst):
        def body(i, carry):
            carry = fluxes_of(src, 2 * i, sum_s, fy_s, carry)
            finish(dst, jnp.maximum(2 * i - 1, 0), sum2_s, fy2_s)
            carry = fluxes_of(src, 2 * i + 1, sum2_s, fy2_s, carry)
            finish(dst, 2 * i, sum_s, fy_s)
            return carry

        zero = [jnp.zeros((8, 128), F32)] * 3
        lax.fori_loop(0, blocks // 2, body, (zero,) * 5)
        finish(dst, blocks - 1, sum2_s, fy2_s)

    for s in range(SUBSTEPS):
        step(*((p0, p1) if s % 2 == 0 else (p1, p0)))
    last = p0 if SUBSTEPS % 2 == 0 else p1

    def leave(i, _):
        x = pl.multiple_of(i * 8, 8)
        for u in range(8):
            row = last[x + 9 + u, :, 0:256] * F32(2)
            out_ref[2 * x + 2 * u] = row[:, 0:128]
            out_ref[2 * x + 2 * u + 1] = row[:, 128:256]
            round_ref[x + u] = row.astype(BF16)
        return 0

    lax.fori_loop(0, size_x // 8, leave, 0)


def run_steps(pt, wt, e, k, above, below, from_left, from_right):
    size_x, members, size_y = pt.shape
    tile = pltpu.VMEM((size_x + 17, members, size_y + 128), F32)
    flat = pltpu.VMEM((size_x // 8 + 2, 8, size_y + 128), F32)
    few = pltpu.VMEM((8, members, size_y + 128), F32)
    return pl.pallas_call(
        steps_kernel,
        in_specs=[HBM_SPEC] * 2 + [VMEM_SPEC] * 6,
        out_specs=[VMEM_SPEC] * 2,
        scratch_shapes=[tile] * 3 + [few] * 4 + [flat] * 4 + [pltpu.SemaphoreType.DMA((2,))],
        out_shape=[
            jax.ShapeDtypeStruct((size_x * (size_y // 128), members, 128), F32),
            jax.ShapeDtypeStruct((size_x, members, size_y), BF16),
        ],
        compiler_params=pltpu.CompilerParams(vmem_limit_bytes=50 * 2**20),
        name="steps",
    )(pt, wt, e, k, above, below, from_left, from_right)


def pick_kernel(code_ref, f_ref, inside_ref, pick_ref):
    lane = lanes()

    def pick(g, _):
        acc = jnp.zeros((8, 128), F32)
        for u in range(128):
            code = code_ref[g, u]
            v = pltpu.roll(f_ref[lax.shift_right_logical(code, 7)], code, 1)
            acc = jnp.where(lane == u, v, acc)
        keep = wide(inside_ref[pl.ds(g, 1), :]) > F32(0.5)
        pick_ref[:, pl.ds(pl.multiple_of(g * 128, 128), 128)] = jnp.where(keep, acc, F32(0))
        return 0

    lax.fori_loop(0, code_ref.shape[0], pick, 0)


def picks(code, forecast, inside):
    return pl.pallas_call(
        pick_kernel,
        grid_spec=pltpu.PrefetchScalarGridSpec(
            num_scalar_prefetch=1, grid=(), in_specs=[VMEM_SPEC] * 2, out_specs=VMEM_SPEC
        ),
        out_shape=jax.ShapeDtypeStruct((8, code.size), F32),
        compiler_params=pltpu.CompilerParams(vmem_limit_bytes=8 * 2**20),
        name="picks",
    )(code, forecast, inside)


def weights_kernel(near_ref, far_ref, target_ref, error_ref, first_ref, last_ref, x_s, m_s):
    half = near_ref.shape[0]
    members = 2 * half
    blocks = members // 8
    parts = [r[8 * b : 8 * b + 8, :] for r in (near_ref, far_ref) for b in range(half // 8)]
    total = parts[0]
    for part in parts[1:]:
        total = total + part
    mean = jnp.sum(total, axis=0, keepdims=True) * F32(1.0 / members)
    error = jnp.concatenate([error_ref[r : r + 1, :] for r in range(error_ref.shape[0])], axis=1)
    inverse = F32(1) / error
    for b, part in enumerate(parts):
        x_s[8 * b : 8 * b + 8, :] = (part - mean) * inverse
    innovation = (target_ref[...] - parts[0]) * inverse
    x = x_s[...]
    dims = (((1,), (1,)), ((), ()))
    dot = functools.partial(
        lax.dot_general, dimension_numbers=dims, precision=lax.Precision.HIGHEST,
        preferred_element_type=F32,
    )
    r = lax.broadcasted_iota(jnp.int32, (members, members), 0)
    c = lax.broadcasted_iota(jnp.int32, (members, members), 1)
    m_s[:, 0:members] = dot(x, x) + jnp.where(r == c, F32(members - 1), F32(0))
    m_s[:, members : 2 * members] = jnp.zeros((members, members), F32)
    m_s[:, members : members + 8] = dot(x, innovation)
    m = [m_s[8 * b : 8 * b + 8, :] for b in range(blocks)]
    sub = sublanes()
    for kb in range(blocks):
        cols = [
            [jnp.broadcast_to(m[b][:, 8 * kb + j : 8 * kb + j + 1], (8, 128)) for j in range(8)]
            for b in range(blocks)
        ]
        rows = m[kb]
        piv = list(cols[kb])
        for j in range(8):
            inv = F32(1) / wide(piv[j][j : j + 1])
            here = sub == j
            factor = piv[j]
            top = wide(rows[j : j + 1]) * inv
            rows = jnp.where(here, top, rows - factor * top)
            for q in range(j + 1, 8):
                top = wide(piv[q][j : j + 1]) * inv
                piv[q] = jnp.where(here, top, piv[q] - factor * top)
        spread = [wide(rows[j : j + 1]) for j in range(8)]
        for b in range(blocks):
            if b == kb:
                m[b] = rows
            else:
                acc = cols[b][0] * spread[0]
                for j in range(1, 8):
                    acc = acc + cols[b][j] * spread[j]
                m[b] = m[b] - acc
    for b in range(blocks):
        m_s[8 * b : 8 * b + 8, :] = m[b]
    turned = jnp.transpose(m_s[...], (1, 0))
    turned = turned[members : members + 8, :]
    for h in range(2):
        at = h * half
        first_ref[:, h * (half - 8) : (h + 1) * (half - 8)] = turned[:, at : at + half - 8]
        last_ref[:, 8 * h : 8 * h + 8] = turned[:, at + half - 8 : at + half]


def solve_weights(near, far, target, error):
    half, n_obs = near.shape
    members = 2 * half
    return pl.pallas_call(
        weights_kernel,
        in_specs=[VMEM_SPEC] * 4,
        out_specs=[VMEM_SPEC] * 2,
        scratch_shapes=[
            pltpu.VMEM((members, n_obs), F32),
            pltpu.VMEM((members, 2 * members), F32),
        ],
        out_shape=[
            jax.ShapeDtypeStruct((8, members - 16), F32), jax.ShapeDtypeStruct((8, 16), F32),
        ],
        compiler_params=pltpu.CompilerParams(vmem_limit_bytes=4 * 2**20),
        name="weights",
    )(near, far, target, error)


def shifted(w, pieces, f_ref, x, to):
    rows = jnp.concatenate([v[x].astype(F32) for v in pieces], axis=0).astype(BF16)
    shift = jnp.dot(w, rows, preferred_element_type=F32)
    return [f_ref[2 * to + t] + shift[:, 128 * t : 128 * t + 128] for t in range(2)]


def begin_kernel(w_ref, *refs):
    pieces, (f_ref, out_ref) = refs[:-2], refs[-2:]
    w = w_ref[...].astype(BF16)

    def chunk(g, _):
        for r in range(16):
            x = g * 16 + r
            for t, v in enumerate(shifted(w, pieces, f_ref, x, x)):
                out_ref[2 * x + t] = v
        return 0

    lax.fori_loop(0, pieces[0].shape[0] // 16, chunk, 0)


def update_kernel(w_ref, *refs):
    pieces, (f_ref, out_ref, row_s, done_s, sems) = refs[:-5], refs[-5:]
    step = row_s.shape[0]
    w = w_ref[...].astype(BF16)

    def leave(g):
        at = pl.ds(pl.multiple_of(g * step, step), step)
        return pltpu.make_async_copy(done_s.at[:, at, :], out_ref.at[:, at, :], sems.at[g])

    count = pieces[0].shape[0] // step

    def chunk(half, i, _):
        g = half * count + i
        for r in range(step):
            at = (i * step + r, g * step + r)
            for t, v in enumerate(shifted(w, pieces[half::2], f_ref, *at)):
                row_s[r, :, 128 * t : 128 * t + 128] = v
        at = pl.ds(pl.multiple_of(g * step, step), step)
        done_s[:, at, :] = jnp.swapaxes(row_s[...], 0, 1)
        leave(g).start()
        return 0

    for half in range(2):
        lax.fori_loop(0, count, functools.partial(chunk, half), 0)
    for g in range(2 * count):
        leave(g).wait()


def begin(weights, pieces, forecast):
    return pl.pallas_call(
        begin_kernel,
        in_specs=[VMEM_SPEC] * (len(pieces) + 2),
        out_specs=VMEM_SPEC,
        out_shape=jax.ShapeDtypeStruct(forecast.shape, F32),
        compiler_params=pltpu.CompilerParams(vmem_limit_bytes=12 * 2**20),
        name="begin",
    )(weights, *pieces, forecast)


def update(weights, pieces, forecast):
    rows, members, size_y = pieces[0].shape
    size_x = 2 * rows
    step = 32
    whole = (members, size_x, size_y)
    return pl.pallas_call(
        update_kernel,
        in_specs=[VMEM_SPEC] * (len(pieces) + 2),
        out_specs=HBM_SPEC,
        out_shape=jax.ShapeDtypeStruct(whole, F32),
        scratch_shapes=[
            pltpu.VMEM((step, members, size_y), F32),
            pltpu.VMEM(whole, F32),
            pltpu.SemaphoreType.DMA((size_x // step,)),
        ],
        compiler_params=pltpu.CompilerParams(vmem_limit_bytes=8 * 2**20),
        name="update",
    )(weights, *pieces, forecast)


def local(pressure, elevation, ks_field, melt_rate, obs_index, obs_value, obs_error, perturbation):
    _, size_x, _ = pressure.shape
    n_x, n_y, n_m = (lax.axis_size(a) for a in ("tx", "ty", "mem"))
    tile_x, tile_y = lax.axis_index("tx"), lax.axis_index("ty")

    def ring(n, by):
        return [(i, (i + by) % n) for i in range(n)]

    n_obs = obs_index.shape[0]
    top, bottom, code, inside = ends(
        obs_index.reshape(n_obs // 128, 128), pressure, melt_rate, elevation, ks_field
    )
    up = lax.ppermute(bottom, "tx", ring(n_x, 1))
    down = lax.ppermute(top, "tx", ring(n_x, -1))
    pt, wt, left, right = turn(pressure, melt_rate, elevation, ks_field)
    above, below, left, right = halo_rows(up, down, top, bottom, left, right)
    from_left = lax.ppermute(right, "ty", ring(n_y, 1))
    from_right = lax.ppermute(left, "ty", ring(n_y, -1))
    forecast, rounded = run_steps(
        pt, wt, elevation, ks_field, above, below, from_left, from_right
    )
    picked = picks(code, forecast, inside)

    def send(v, by, swap=False):
        to = [(i, (i + 2 * (by if i % 2 == 0 else -by)) % n_m) for i in range(n_m)]
        return lax.ppermute(v, "mem", [(i, i ^ 1) for i in range(n_m)] if swap else to)

    block = n_obs // (n_x * n_y)
    tile = tile_x * n_y + tile_y
    target = (obs_value[:, None] + obs_error[:, None] * perturbation).T
    target = lax.dynamic_update_slice(jnp.zeros((8, n_obs), F32), target, (0, tile * block))
    per_row = 128 // block
    error = lax.dynamic_update_slice(
        jnp.zeros((n_obs // 128, 128), F32), obs_error[None],
        (tile // per_row, tile % per_row * block),
    )
    line = jnp.concatenate([picked, target, error], axis=1)
    a, b = send(rounded, 1), send(rounded, -1)
    own_far = send(rounded, 0, True)
    for axis, n in (("ty", n_y), ("tx", n_x)):
        span = 2
        while span <= n:
            line = line + lax.ppermute(line, axis, [(i, i ^ (span - 1)) for i in range(n)])
            if span == 2 and axis == "ty":
                line, own_far = lax.optimization_barrier((line, own_far))
            span *= 2
    observed, target, error = (
        line[:, 0:n_obs], line[:, n_obs : 2 * n_obs], line[:, 2 * n_obs :]
    )
    observed, a, b = lax.optimization_barrier((observed, a, b))
    half = size_x // 2
    c0 = send(a[:half], 1)
    c1 = send(b[half:], -1)
    opposite, up_part = send(observed, 2), send(observed, 1)
    parts = [up_part, send(observed, -1), opposite]
    near = jnp.concatenate([observed] + parts)
    far = send(near, 0, True)
    far, a, b = lax.optimization_barrier((far, a, b))
    a_far, b_far = send(a, 0, True), send(b, 0, True)
    w_first, w_last = solve_weights(near, far, target, error)
    begun = begin(w_first, [rounded, a, b, own_far, a_far, b_far], forecast)
    return update(w_last, [c0, c1, send(c0, 0, True), send(c1, 0, True)], begun)


def solution(mesh):
    placed = (
        P("mem", "tx", "ty"),
        P("tx", "ty"),
        P("tx", "ty"),
        P("mem", "tx", "ty"),
        P(),
        P(("tx", "ty")),
        P(("tx", "ty")),
        P(("tx", "ty"), "mem"),
    )
    return jax.shard_map(
        local, mesh=mesh, in_specs=placed, out_specs=P("mem", "tx", "ty"), check_vma=False
    )
```

```python
import functools

import jax
import jax.numpy as jnp
from jax import lax
from jax.experimental import pallas as pl
from jax.experimental.pallas import tpu as pltpu
from jax.sharding import PartitionSpec as P

SUBSTEPS = 4
W = SUBSTEPS
GROUP = 128 // W
F32 = jnp.float32
BF16 = jnp.bfloat16
VMEM_SPEC = pl.BlockSpec(memory_space=pltpu.VMEM)
HBM_SPEC = pl.BlockSpec(memory_space=pltpu.HBM)


def lanes():
    return lax.broadcasted_iota(jnp.int32, (8, 128), 1)


def sublanes():
    return lax.broadcasted_iota(jnp.int32, (8, 128), 0)


def wide(row):
    return jnp.broadcast_to(row, (8, 128))


def ends_kernel(
    obs_ref, p_ref, w_ref, e_ref, k_ref, top_ref, bottom_ref, code_ref, inside_ref,
    cubes, sems,
):
    _, size_x, size_y = p_ref.shape
    copies = []
    for i, lo in enumerate((0, size_x - 8)):
        for j, ref in enumerate((p_ref, w_ref)):
            copies.append((ref.at[:, pl.ds(lo, 8), :], cubes.at[2 * i + j]))
    copies = [pltpu.make_async_copy(a, b, sems.at[n]) for n, (a, b) in enumerate(copies)]
    for c in copies:
        c.start()
    bits_x, bits_y = size_x.bit_length() - 1, size_y.bit_length() - 1
    total_y = size_y * lax.axis_size("ty")
    obs = obs_ref[...]
    x = lax.shift_right_logical(obs, total_y.bit_length() - 1)
    y = obs & (total_y - 1)
    mine = (lax.shift_right_logical(x, bits_x) == lax.axis_index("tx")) & (
        lax.shift_right_logical(y, bits_y) == lax.axis_index("ty")
    )
    x, y = x & (size_x - 1), y & (size_y - 1)
    tile = x * (size_y // 128) + lax.shift_right_logical(y, 7)
    code_ref[...] = tile * 1024 + ((lanes() - y) & 127)
    inside_ref[...] = jnp.where(mine, F32(1), F32(0))
    for c in copies:
        c.wait()
    sub = lax.broadcasted_iota(jnp.int32, (8, size_y), 0)
    for i, out in enumerate((top_ref, bottom_ref)):
        for j in range(2):
            turned = jnp.swapaxes(cubes[2 * i + j], 0, 1)
            for r in range(W):
                out[j * W + r] = turned[r if i == 0 else 8 - W + r]
        lo = (0, size_x - 8)[i]
        e, k = e_ref[lo : lo + 8, :], k_ref[lo : lo + 8, :]
        if i == 0:
            k = pltpu.roll(k, 4, 0)
        else:
            e = pltpu.roll(e, 4, 0)
        out[2 * W] = jnp.where(sub < 4, e, k)


def ends(obs, p, w, e, k):
    members, _, size_y = p.shape
    edge = jax.ShapeDtypeStruct((2 * W + 1, members, size_y), F32)
    return pl.pallas_call(
        ends_kernel,
        in_specs=[VMEM_SPEC] + [HBM_SPEC] * 2 + [VMEM_SPEC] * 2,
        out_specs=[VMEM_SPEC] * 4,
        out_shape=[
            edge, edge, jax.ShapeDtypeStruct(obs.shape, jnp.int32),
            jax.ShapeDtypeStruct(obs.shape, F32),
        ],
        scratch_shapes=[
            pltpu.VMEM((4, members, 8, size_y), F32),
            pltpu.SemaphoreType.DMA((4,)),
        ],
        compiler_params=pltpu.CompilerParams(vmem_limit_bytes=56 * 2**20),
        name="ends",
    )(obs, p, w, e, k)


def pack_rows(rows):
    slot = lanes() // W
    left = jnp.zeros((8, 128), F32)
    right = jnp.zeros((8, 128), F32)
    for r, a, b in rows:
        if r:
            a = pltpu.roll(a, W * r, 1)
            b = pltpu.roll(b, W * r, 1)
        left = jnp.where(slot == r, a, left)
        right = jnp.where(slot == (r - 1) % GROUP, b, right)
    return left, right


def turn_kernel(
    p_in, w_in, e_ref, k_ref, pt_out, wt_out, left_ref, right_ref,
    p_ref, w_ref, pt_ref, wt_ref, in_sems, out_sems,
):
    groups = left_ref.shape[0]

    def rows_of(g):
        return pl.ds(pl.multiple_of(g * GROUP, GROUP), GROUP)

    def fetch(g, f):
        src, dst = ((p_in, p_ref), (w_in, w_ref))[f]
        at = rows_of(g)
        return pltpu.make_async_copy(src.at[:, at, :], dst.at[:, at, :], in_sems.at[f, g])

    def leave(g, f):
        src, dst = ((pt_ref, pt_out), (wt_ref, wt_out))[f]
        at = rows_of(g)
        return pltpu.make_async_copy(src.at[at], dst.at[at], out_sems.at[f, g])

    for g in range(groups):
        for f in range(2):
            fetch(g, f).start()

    def group(g, _):
        at = rows_of(g)
        for f, (src, dst) in enumerate(((p_ref, pt_ref), (w_ref, wt_ref))):
            fetch(g, f).wait()
            rows = jnp.swapaxes(src[:, at, :] * F32(0.5), 0, 1)
            dst[at] = rows
            left_ref[g, f], right_ref[g, f] = pack_rows(
                (r, rows[r, :, 0:128], rows[r, :, 128:256]) for r in range(GROUP)
            )
            leave(g, f).start()
        fields = []
        for base, ref, factor in ((0, e_ref, 0.5), (4, k_ref, 0.25)):
            block = ref[at, :] * F32(factor)
            for q in range(GROUP // 8):
                part = block[8 * q : 8 * q + 8]
                fields.append((base + q, part[:, 0:128], part[:, 128:256]))
        left_ref[g, 2], right_ref[g, 2] = pack_rows(fields)
        return 0

    lax.fori_loop(0, groups, group, 0)
    for g in range(groups):
        for f in range(2):
            leave(g, f).wait()


def turn(p, w, e, k):
    members, size_x, size_y = p.shape
    groups = size_x // GROUP
    turned = (size_x, members, size_y)
    return pl.pallas_call(
        turn_kernel,
        in_specs=[HBM_SPEC] * 2 + [VMEM_SPEC] * 2,
        out_specs=[HBM_SPEC] * 2 + [VMEM_SPEC] * 2,
        out_shape=[jax.ShapeDtypeStruct(turned, F32)] * 2
        + [jax.ShapeDtypeStruct((groups, 3, 8, 128), F32)] * 2,
        scratch_shapes=[pltpu.VMEM(p.shape, F32)] * 2 + [pltpu.VMEM(turned, F32)] * 2
        + [pltpu.SemaphoreType.DMA((2, groups))] * 2,
        cost_estimate=pl.CostEstimate(flops=10**7, bytes_accessed=9 * 2**20, transcendentals=0),
        compiler_params=pltpu.CompilerParams(vmem_limit_bytes=52 * 2**20),
        name="turn",
    )(p, w, e, k)


def rows_kernel(
    up_ref, down_ref, top_ref, bottom_ref, left_in, right_in, above_ref, below_ref,
    left_ref, right_ref,
):
    tile, groups = lax.axis_index("tx"), left_in.shape[0]
    first, last = tile == 0, tile == lax.axis_size("tx") - 1
    left_ref[0:groups] = left_in[...]
    right_ref[0:groups] = right_in[...]
    sub = lax.broadcasted_iota(jnp.int32, (8, 256), 0)

    def mirrored(block):
        out = block
        for i in range(4):
            for base in (0, 4):
                row = block[base + 3 - i : base + 4 - i, :]
                out = jnp.where(sub == base + i, jnp.broadcast_to(row, (8, 256)), out)
        return out

    for flag, got, own, out in (
        (first, up_ref, top_ref, above_ref),
        (last, down_ref, bottom_ref, below_ref),
    ):
        for f in range(2):
            for i in range(W):
                row = jnp.where(flag, own[f * W + W - 1 - i], got[f * W + i])
                out[f * W + i] = row * F32(0.5)
        block = jnp.where(flag, mirrored(own[2 * W]), got[2 * W])
        out[2 * W] = block * jnp.where(sub < 4, F32(0.5), F32(0.25))
    for f in range(2):
        left_ref[groups, f], right_ref[groups, f] = pack_rows(
            (half * W + i, out[f * W + i, :, 0:128], out[f * W + i, :, 128:256])
            for half, out in enumerate((above_ref, below_ref))
            for i in range(W)
        )
    above, below = above_ref[2 * W], below_ref[2 * W]
    e = jnp.where(sub < 4, above, pltpu.roll(below, 4, 0))
    k = jnp.where(sub < 4, pltpu.roll(above, 4, 0), below)
    left_ref[groups, 2], right_ref[groups, 2] = pack_rows(
        (slot, v[:, 0:128], v[:, 128:256]) for slot, v in ((0, e), (4, k))
    )


def halo_rows(up, down, top, bottom, left, right):
    packs = jax.ShapeDtypeStruct((left.shape[0] + 1, *left.shape[1:]), F32)
    return pl.pallas_call(
        rows_kernel,
        in_specs=[VMEM_SPEC] * 6,
        out_specs=[VMEM_SPEC] * 4,
        out_shape=[jax.ShapeDtypeStruct(up.shape, F32)] * 2 + [packs] * 2,
        compiler_params=pltpu.CompilerParams(vmem_limit_bytes=4 * 2**20),
        name="rows",
    )(up, down, top, bottom, left, right)


def steps_kernel(
    pt_in, wt_in, e_ref, k_ref, above_ref, below_ref, fl_ref, fr_ref,
    out_ref, round_ref,
    p0, p1, w_s, fy_s, sum_s, fy2_s, sum2_s, e_s, er_s, k_s, kr_s, sems,
):
    size_x = pt_in.shape[0]
    lane = lanes()
    is_first, is_last = lane == 0, lane == 127
    groups = size_x // GROUP
    blocks = size_x // 8 + 2
    inner = (pl.ds(9, size_x), slice(None), pl.ds(0, 256))
    loads = [
        pltpu.make_async_copy(src, dst.at[inner], sems.at[i])
        for i, (src, dst) in enumerate(((pt_in, p0), (wt_in, w_s)))
    ]
    for c in loads:
        c.start()

    def halo(g, f, r):
        a, b = fr_ref[g, f], fl_ref[g, f]
        if r:
            a = pltpu.roll(a, 128 - W * r, 1)
            b = pltpu.roll(b, 128 - W * r, 1)
        return jnp.where(lane < 64, a, b)

    def spread(at, v, here, shifted):
        rolled = [pltpu.roll(u, 127, 1) for u in v]
        for t in range(3):
            here[at, :, 128 * t : 128 * t + 128] = v[t]
            shifted[at, :, 128 * t : 128 * t + 128] = jnp.where(
                is_last, rolled[(t + 1) % 3], rolled[t]
            )

    def unpack_group(g, _):
        for r in range(GROUP):
            for f, dst in ((0, p0), (1, w_s)):
                dst[g * GROUP + r + 9, :, 256:384] = halo(g, f, r)
        for q in range(GROUP // 8):
            rows = pl.ds(pl.multiple_of(g * GROUP + 8 * q, 8), 8)
            for base, ref, factor, here, shifted in (
                (0, e_ref, 0.5, e_s, er_s), (4, k_ref, 0.25, k_s, kr_s),
            ):
                v = [ref[rows, 128 * t : 128 * t + 128] * F32(factor) for t in range(2)]
                spread(g * (GROUP // 8) + q + 1, v + [halo(g, 2, base + q)], here, shifted)
        return 0

    lax.fori_loop(0, groups, unpack_group, 0)
    for r in range(2 * W):
        ref, y = (above_ref, 4 + r) if r < W else (below_ref, size_x + 4 + r)
        for f, dst in ((0, p0), (1, w_s)):
            dst[y + 1, :, 0:256] = ref[f * W + r % W]
            dst[y + 1, :, 256:384] = halo(groups, f, r)
    for base, here, shifted in ((0, e_s, er_s), (4, k_s, kr_s)):
        edge = pltpu.roll(halo(groups, 2, base), 4, 0)
        for at, ref, up in ((0, above_ref, base == 0), (blocks - 1, below_ref, base == 4)):
            v = ref[2 * W]
            v = pltpu.roll(v, 4, 0) if up else v
            spread(at, [v[:, 0:128], v[:, 128:256], edge], here, shifted)

    one, none = F32(1), F32(0)

    tile = lax.axis_index("ty")

    def edge_mask(at):
        return jnp.where(is_last & (jnp.broadcast_to(tile, (8, 128)) == at), none, one)

    mask_right, mask_left = edge_mask(lax.axis_size("ty") - 1), edge_mask(0)
    for c in loads:
        c.wait()

    def tiles(ref, at):
        return [ref[at, :, 128 * t : 128 * t + 128] for t in range(3)]

    def put(ref, at, v):
        for t in range(3):
            ref[at, :, 128 * t : 128 * t + 128] = v[t]

    def row_of(ref, b, u):
        return [wide(ref[b, u : u + 1, 128 * t : 128 * t + 128]) for t in range(3)]

    def finish(dst, at, sums, fluxes):
        for u in range(8):
            fy = tiles(fluxes, u)
            fr = [pltpu.roll(v, 1, 1) for v in fy]
            s = tiles(sums, u)
            back = [jnp.where(is_first, fr[(t - 1) % 3], fr[t]) for t in range(3)]
            put(dst, at * 8 + u, [s[t] + (fy[t] - back[t]) for t in range(3)])

    def fluxes_of(src, at, sums, fluxes, carry):
        p_old, h_old, c_old, fx_old, fy_old = carry
        for u in range(8):
            p = tiles(src, at * 8 + u + 1)
            raw = [pltpu.roll(v, 127, 1) for v in p]
            pr = [jnp.where(is_last, raw[(t + 1) % 3], raw[t]) for t in range(3)]
            e, er = row_of(e_s, at, u), row_of(er_s, at, u)
            k, kr = row_of(k_s, at, u), row_of(kr_s, at, u)
            w = tiles(w_s, at * 8 + u)
            h = [p[t] + e[t] for t in range(3)]
            c = [k[t] * jnp.tanh(p[t]) + k[t] for t in range(3)]
            fy = [
                (c[t] + (kr[t] * jnp.tanh(pr[t]) + kr[t])) * ((pr[t] + er[t]) - h[t])
                for t in range(3)
            ]
            fy[1] = fy[1] * mask_right
            fy[2] = fy[2] * mask_left
            fx = [(c_old[t] + c[t]) * (h[t] - h_old[t]) for t in range(3)]
            put(sums, u, [(p_old[t] + w[t]) + (fx[t] - fx_old[t]) for t in range(3)])
            put(fluxes, u, fy_old)
            p_old, h_old, c_old, fx_old, fy_old = p, h, c, fx, fy
        return p_old, h_old, c_old, fx_old, fy_old

    def step(src, dst):
        def body(i, carry):
            carry = fluxes_of(src, 2 * i, sum_s, fy_s, carry)
            finish(dst, jnp.maximum(2 * i - 1, 0), sum2_s, fy2_s)
            carry = fluxes_of(src, 2 * i + 1, sum2_s, fy2_s, carry)
            finish(dst, 2 * i, sum_s, fy_s)
            return carry

        zero = [jnp.zeros((8, 128), F32)] * 3
        lax.fori_loop(0, blocks // 2, body, (zero,) * 5)
        finish(dst, blocks - 1, sum2_s, fy2_s)

    for s in range(SUBSTEPS):
        step(*((p0, p1) if s % 2 == 0 else (p1, p0)))
    last = p0 if SUBSTEPS % 2 == 0 else p1

    def leave(i, _):
        x = pl.multiple_of(i * 8, 8)
        for u in range(8):
            row = last[x + 9 + u, :, 0:256] * F32(2)
            out_ref[2 * x + 2 * u] = row[:, 0:128]
            out_ref[2 * x + 2 * u + 1] = row[:, 128:256]
            round_ref[x + u] = row.astype(BF16)
        return 0

    lax.fori_loop(0, size_x // 8, leave, 0)


def run_steps(pt, wt, e, k, above, below, from_left, from_right):
    size_x, members, size_y = pt.shape
    tile = pltpu.VMEM((size_x + 17, members, size_y + 128), F32)
    flat = pltpu.VMEM((size_x // 8 + 2, 8, size_y + 128), F32)
    few = pltpu.VMEM((8, members, size_y + 128), F32)
    return pl.pallas_call(
        steps_kernel,
        in_specs=[HBM_SPEC] * 2 + [VMEM_SPEC] * 6,
        out_specs=[VMEM_SPEC] * 2,
        scratch_shapes=[tile] * 3 + [few] * 4 + [flat] * 4 + [pltpu.SemaphoreType.DMA((2,))],
        out_shape=[
            jax.ShapeDtypeStruct((size_x * (size_y // 128), members, 128), F32),
            jax.ShapeDtypeStruct((size_x, members, size_y), BF16),
        ],
        compiler_params=pltpu.CompilerParams(vmem_limit_bytes=50 * 2**20),
        name="steps",
    )(pt, wt, e, k, above, below, from_left, from_right)


def pick_kernel(code_ref, f_ref, inside_ref, pick_ref):
    lane = lanes()

    def pick(g, _):
        acc = jnp.zeros((8, 128), F32)
        for u in range(128):
            code = code_ref[g, u]
            at = pl.multiple_of(lax.shift_right_logical(code, 7), 8)
            v = pltpu.roll(f_ref[pl.ds(at, 8), :], code, 1)
            acc = jnp.where(lane == u, v, acc)
        keep = wide(inside_ref[pl.ds(g, 1), :]) > F32(0.5)
        pick_ref[:, pl.ds(pl.multiple_of(g * 128, 128), 128)] = jnp.where(keep, acc, F32(0))
        return 0

    lax.fori_loop(0, code_ref.shape[0], pick, 0)


def picks(code, forecast, inside):
    return pl.pallas_call(
        pick_kernel,
        grid_spec=pltpu.PrefetchScalarGridSpec(
            num_scalar_prefetch=1, grid=(), in_specs=[VMEM_SPEC] * 2, out_specs=VMEM_SPEC
        ),
        out_shape=jax.ShapeDtypeStruct((8, code.size), F32),
        compiler_params=pltpu.CompilerParams(vmem_limit_bytes=8 * 2**20),
        name="picks",
    )(code, forecast.reshape(-1, 128), inside)


def weights_kernel(near_ref, far_ref, target_ref, error_ref, first_ref, last_ref, x_s, m_s):
    half = near_ref.shape[0]
    members = 2 * half
    blocks = members // 8
    parts = [r[8 * b : 8 * b + 8, :] for r in (near_ref, far_ref) for b in range(half // 8)]
    total = parts[0]
    for part in parts[1:]:
        total = total + part
    mean = jnp.sum(total, axis=0, keepdims=True) * F32(1.0 / members)
    error = jnp.concatenate([error_ref[r : r + 1, :] for r in range(error_ref.shape[0])], axis=1)
    inverse = F32(1) / error
    for b, part in enumerate(parts):
        x_s[8 * b : 8 * b + 8, :] = (part - mean) * inverse
    innovation = (target_ref[...] - parts[0]) * inverse
    x = x_s[...]
    dims = (((1,), (1,)), ((), ()))
    dot = functools.partial(
        lax.dot_general, dimension_numbers=dims, precision=lax.Precision.HIGHEST,
        preferred_element_type=F32,
    )
    r = lax.broadcasted_iota(jnp.int32, (members, members), 0)
    c = lax.broadcasted_iota(jnp.int32, (members, members), 1)
    m_s[:, 0:members] = dot(x, x) + jnp.where(r == c, F32(members - 1), F32(0))
    m_s[:, members : 2 * members] = jnp.zeros((members, members), F32)
    m_s[:, members : members + 8] = dot(x, innovation)
    m = [m_s[8 * b : 8 * b + 8, :] for b in range(blocks)]
    sub = sublanes()
    for kb in range(blocks):
        cols = [
            [jnp.broadcast_to(m[b][:, 8 * kb + j : 8 * kb + j + 1], (8, 128)) for j in range(8)]
            for b in range(blocks)
        ]
        rows = m[kb]
        piv = list(cols[kb])
        for j in range(8):
            inv = F32(1) / wide(piv[j][j : j + 1])
            here = sub == j
            factor = piv[j]
            top = wide(rows[j : j + 1]) * inv
            rows = jnp.where(here, top, rows - factor * top)
            for q in range(j + 1, 8):
                top = wide(piv[q][j : j + 1]) * inv
                piv[q] = jnp.where(here, top, piv[q] - factor * top)
        spread = [wide(rows[j : j + 1]) for j in range(8)]
        for b in range(blocks):
            if b == kb:
                m[b] = rows
            else:
                acc = cols[b][0] * spread[0]
                for j in range(1, 8):
                    acc = acc + cols[b][j] * spread[j]
                m[b] = m[b] - acc
    for b in range(blocks):
        m_s[8 * b : 8 * b + 8, :] = m[b]
    turned = jnp.transpose(m_s[...], (1, 0))
    turned = turned[members : members + 8, :]
    for h in range(2):
        at = h * half
        first_ref[:, h * (half - 8) : (h + 1) * (half - 8)] = turned[:, at : at + half - 8]
        last_ref[:, 8 * h : 8 * h + 8] = turned[:, at + half - 8 : at + half]


def solve_weights(near, far, target, error):
    half, n_obs = near.shape
    members = 2 * half
    return pl.pallas_call(
        weights_kernel,
        in_specs=[VMEM_SPEC] * 4,
        out_specs=[VMEM_SPEC] * 2,
        scratch_shapes=[
            pltpu.VMEM((members, n_obs), F32),
            pltpu.VMEM((members, 2 * members), F32),
        ],
        out_shape=[
            jax.ShapeDtypeStruct((8, members - 16), F32), jax.ShapeDtypeStruct((8, 16), F32),
        ],
        compiler_params=pltpu.CompilerParams(vmem_limit_bytes=4 * 2**20),
        name="weights",
    )(near, far, target, error)


def shifted(w, pieces, f_ref, x, to):
    rows = jnp.concatenate([v[x].astype(F32) for v in pieces], axis=0).astype(BF16)
    shift = jnp.dot(w, rows, preferred_element_type=F32)
    return [f_ref[2 * to + t] + shift[:, 128 * t : 128 * t + 128] for t in range(2)]


def begin_kernel(w_ref, *refs):
    pieces, (f_ref, out_ref) = refs[:-2], refs[-2:]
    w = w_ref[...].astype(BF16)

    def chunk(g, _):
        for r in range(64):
            x = g * 64 + r
            for t, v in enumerate(shifted(w, pieces, f_ref, x, x)):
                out_ref[2 * x + t] = v
        return 0

    lax.fori_loop(0, pieces[0].shape[0] // 64, chunk, 0)


def update_kernel(w_ref, *refs):
    pieces, (f_ref, out_ref, row_s, done_s, sems) = refs[:-5], refs[-5:]
    step = row_s.shape[0]
    w = w_ref[...].astype(BF16)

    def leave(g):
        at = pl.ds(pl.multiple_of(g * step, step), step)
        return pltpu.make_async_copy(done_s.at[:, at, :], out_ref.at[:, at, :], sems.at[g])

    count = pieces[0].shape[0] // step

    def chunk(half, i, _):
        g = half * count + i
        for r in range(step):
            at = (i * step + r, g * step + r)
            for t, v in enumerate(shifted(w, pieces[half::2], f_ref, *at)):
                row_s[r, :, 128 * t : 128 * t + 128] = v
        at = pl.ds(pl.multiple_of(g * step, step), step)
        done_s[:, at, :] = jnp.swapaxes(row_s[...], 0, 1)
        leave(g).start()
        return 0

    for half in range(2):
        lax.fori_loop(0, count, functools.partial(chunk, half), 0)
    for g in range(2 * count):
        leave(g).wait()


def begin(weights, pieces, forecast):
    return pl.pallas_call(
        begin_kernel,
        in_specs=[VMEM_SPEC] * (len(pieces) + 2),
        out_specs=VMEM_SPEC,
        out_shape=jax.ShapeDtypeStruct(forecast.shape, F32),
        compiler_params=pltpu.CompilerParams(vmem_limit_bytes=12 * 2**20),
        name="begin",
    )(weights, *pieces, forecast)


def update(weights, pieces, forecast):
    rows, members, size_y = pieces[0].shape
    size_x = 2 * rows
    step = 32
    whole = (members, size_x, size_y)
    return pl.pallas_call(
        update_kernel,
        in_specs=[VMEM_SPEC] * (len(pieces) + 2),
        out_specs=HBM_SPEC,
        out_shape=jax.ShapeDtypeStruct(whole, F32),
        scratch_shapes=[
            pltpu.VMEM((step, members, size_y), F32),
            pltpu.VMEM(whole, F32),
            pltpu.SemaphoreType.DMA((size_x // step,)),
        ],
        compiler_params=pltpu.CompilerParams(vmem_limit_bytes=8 * 2**20),
        name="update",
    )(weights, *pieces, forecast)


def local(pressure, elevation, ks_field, melt_rate, obs_index, obs_value, obs_error, perturbation):
    _, size_x, _ = pressure.shape
    n_x, n_y, n_m = (lax.axis_size(a) for a in ("tx", "ty", "mem"))
    tile_x, tile_y = lax.axis_index("tx"), lax.axis_index("ty")

    def ring(n, by):
        return [(i, (i + by) % n) for i in range(n)]

    n_obs = obs_index.shape[0]
    top, bottom, code, inside = ends(
        obs_index.reshape(n_obs // 128, 128), pressure, melt_rate, elevation, ks_field
    )
    up = lax.ppermute(bottom, "tx", ring(n_x, 1))
    down = lax.ppermute(top, "tx", ring(n_x, -1))
    pt, wt, left, right = turn(pressure, melt_rate, elevation, ks_field)
    above, below, left, right = halo_rows(up, down, top, bottom, left, right)
    from_left = lax.ppermute(right, "ty", ring(n_y, 1))
    from_right = lax.ppermute(left, "ty", ring(n_y, -1))
    forecast, rounded = run_steps(
        pt, wt, elevation, ks_field, above, below, from_left, from_right
    )
    picked = picks(code, forecast, inside)

    def send(v, by, swap=False):
        to = [(i, (i + 2 * (by if i % 2 == 0 else -by)) % n_m) for i in range(n_m)]
        return lax.ppermute(v, "mem", [(i, i ^ 1) for i in range(n_m)] if swap else to)

    block = n_obs // (n_x * n_y)
    tile = tile_x * n_y + tile_y
    target = (obs_value[:, None] + obs_error[:, None] * perturbation).T
    target = lax.dynamic_update_slice(jnp.zeros((8, n_obs), F32), target, (0, tile * block))
    per_row = 128 // block
    error = lax.dynamic_update_slice(
        jnp.zeros((n_obs // 128, 128), F32), obs_error[None],
        (tile // per_row, tile % per_row * block),
    )
    line = jnp.concatenate([picked, target, error], axis=1)
    a, b = send(rounded, 1), send(rounded, -1)
    own_far = send(rounded, 0, True)
    for axis, n in (("ty", n_y), ("tx", n_x)):
        span = 2
        while span <= n:
            line = line + lax.ppermute(line, axis, [(i, i ^ (span - 1)) for i in range(n)])
            if span == 2 and axis == "ty":
                line, own_far = lax.optimization_barrier((line, own_far))
            span *= 2
    observed, target, error = (
        line[:, 0:n_obs], line[:, n_obs : 2 * n_obs], line[:, 2 * n_obs :]
    )
    observed, a, b = lax.optimization_barrier((observed, a, b))
    half = size_x // 2
    c0, c1 = send(a[:half], 1), send(b[half:], -1)
    parts = [send(observed, by) for by in (1, -1, 2)]
    near = jnp.concatenate([observed] + parts)
    far = send(near, 0, True)
    far, a, b = lax.optimization_barrier((far, a, b))
    a_far, b_far = send(a, 0, True), send(b, 0, True)
    w_first, w_last = solve_weights(near, far, target, error)
    begun = begin(w_first, [rounded, a, b, own_far, a_far, b_far], forecast)
    return update(w_last, [c0, c1, send(c0, 0, True), send(c1, 0, True)], begun)


def solution(mesh):
    placed = (
        P("mem", "tx", "ty"),
        P("tx", "ty"),
        P("tx", "ty"),
        P("mem", "tx", "ty"),
        P(),
        P(("tx", "ty")),
        P(("tx", "ty")),
        P(("tx", "ty"), "mem"),
    )
    return jax.shard_map(
        local, mesh=mesh, in_specs=placed, out_specs=P("mem", "tx", "ty"), check_vma=False
    )
```
